32 devices in a mesh: groups: 2 (over y), inst: 4 (over z), section: 2 (over x), tp: 2 (over core).
Axes of the slice: x: 2, y: 2, z: 4, core: 2. Of those that a mesh axis runs over, the one named last changes fastest.
Arguments:
- emb: bfloat16 [4, 32, 8192], P(None, ('groups', 'inst'), 'tp'), parts along dimension 1, may hold values from -24 to 24
- attn_gain: float32 [2, 8192], P('section', 'tp'), may hold values from 0.1 to 1.9
- out_gain: float32 [2, 8192], P('section', 'tp'), may hold values from 0.4 to 1.6
- k_cache: bfloat16 [8, 2, 24, 128, 1024], P(('groups', 'inst'), 'section', None, None, 'tp'), parts along dimension 0, may hold values from -128 to 128
- v_cache: bfloat16 [8, 2, 24, 128, 1024], P(('groups', 'inst'), 'section', None, None, 'tp'), parts along dimension 0, may hold values from -6 to 6
- tables: int32 [8, 4, 6], P(('groups', 'inst')), parts along dimension 0, may hold values from 0 to 23, as said below
- lens: int32 [8, 4], P('groups'), parts along dimension 0, may hold values from 2 to 764
- partner: int32 [4], replicated, may hold values from 0 to 3, as said below
- mig_req: int32 [8], P('groups'), parts along dimension 0, may hold values from 0 to 3
Outputs:
- layer_out: bfloat16 [2, 4, 32, 8192], P('section', None, ('groups', 'inst'), 'tp'), parts along dimension 2
- arrived_k: bfloat16 [8, 2, 768, 1024], P(('groups', 'inst'), 'section', None, 'tp'), parts along dimension 0
- arrived_v: bfloat16 [8, 2, 768, 1024], P(('groups', 'inst'), 'section', None, 'tp'), parts along dimension 0
The draws below stay inside these ranges and needn't reach their ends.
There are 2 independent parts, one for each index of `groups`. The reference program is written for one: setup_inputs(seed, part) draws one part's arguments, and reference() takes and returns one part's arrays. A program takes and returns all parts, laid end to end along the dimension named above; an argument that names none is the same for every part. Nothing has to cross between parts.
Inputs may be any that keep to these rules, and one draw needn't show every extreme that they name: partner[i] = i XOR m for one m of 1 .. 3, the same for every i. `tables`: each instance's table names each of its 24 pool blocks exactly once.
All inputs are finite; a program needn't handle non-finite values.
Results may differ from the reference program's by a relative error of at most 0.0061.
Values may be sent and summed in bfloat16 or wider, within the bound.
A program may use at most 64 MiB of HBM per device.

```python
import jax
import jax.numpy as jnp
from jax import lax

QH = 64
KVH = 8
HD = 128
BLK = 128
REQ = 4
MAXBLK = 6
STEPS = 4
D = 8192
KVD = 1024
LAYERS = 2
CTX = 768
NPOOL = 24
L_MAX = 764
N_INST = 4


def pool_tables(key):
    subkeys = jax.random.split(jax.random.fold_in(key, 11), N_INST)
    perms = jax.vmap(lambda subkey: jax.random.permutation(subkey, NPOOL))(subkeys)
    return perms.reshape(N_INST, REQ, MAXBLK).astype(jnp.int32)


def draw_emb(key, part):
    feats = jnp.arange(D)
    rough = jnp.exp(jax.random.uniform(jax.random.fold_in(key, 21), (D,), jnp.float32, -0.35, 0.35))
    scales = jnp.where(feats < D // 2, 0.6, 1.2) * rough
    noise = jax.random.normal(jax.random.fold_in(key, 22), (STEPS, N_INST * REQ, D), jnp.float32)
    values = noise * scales
    return jnp.clip(values, -24.0, 24.0).astype(jnp.bfloat16)


def draw_out_gain(key, part):
    feats = jnp.arange(D)
    unit = jax.random.uniform(jax.random.fold_in(key, 31), (LAYERS, D), jnp.float32)
    low = jnp.where(feats < D // 2, 0.4, 0.8)
    return (low * jnp.exp(unit * jnp.log(2.0))).astype(jnp.float32)


def draw_k_cache(key, part):
    base = jax.random.normal(jax.random.fold_in(key, 41), (N_INST, LAYERS, NPOOL, BLK, KVD), jnp.float32)
    base = jnp.clip(base, -6.0, 6.0)
    return base.astype(jnp.bfloat16)


def draw_tables(key, part):
    return pool_tables(key)


def draw_lens(key, part):
    values = jax.random.randint(jax.random.fold_in(key, 13), (N_INST * REQ,), 2, L_MAX + 1, jnp.int32)
    longest = jax.random.randint(jax.random.fold_in(key, 14), (), 0, N_INST * REQ, jnp.int32)
    values = values.at[longest].set(L_MAX)
    return values.reshape(N_INST, REQ)


def draw_partner(key, part):
    offset = jax.random.randint(jax.random.fold_in(key, 15), (), 1, N_INST, jnp.int32)
    return jnp.bitwise_xor(jnp.arange(N_INST, dtype=jnp.int32), offset)


def set_ends(array, own_key, low, high):
    spot = [jax.random.randint(jax.random.fold_in(own_key, axis), (), 0, length) for axis, length in enumerate(array.shape)]
    widest = array.shape.index(max(array.shape))
    neighbour = spot[:widest] + [(spot[widest] + 1) % array.shape[widest]] + spot[widest + 1:]
    return array.at[tuple(spot)].set(low).at[tuple(neighbour)].set(high)


def steps_of(key, shape, cuts, smallest, largest):
    level, own = 1.0, jax.random.fold_in(key, 6)
    for position, blocks in cuts:
        heights = jnp.exp(jax.random.uniform(jax.random.fold_in(own, position), (blocks,), jnp.float32, smallest / len(cuts), largest / len(cuts)))
        level = level * jnp.repeat(heights, shape[position] // blocks).reshape([-1 if axis == position else 1 for axis in range(len(shape))])
    return level


def gaussian(own_key, dims, scale, limit, cuts=(), kind=jnp.bfloat16):
    values = jax.random.normal(own_key, dims, jnp.float32) * scale
    if len(cuts) > 0:
        values = steps_of(own_key, dims, cuts, -0.22, 0.18) * values
    return jnp.clip(values, min=-limit, max=limit).astype(kind)


def setup_inputs(seed: int = 0, part: int = 0) -> dict:
    key_list = jax.random.split(jax.random.key(seed), 10)
    own_keys = jax.random.split(jax.random.fold_in(key_list[9], part), 10)
    emb = draw_emb(jax.random.fold_in(jax.random.fold_in(key_list[9], part), 71), part)
    attn_gain = jnp.clip(1.0 + 0.18 * jax.random.normal(key_list[1], (LAYERS, D), jnp.float32), 0.1, 1.9)
    out_gain = draw_out_gain(jax.random.fold_in(key_list[9], 71), part)
    k_cache = draw_k_cache(jax.random.fold_in(jax.random.fold_in(key_list[9], part), 71), part)
    v_cache = gaussian(own_keys[4], (N_INST, LAYERS, NPOOL, BLK, KVD), 1.0, 6.0, ((0, 4), (1, 2), (4, 2)))
    tables = draw_tables(jax.random.fold_in(jax.random.fold_in(key_list[9], part), 71), part)
    lens = draw_lens(jax.random.fold_in(jax.random.fold_in(key_list[9], part), 71), part)
    partner = draw_partner(jax.random.fold_in(key_list[9], 71), part)
    mig_req = set_ends(jax.random.randint(own_keys[8], (N_INST,), 0, REQ), jax.random.fold_in(own_keys[8], 1), 0, REQ - 1).astype(jnp.int32)
    return dict(emb=emb, attn_gain=attn_gain, out_gain=out_gain, k_cache=k_cache, v_cache=v_cache, tables=tables, lens=lens, partner=partner, mig_req=mig_req)


def layer_keys(cache_layer, tables):

    def one_instance(pool_blocks, table_rows):
        return pool_blocks[table_rows.reshape(-1)].reshape(REQ, CTX, KVD)
    return jax.vmap(one_instance)(cache_layer, tables)

def reference(emb, attn_gain, out_gain, k_cache, v_cache, tables, lens, partner, mig_req):
    rows = N_INST * REQ
    group = QH // KVH
    scale = HD ** (-0.5)
    lens_flat = lens.reshape(rows)
    positions = jnp.arange(CTX, dtype=jnp.int32)
    old_mask = positions[None, :] < lens_flat[:, None]
    step_index = jnp.arange(STEPS, dtype=jnp.int32)
    new_keys = jnp.zeros((LAYERS, STEPS, rows, KVD), jnp.bfloat16)
    new_values = jnp.zeros((LAYERS, STEPS, rows, KVD), jnp.bfloat16)
    results = [[None] * STEPS for layer in range(LAYERS)]
    for step in range(STEPS):
        hidden = emb[step]
        for layer in range(LAYERS):
            hidden_f = hidden.astype(jnp.float32)
            squares = lax.optimization_barrier(jnp.sum(hidden_f * hidden_f, axis=-1))
            normed = hidden_f * lax.rsqrt(squares / D + 1e-05)[:, None] * attn_gain[layer]
            heads = normed.reshape(rows, KVH, group, HD)
            query = heads.astype(jnp.bfloat16)
            key_step = lax.optimization_barrier(jnp.mean(heads, axis=2)).reshape(rows, KVD).astype(jnp.bfloat16)
            value_step = lax.optimization_barrier(jnp.mean(hidden_f.reshape(rows, KVH, group, HD), axis=2)).reshape(rows, KVD).astype(jnp.bfloat16)
            new_keys = new_keys.at[layer, step].set(key_step)
            new_values = new_values.at[layer, step].set(value_step)
            keys_old = layer_keys(k_cache[:, layer], tables).reshape(rows, CTX, KVH, HD)
            values_old = layer_keys(v_cache[:, layer], tables).reshape(rows, CTX, KVH, HD)
            keys_fresh = new_keys[layer].reshape(STEPS, rows, KVH, HD)
            values_fresh = new_values[layer].reshape(STEPS, rows, KVH, HD)
            query_f = query.astype(jnp.float32)
            score_old = jnp.einsum('rgqd,rcgd->rgqc', query_f, keys_old.astype(jnp.float32)) * scale
            score_old = jnp.where(old_mask[:, None, None, :], score_old, -jnp.inf)
            score_new = jnp.einsum('rgqd,trgd->rgqt', query_f, keys_fresh.astype(jnp.float32)) * scale
            score_new = jnp.where((step_index <= step)[None, None, None, :], score_new, -jnp.inf)
            top = jnp.maximum(lax.optimization_barrier(jnp.max(score_old, axis=-1)), lax.optimization_barrier(jnp.max(score_new, axis=-1)))
            expo_old = jnp.exp(score_old - top[..., None])
            expo_new = jnp.exp(score_new - top[..., None])
            total = lax.optimization_barrier(jnp.sum(expo_old, axis=-1)) + lax.optimization_barrier(jnp.sum(expo_new, axis=-1))
            weight_old = (expo_old / total[..., None]).astype(jnp.bfloat16)
            weight_new = (expo_new / total[..., None]).astype(jnp.bfloat16)
            attended = jnp.einsum('rgqc,rcgd->rgqd', weight_old.astype(jnp.float32), values_old.astype(jnp.float32))
            attended = attended + jnp.einsum('rgqt,trgd->rgqd', weight_new.astype(jnp.float32), values_fresh.astype(jnp.float32))
            head_norm = attended * lax.rsqrt(lax.optimization_barrier(jnp.mean(attended * attended, axis=-1)) + 1e-05)[..., None]
            hidden = (hidden_f + head_norm.reshape(rows, D) * out_gain[layer]).astype(jnp.bfloat16)
            results[layer][step] = hidden
    layer_out = jnp.stack([jnp.stack(results[layer]) for layer in range(LAYERS)])
    source = partner
    chosen = mig_req[source]
    length = lens[source, chosen]
    flat_index = source * REQ + chosen

    def place(base, piece, start):
        return lax.dynamic_update_slice(base, piece, (start, jnp.int32(0)))
    arrived = []
    for cache, fresh_all in ((k_cache, new_keys), (v_cache, new_values)):
        per_layer = []
        for layer in range(LAYERS):
            logical = layer_keys(cache[:, layer], tables)
            picked = logical[source, chosen]
            picked = jnp.where(positions[None, :, None] < length[:, None, None], picked, jnp.zeros((), picked.dtype))
            fresh = jnp.transpose(fresh_all[layer][:, flat_index], (1, 0, 2))
            per_layer.append(jax.vmap(place)(picked, fresh, length))
        arrived.append(jnp.stack(per_layer, axis=1))
    return (layer_out, arrived[0], arrived[1])
```

```python
import functools

import jax
import jax.numpy as jnp
from jax import lax
from jax.experimental import pallas as pl
from jax.experimental.pallas import tpu as pltpu
from jax.sharding import PartitionSpec as P

QH = 64
KVH = 8
HD = 128
LOADS = 6
PAD = 8
KINDS = 2
WINDOW = 3
LIMIT = 20 << 20
FEW = 3
MESH = pl.DeviceIdType.MESH
NT = (((1,), (1,)), ((), ()))


def place(block, fresh, first_row, source_len):
    blk, width = block.shape
    pos = lax.broadcasted_iota(jnp.int32, (blk, PAD), 0) + first_row - source_len
    hit = jnp.where(pos == lax.broadcasted_iota(jnp.int32, (blk, PAD), 1), 1.0, 0.0).astype(jnp.bfloat16)
    placed = jnp.dot(hit, fresh, preferred_element_type=jnp.float32)
    row = lax.broadcasted_iota(jnp.int32, (blk, width), 0) + first_row
    return jnp.where(row < source_len, block.astype(jnp.float32), placed).astype(jnp.bfloat16)


def begin(offset, levels, tables_hbm, lens_hbm, mig_hbm, emb_hbm, gain_attn_hbm, gain_out_hbm, k_hbm, v_hbm,
          pick, out, send, moved, fresh_recv, front,
          tables, lens, mig_req, emb, gain_attn, gain_out, gain_q, gain_o, turn,
          k_all, v_all, recv, counts, fresh_send,
          h_rows, y_rows, res, h_in, ss_all, ss_out, fk, fv, q_diag,
          small_sem, load_sem, mig_send, mig_recv, moved_send, moved_recv, count_ssem, count_rsem, fresh_ssem, fresh_rsem,
          h_ssem, h_rsem, ss_ssem, ss_rsem, peer_sem):
    sections = lax.axis_size("section")
    cores = lax.axis_size("tp")
    groups = lax.axis_size("groups")
    section = lax.axis_index("section")
    core = lax.axis_index("tp")
    inst = lax.axis_index("inst")
    group = lax.axis_index("groups")
    steps, requests, width = emb.shape
    pool, blk, kv_local = k_all.shape
    instances = lens.shape[0]
    total = send.shape[0]
    maxblk = total // KINDS
    spare = total - levels[0]
    lead = recv.shape[0]
    heads_kv = kv_local // HD
    heads = width // HD
    share = QH // KVH
    rows = heads * steps
    part = share * steps
    scale = HD ** (-0.5)
    total_width = width * cores
    source = jnp.bitwise_xor(inst, offset)
    beside = jnp.bitwise_xor(group, 1)

    small = []
    for i, (src, dst) in enumerate((
            (mig_hbm, mig_req), (tables_hbm, tables), (lens_hbm, lens),
            (emb_hbm, emb), (gain_attn_hbm, gain_attn), (gain_out_hbm, gain_out))):
        small.append(pltpu.make_async_copy(src, dst, small_sem.at[i]))
    loads = []
    piece = pool // LOADS
    for which, (src, dst) in enumerate(((k_hbm, k_all), (v_hbm, v_all))):
        for i in range(LOADS):
            loads.append(pltpu.make_async_copy(
                src.at[0, 0, pl.ds(i * piece, piece)], dst.at[pl.ds(i * piece, piece)], load_sem.at[which, i]))
    for copy in small[:3] + loads[:LOADS] + small[3:] + loads[LOADS:]:
        copy.start()

    barrier = pltpu.get_barrier_semaphore()
    pl.semaphore_signal(barrier, inc=1, device_id={"inst": source}, device_id_type=MESH)
    greeted = cores
    if spare > 0:
        for step in range(1, groups):
            pl.semaphore_signal(barrier, inc=1, device_id={"groups": lax.rem(group + step, groups)}, device_id_type=MESH)
        greeted = greeted + groups - 1
    for step in range(1, cores):
        pl.semaphore_signal(barrier, inc=1, device_id={"tp": lax.rem(core + step, cores)}, device_id_type=MESH)

    @pl.when(section > 0)
    def _():
        for other in range(cores):
            pl.semaphore_signal(barrier, inc=1, device_id={"section": section - 1, "tp": other}, device_id_type=MESH)

    @pl.when(section < sections - 1)
    def _():
        for other in range(cores):
            pl.semaphore_signal(barrier, inc=1, device_id={"section": section + 1, "tp": other}, device_id_type=MESH)

    def peer_copy(step):
        return pltpu.make_async_remote_copy(
            src_ref=ss_all.at[core], dst_ref=ss_all.at[core],
            send_sem=peer_sem.at[0, step], recv_sem=peer_sem.at[1, core],
            device_id={"tp": lax.rem(core + step, cores)}, device_id_type=MESH)

    def peer_arrival(other):
        return pltpu.make_async_remote_copy(
            src_ref=ss_all.at[other], dst_ref=ss_all.at[other],
            send_sem=peer_sem.at[0, 0], recv_sem=peer_sem.at[1, other],
            device_id={"tp": lax.rem(core + 1, cores)}, device_id_type=MESH)

    def next_copy(r):
        return pltpu.make_async_remote_copy(
            src_ref=res.at[r], dst_ref=h_in.at[r],
            send_sem=h_ssem.at[r], recv_sem=h_rsem.at[r],
            device_id={"section": section + 1}, device_id_type=MESH)

    def next_sum(r, other):
        return pltpu.make_async_remote_copy(
            src_ref=ss_out.at[r], dst_ref=ss_all.at[core, r],
            send_sem=ss_ssem.at[r, other], recv_sem=ss_rsem.at[r, core],
            device_id={"section": section + 1, "tp": other}, device_id_type=MESH)

    def sum_arrival(r, other):
        return pltpu.make_async_remote_copy(
            src_ref=ss_out.at[r], dst_ref=ss_all.at[other, r],
            send_sem=ss_ssem.at[r, other], recv_sem=ss_rsem.at[r, other],
            device_id={"tp": lax.rem(core + 1, cores)}, device_id_type=MESH)

    def own_copy(u):
        return pltpu.make_async_remote_copy(
            src_ref=send.at[u], dst_ref=recv.at[u],
            send_sem=mig_send.at[u], recv_sem=mig_recv.at[u],
            device_id={"inst": source}, device_id_type=MESH)

    def moved_copy(j):
        return pltpu.make_async_remote_copy(
            src_ref=send.at[levels[0] + j], dst_ref=moved.at[j],
            send_sem=moved_send.at[j], recv_sem=moved_recv.at[j],
            device_id={"groups": beside}, device_id_type=MESH)

    def count_copy(step, slot):
        return pltpu.make_async_remote_copy(
            src_ref=counts.at[slot], dst_ref=counts.at[slot],
            send_sem=count_ssem.at[step], recv_sem=count_rsem.at[slot],
            device_id={"groups": lax.rem(group + step, groups)}, device_id_type=MESH)

    fresh_copy = pltpu.make_async_remote_copy(
        src_ref=fresh_send, dst_ref=fresh_recv, send_sem=fresh_ssem, recv_sem=fresh_rsem,
        device_id={"inst": source}, device_id_type=MESH)

    for copy in small[:3]:
        copy.wait()
    if spare > 0:
        lane = lax.broadcasted_iota(jnp.int32, counts.shape[1:], 1)
        held = jnp.zeros(counts.shape[1:], jnp.int32)
        for i in range(instances):
            held = jnp.where(lane == i, lax.div(lens[i, mig_req[i]] + (blk - 1), blk), held)
        counts[group] = held
    neighbours = jnp.minimum(section, 1) + jnp.minimum(sections - 1 - section, 1)
    pl.semaphore_wait(barrier, greeted + cores * neighbours)
    if spare > 0:
        for step in range(1, groups):
            count_copy(step, group).start()

    handed = mig_req[inst]
    for which, stored in enumerate((k_all, v_all)):
        for i in range(LOADS):
            loads[which * LOADS + i].wait()

        def gather(b, carry, which=which, stored=stored):
            u = KINDS * b + which
            send[u] = stored[tables[0, handed, b]]

            @pl.when(u < lead)
            def _():
                own_copy(u).start()
            if spare > 0:
                @pl.when(u >= levels[0])
                def _():
                    moved_copy(u - levels[0]).start()
            return carry
        lax.fori_loop(0, maxblk, gather, 0)
    for copy in small[3:]:
        copy.wait()

    for i in range(heads):
        lanes = slice(i * HD, (i + 1) * HD)
        span = slice(i * steps, (i + 1) * steps)
        gain_q[span, :] = jnp.broadcast_to(gain_attn[0:1, lanes], (steps, HD))
        gain_o[span, :] = jnp.broadcast_to(gain_out[0:1, lanes], (steps, HD))

    tile = 2 * steps

    def row_sums(a):
        a = jnp.sum((a * a).reshape(rows // tile, tile, HD), axis=0)
        a = a[:steps] + a[steps:]
        a = jnp.broadcast_to(jnp.sum(a, axis=-1, keepdims=True), (steps, HD))
        return jnp.concatenate([a, a], axis=0)

    @pl.when(section == 0)
    def _():
        for t in range(steps):
            e = emb[t].astype(jnp.float32)
            for i in range(heads):
                h_rows[pl.ds(i * steps + t, requests, stride=rows), :] = e[:, i * HD:(i + 1) * HD]
        for r in range(requests):
            ss_all[core, r] = row_sums(h_rows[r * rows:(r + 1) * rows, :])
        for step in range(1, cores):
            peer_copy(step).start()

    fk[...] = jnp.zeros_like(fk)
    fv[...] = jnp.zeros_like(fv)
    q_diag[...] = jnp.zeros_like(q_diag)

    @pl.when(section == 0)
    def _():
        for step in range(1, cores):
            peer_arrival(lax.rem(core + step, cores)).wait_recv()

    def one_request(r, carry):
        @pl.when(section > 0)
        def _():
            next_copy(r).wait_recv()
            for other in range(cores):
                sum_arrival(r, other).wait_recv()
            h_rows[pl.ds(pl.multiple_of(r * rows, rows), rows), :] = h_in[r].astype(jnp.float32)

        squares = ss_all[0, r]
        for other in range(1, cores):
            squares = squares + ss_all[other, r]
        ratio = lax.rsqrt(squares / total_width + 1e-05)
        length = lens[inst, r]
        h = h_rows[pl.ds(pl.multiple_of(r * rows, rows), rows), :]
        x = h.reshape(rows // tile, tile, HD) * ratio[None] * gain_q[...].reshape(rows // tile, tile, HD)
        x = x.reshape(rows, HD)
        for g in range(heads_kv):
            lanes = slice(g * HD, (g + 1) * HD)
            span = slice(g * part, (g + 1) * part)
            key_sum = jnp.sum(x[span].reshape(part // tile, tile, HD), axis=0)
            value_sum = jnp.sum(h[span].reshape(part // tile, tile, HD), axis=0)
            fk[r, 0:steps, lanes] = (key_sum[:steps] + key_sum[steps:]) * (1.0 / share)
            fv[r, 0:steps, lanes] = (value_sum[:steps] + value_sum[steps:]) * (1.0 / share)
            q_diag[span, lanes] = x[span].astype(jnp.bfloat16)
        q = q_diag[...]
        row = lax.broadcasted_iota(jnp.int32, (blk, rows), 0)
        new_row = lax.broadcasted_iota(jnp.int32, (PAD, rows), 0)
        new_step = lax.rem(lax.broadcasted_iota(jnp.int32, (PAD, rows), 1), steps)
        scores = []
        for b in range(maxblk):
            s = lax.dot_general(k_all[tables[0, r, b]], q, NT, preferred_element_type=jnp.float32) * scale
            scores.append(jnp.where(row + b * blk < length, s, -jnp.inf))
        new = lax.dot_general(fk[r].astype(jnp.bfloat16), q, NT, preferred_element_type=jnp.float32) * scale
        new = jnp.where(new_row <= new_step, new, -jnp.inf)
        top = functools.reduce(jnp.maximum, scores)
        top = jnp.maximum(jnp.max(top, axis=0, keepdims=True), jnp.max(new, axis=0, keepdims=True))
        expo = [jnp.exp(s - top) for s in scores]
        expo_new = jnp.exp(new - top)
        total_weight = jnp.sum(functools.reduce(jnp.add, expo), axis=0, keepdims=True)
        total_weight = total_weight + jnp.sum(expo_new, axis=0, keepdims=True)
        inverse = 1.0 / total_weight
        weights = jnp.concatenate([(e * inverse).astype(jnp.bfloat16).T for e in expo], axis=1)
        weights_new = (expo_new * inverse).T.astype(jnp.bfloat16)
        values = [v_all[tables[0, r, b]] for b in range(maxblk)]
        fresh_values = fv[r].astype(jnp.bfloat16)
        outs = []
        for g in range(heads_kv):
            lanes = slice(g * HD, (g + 1) * HD)
            span = slice(g * part, (g + 1) * part)
            o = jnp.dot(weights[span], jnp.concatenate([v[:, lanes] for v in values], axis=0),
                        preferred_element_type=jnp.float32)
            o = o + jnp.dot(weights_new[span], fresh_values[:, lanes], preferred_element_type=jnp.float32)
            o = o * lax.rsqrt(jnp.mean(o * o, axis=-1, keepdims=True) + 1e-05)
            outs.append(o)
        y = (h + jnp.concatenate(outs, axis=0) * gain_o[...]).astype(jnp.bfloat16)
        res[r] = y
        y = y.astype(jnp.float32)
        y_rows[pl.ds(pl.multiple_of(r * rows, rows), rows), :] = y
        ss_out[r] = row_sums(y)

        @pl.when(section < sections - 1)
        def _():
            next_copy(r).start()
            for other in range(cores):
                next_sum(r, other).start()
        return carry

    lax.fori_loop(0, requests, one_request, 0)

    fresh_send[0] = fk[handed].astype(jnp.bfloat16)
    fresh_send[1] = fv[handed].astype(jnp.bfloat16)
    fresh_copy.start()

    if spare > 0:
        for step in range(1, groups):
            count_copy(step, lax.rem(group + step, groups)).wait_recv()
        most = jnp.zeros(counts.shape[1:], jnp.int32)
        for pair in range(0, groups, 2):
            most = jnp.maximum(most, counts[pair] + counts[pair + 1])
        stride = levels[1] - levels[0]
        pick[0] = lax.div(jnp.maximum(jnp.max(most) - levels[0], 0) + (stride - 1), stride)
    else:
        pick[0] = 0

    for t in range(steps):
        for i in range(heads):
            turn[t, :, i * HD:(i + 1) * HD] = y_rows[pl.ds(i * steps + t, requests, stride=rows), :]
    out[0] = turn[...].astype(jnp.bfloat16)

    fresh_copy.wait_recv()
    source_len = lens[source, mig_req[source]]

    for which in range(KINDS):
        def settle(b, carry, which=which):
            u = KINDS * b + which
            own_copy(u).wait_recv()
            front[u] = place(recv[u], fresh_recv[which], b * blk, source_len)
            return carry
        lax.fori_loop(0, lead // KINDS, settle, 0)

    if spare > 0:
        for j in range(spare):
            moved_copy(j).wait_recv()
        for j in range(spare):
            moved_copy(j).wait_send()
        for step in range(1, groups):
            count_copy(step, group).wait_send()
    for u in range(lead):
        own_copy(u).wait_send()
    fresh_copy.wait_send()

    @pl.when(section == 0)
    def _():
        for step in range(1, cores):
            peer_copy(step).wait_send()

    @pl.when(section < sections - 1)
    def _():
        for r in range(requests):
            next_copy(r).wait_send()
            for other in range(cores):
                next_sum(r, other).wait_send()


def finish(offset, slots, lowest, lens_hbm, mig_hbm, send, moved, fresh,
           back,
           lens, mig_req, recv, mix, small_sem, mig_send, mig_recv, back_send):
    inst = lax.axis_index("inst")
    group = lax.axis_index("groups")
    total, blk, _ = send.shape
    lead = total - back.shape[0]
    source = jnp.bitwise_xor(inst, offset)
    beside = jnp.bitwise_xor(group, 1)
    spare = total - slots
    count = slots - lead

    small = [pltpu.make_async_copy(mig_hbm, mig_req, small_sem.at[0]), pltpu.make_async_copy(lens_hbm, lens, small_sem.at[1])]
    for copy in small:
        copy.start()
    barrier = pltpu.get_barrier_semaphore()
    pl.semaphore_signal(barrier, inc=1, device_id={"inst": source}, device_id_type=MESH)
    if spare > 0:
        pl.semaphore_signal(barrier, inc=1, device_id={"groups": beside}, device_id_type=MESH)
    for copy in small:
        copy.wait()
    pl.semaphore_wait(barrier, 2 if spare > 0 else 1)

    def slot(i):
        return jnp.where(i < spare, slots - 1 - i, lead + i - spare)

    def own_copy(u):
        return pltpu.make_async_remote_copy(
            src_ref=send.at[u], dst_ref=recv.at[u - lead],
            send_sem=mig_send.at[u - lead], recv_sem=mig_recv.at[u - lead],
            device_id={"inst": source}, device_id_type=MESH)

    def mix_copy(j):
        u = slots - 1 - j
        return pltpu.make_async_remote_copy(
            src_ref=mix.at[j], dst_ref=recv.at[u - lead],
            send_sem=mig_send.at[u - lead], recv_sem=mig_recv.at[u - lead],
            device_id={"inst": source}, device_id_type=MESH)

    def back_copy(j):
        return pltpu.make_async_remote_copy(
            src_ref=recv.at[slots - 1 - j - lead], dst_ref=recv.at[slots + j - lead],
            send_sem=back_send.at[j], recv_sem=mig_recv.at[slots + j - lead],
            device_id={"groups": beside}, device_id_type=MESH)

    handed_blocks = lax.div(lens[inst, mig_req[inst]] + (blk - 1), blk)
    source_len = lens[source, mig_req[source]]

    def put(i):
        if spare > 0:
            @pl.when(i < spare)
            def _():
                u = slots - 1 - i
                mix[i] = jnp.where(lax.div(u, KINDS) < handed_blocks, send[u], moved[slots + i - lowest])
                mix_copy(i).start()

        @pl.when(i >= spare)
        def _():
            own_copy(lead + i - spare).start()

    def launch(i, carry):
        put(i)
        return carry
    lax.fori_loop(0, min(WINDOW, count), launch, 0)

    def settle(i, carry):
        u = jnp.where(i < count, slot(i), slots + i - count)
        own_copy(u).wait_recv()
        if spare > 0:
            @pl.when(i < spare)
            def _():
                back_copy(i).start()

        @pl.when(i + WINDOW < count)
        def _():
            own_copy(slot(i)).wait_send()
            put(i + WINDOW)
        b = lax.div(u, KINDS)
        back[u - lead] = place(recv[u - lead], fresh[lax.rem(u, KINDS)], b * blk, source_len)
        return carry
    lax.fori_loop(0, total - lead, settle, 0)

    def sent(i, carry):
        own_copy(slot(i)).wait_send()
        return carry
    lax.fori_loop(max(count - WINDOW, 0), count, sent, 0)
    for j in range(spare):
        back_copy(j).wait_send()


def store(res, front, back, res_out, k_out, v_out, sems, res_sem):
    lead, blk, _ = front.shape
    copies = [pltpu.make_async_copy(res, res_out, res_sem)]
    for u in range(lead + back.shape[0]):
        src = front.at[u] if u < lead else back.at[u - lead]
        dst = (k_out, v_out)[u % KINDS]
        copies.append(pltpu.make_async_copy(src, dst.at[0, 0, pl.ds(u // KINDS * blk, blk)], sems.at[u]))
    for copy in copies:
        copy.start()
    for copy in copies:
        copy.wait()


def local(emb, attn_gain, out_gain, k_cache, v_cache, tables, lens, partner, mig_req):
    steps, requests, width = emb.shape
    _, _, pool, blk, kv_local = k_cache.shape
    maxblk = tables.shape[2]
    total = KINDS * maxblk
    cores = lax.axis_size("tp")
    groups = lax.axis_size("groups")
    context = maxblk * blk
    heads_kv = kv_local // HD
    rows = width // HD * steps
    bf16, f32 = jnp.bfloat16, jnp.float32
    vmem = pl.BlockSpec(memory_space=pltpu.VMEM)
    smem = pl.BlockSpec(memory_space=pltpu.SMEM)
    hbm = pl.BlockSpec(memory_space=pltpu.HBM)
    anywhere = pl.BlockSpec(memory_space=pl.ANY)
    dma = pltpu.SemaphoreType.DMA
    offsets = lax.axis_size("inst") - 1
    spare = total // 3 if groups % 2 == 0 else 0
    lead = total - 2 * (total // 3)
    levels = [total]
    if spare > 0:
        stride = 1 if offsets <= FEW else spare // 2
        levels = list(range(total - spare, total + 1, stride))
    buffers = max(spare, 1)

    def unit(count):
        return jax.ShapeDtypeStruct((count, blk, kv_local), bf16)

    def call_begin(offset):
        return pl.pallas_call(
            functools.partial(begin, offset, levels),
            out_shape=(
                jax.ShapeDtypeStruct((1,), jnp.int32),
                jax.ShapeDtypeStruct((1, steps, requests, width), bf16),
                unit(total),
                unit(buffers),
                jax.ShapeDtypeStruct((KINDS, PAD, kv_local), bf16),
                unit(lead),
            ),
            in_specs=[hbm] * 8,
            out_specs=(smem, vmem, vmem, vmem, vmem, vmem),
            scratch_shapes=[
                pltpu.SMEM(tables.shape, jnp.int32),
                pltpu.SMEM(lens.shape, jnp.int32),
                pltpu.SMEM(mig_req.shape, jnp.int32),
                pltpu.VMEM(emb.shape, bf16),
                pltpu.VMEM(attn_gain.shape, f32),
                pltpu.VMEM(out_gain.shape, f32),
                pltpu.VMEM((rows, HD), f32),
                pltpu.VMEM((rows, HD), f32),
                pltpu.VMEM((steps, requests, width), f32),
                pltpu.VMEM((pool, blk, kv_local), bf16),
                pltpu.VMEM((pool, blk, kv_local), bf16),
                pltpu.VMEM((lead, blk, kv_local), bf16),
                pltpu.VMEM((groups, 8, 128), jnp.int32),
                pltpu.VMEM((KINDS, PAD, kv_local), bf16),
                pltpu.VMEM((requests * rows, HD), f32),
                pltpu.VMEM((requests * rows, HD), f32),
                pltpu.VMEM((requests, rows, HD), bf16),
                pltpu.VMEM((requests, rows, HD), bf16),
                pltpu.VMEM((cores, requests, 2 * steps, HD), f32),
                pltpu.VMEM((requests, 2 * steps, HD), f32),
                pltpu.VMEM((requests, PAD, kv_local), f32),
                pltpu.VMEM((requests, PAD, kv_local), f32),
                pltpu.VMEM((rows, heads_kv * HD), bf16),
                dma((6,)),
                dma((KINDS, LOADS)),
                dma((lead,)),
                dma((lead,)),
                dma((buffers,)),
                dma((buffers,)),
                dma((groups,)),
                dma((groups,)),
                dma,
                dma,
                dma((requests,)),
                dma((requests,)),
                dma((requests, cores)),
                dma((requests, cores)),
                dma((2, cores)),
            ],
            compiler_params=pltpu.CompilerParams(
                collective_id=(offset - 1) * (len(levels) + 1), has_side_effects=True, vmem_limit_bytes=LIMIT),
        )

    def call_finish(offset, level):
        return pl.pallas_call(
            functools.partial(finish, offset, levels[level], levels[0]),
            out_shape=unit(total - lead),
            in_specs=[hbm] * 2 + [vmem] * 3,
            out_specs=vmem,
            scratch_shapes=[
                pltpu.SMEM(lens.shape, jnp.int32),
                pltpu.SMEM(mig_req.shape, jnp.int32),
                pltpu.VMEM((total - lead, blk, kv_local), bf16),
                pltpu.VMEM((buffers, blk, kv_local), bf16),
                dma((2,)),
                dma((total - lead,)),
                dma((total - lead,)),
                dma((buffers,)),
            ],
            compiler_params=pltpu.CompilerParams(
                collective_id=(offset - 1) * (len(levels) + 1) + level + 1, has_side_effects=True,
                vmem_limit_bytes=LIMIT),
        )

    call_store = pl.pallas_call(
        store,
        out_shape=(
            jax.ShapeDtypeStruct((1, steps, requests, width), bf16),
            jax.ShapeDtypeStruct((1, 1, context, kv_local), bf16),
            jax.ShapeDtypeStruct((1, 1, context, kv_local), bf16),
        ),
        in_specs=[anywhere] * 3,
        out_specs=(hbm,) * 3,
        scratch_shapes=[dma((total,)), dma],
        compiler_params=pltpu.CompilerParams(vmem_limit_bytes=LIMIT),
    )

    def way(offset):
        def run(*operands):
            pick, out, send, moved, fresh, front = call_begin(offset)(*operands)

            def rest(level):
                def run_rest(lens, mig_req, out, send, moved, fresh, front):
                    return call_store(out, front, call_finish(offset, level)(lens, mig_req, send, moved, fresh))
                return run_rest
            return tuple(lax.switch(
                pick[0], [rest(level) for level in range(len(levels))],
                operands[1], operands[2], out, send, moved, fresh, front))
        return run

    return tuple(lax.switch(
        partner[0] - 1, [way(offset) for offset in range(1, offsets + 1)],
        tables, lens, mig_req, emb, attn_gain, out_gain, k_cache, v_cache))


def solution(mesh):
    return jax.shard_map(
        local,
        mesh=mesh,
        in_specs=(
            P(None, ("groups", "inst"), "tp"),
            P("section", "tp"),
            P("section", "tp"),
            P(("groups", "inst"), "section", None, None, "tp"),
            P(("groups", "inst"), "section", None, None, "tp"),
            P(("groups", "inst"), None, None),
            P("groups", None),
            P(),
            P("groups"),
        ),
        out_specs=(
            P("section", None, ("groups", "inst"), "tp"),
            P(("groups", "inst"), "section", None, "tp"),
            P(("groups", "inst"), "section", None, "tp"),
        ),
        check_vma=False,
    )
```

```python
import functools
import itertools

import jax
import jax.numpy as jnp
from jax import lax
from jax.experimental import pallas as pl
from jax.experimental.pallas import tpu as pltpu
from jax.sharding import PartitionSpec as P

QH = 64
KVH = 8
HD = 128
LOADS = 6
PAD = 8
KINDS = 2
SPLIT = 2
WINDOW = 4
LIMIT = 20 << 20
FEW = 3
MESH = pl.DeviceIdType.MESH
NT = (((1,), (1,)), ((), ()))


def place(block, fresh, first_row, source_len):
    blk, width = block.shape
    pos = lax.broadcasted_iota(jnp.int32, (blk, PAD), 0) + first_row - source_len
    hit = jnp.where(pos == lax.broadcasted_iota(jnp.int32, (blk, PAD), 1), 1.0, 0.0).astype(jnp.bfloat16)
    placed = jnp.dot(hit, fresh, preferred_element_type=jnp.float32)
    row = lax.broadcasted_iota(jnp.int32, (blk, width), 0) + first_row
    return jnp.where(row < source_len, block.astype(jnp.float32), placed).astype(jnp.bfloat16)


def begin(offset, classes, levels, tables_hbm, lens_hbm, mig_hbm, emb_hbm, gain_attn_hbm, gain_out_hbm, k_hbm, v_hbm,
          pick, out, send, moved, fresh_recv, front,
          tables, lens, mig_req, emb, gain_attn, gain_out, gain_q, gain_o, turn,
          k_all, v_all, recv, counts, fresh_send,
          h_rows, y_rows, res, h_in, ss_all, ss_out, fk, fv, q_diag,
          small_sem, load_sem, mig_send, mig_recv, moved_send, moved_recv, count_ssem, count_rsem, fresh_ssem, fresh_rsem,
          h_ssem, h_rsem, ss_ssem, ss_rsem, peer_sem):
    sections = lax.axis_size("section")
    cores = lax.axis_size("tp")
    groups = lax.axis_size("groups")
    section = lax.axis_index("section")
    core = lax.axis_index("tp")
    inst = lax.axis_index("inst")
    group = lax.axis_index("groups")
    steps, requests, width = emb.shape
    pool, blk, kv_local = k_all.shape
    instances = lens.shape[0]
    total, unit, _ = send.shape
    chunks = total // KINDS
    split = blk // unit
    maxblk = chunks // split
    spare = total - levels[0]
    lead = recv.shape[0]
    heads_kv = kv_local // HD
    heads = width // HD
    share = QH // KVH
    rows = heads * steps
    part = share * steps
    scale = HD ** (-0.5)
    total_width = width * cores
    source = jnp.bitwise_xor(inst, offset)
    beside = jnp.bitwise_xor(group, 1)

    small = []
    for i, (src, dst) in enumerate((
            (mig_hbm, mig_req), (tables_hbm, tables), (lens_hbm, lens),
            (emb_hbm, emb), (gain_attn_hbm, gain_attn), (gain_out_hbm, gain_out))):
        small.append(pltpu.make_async_copy(src, dst, small_sem.at[i]))
    loads = []
    piece = pool // LOADS
    for which, (src, dst) in enumerate(((k_hbm, k_all), (v_hbm, v_all))):
        for i in range(LOADS):
            loads.append(pltpu.make_async_copy(
                src.at[0, 0, pl.ds(i * piece, piece)], dst.at[pl.ds(i * piece, piece)], load_sem.at[which, i]))
    for copy in small[:3] + loads[:LOADS] + small[3:] + loads[LOADS:]:
        copy.start()

    barrier = pltpu.get_barrier_semaphore()
    pl.semaphore_signal(barrier, inc=1, device_id={"inst": source}, device_id_type=MESH)
    greeted = cores
    if spare > 0:
        for step in range(1, groups):
            pl.semaphore_signal(barrier, inc=1, device_id={"groups": lax.rem(group + step, groups)}, device_id_type=MESH)
        greeted = greeted + groups - 1
    for step in range(1, cores):
        pl.semaphore_signal(barrier, inc=1, device_id={"tp": lax.rem(core + step, cores)}, device_id_type=MESH)

    @pl.when(section > 0)
    def _():
        for other in range(cores):
            pl.semaphore_signal(barrier, inc=1, device_id={"section": section - 1, "tp": other}, device_id_type=MESH)

    @pl.when(section < sections - 1)
    def _():
        for other in range(cores):
            pl.semaphore_signal(barrier, inc=1, device_id={"section": section + 1, "tp": other}, device_id_type=MESH)

    def peer_copy(step):
        return pltpu.make_async_remote_copy(
            src_ref=ss_all.at[core], dst_ref=ss_all.at[core],
            send_sem=peer_sem.at[0, step], recv_sem=peer_sem.at[1, core],
            device_id={"tp": lax.rem(core + step, cores)}, device_id_type=MESH)

    def peer_arrival(other):
        return pltpu.make_async_remote_copy(
            src_ref=ss_all.at[other], dst_ref=ss_all.at[other],
            send_sem=peer_sem.at[0, 0], recv_sem=peer_sem.at[1, other],
            device_id={"tp": lax.rem(core + 1, cores)}, device_id_type=MESH)

    def next_copy(r):
        return pltpu.make_async_remote_copy(
            src_ref=res.at[r], dst_ref=h_in.at[r],
            send_sem=h_ssem.at[r], recv_sem=h_rsem.at[r],
            device_id={"section": section + 1}, device_id_type=MESH)

    def next_sum(r, other):
        return pltpu.make_async_remote_copy(
            src_ref=ss_out.at[r], dst_ref=ss_all.at[core, r],
            send_sem=ss_ssem.at[r, other], recv_sem=ss_rsem.at[r, core],
            device_id={"section": section + 1, "tp": other}, device_id_type=MESH)

    def sum_arrival(r, other):
        return pltpu.make_async_remote_copy(
            src_ref=ss_out.at[r], dst_ref=ss_all.at[other, r],
            send_sem=ss_ssem.at[r, other], recv_sem=ss_rsem.at[r, other],
            device_id={"tp": lax.rem(core + 1, cores)}, device_id_type=MESH)

    def own_copy(u):
        return pltpu.make_async_remote_copy(
            src_ref=send.at[u], dst_ref=recv.at[u],
            send_sem=mig_send.at[u], recv_sem=mig_recv.at[u],
            device_id={"inst": source}, device_id_type=MESH)

    def moved_copy(j):
        return pltpu.make_async_remote_copy(
            src_ref=send.at[levels[0] + j], dst_ref=moved.at[j],
            send_sem=moved_send.at[j], recv_sem=moved_recv.at[j],
            device_id={"groups": beside}, device_id_type=MESH)

    def count_copy(step, slot):
        return pltpu.make_async_remote_copy(
            src_ref=counts.at[slot], dst_ref=counts.at[slot],
            send_sem=count_ssem.at[step], recv_sem=count_rsem.at[slot],
            device_id={"groups": lax.rem(group + step, groups)}, device_id_type=MESH)

    fresh_copy = pltpu.make_async_remote_copy(
        src_ref=fresh_send, dst_ref=fresh_recv, send_sem=fresh_ssem, recv_sem=fresh_rsem,
        device_id={"inst": source}, device_id_type=MESH)

    for copy in small[:3]:
        copy.wait()
    if spare > 0:
        lane = lax.broadcasted_iota(jnp.int32, counts.shape[1:], 1)
        held = jnp.zeros(counts.shape[1:], jnp.int32)
        for i in range(instances):
            held = jnp.where(lane == i, lax.div(lens[i, mig_req[i]] + (unit - 1), unit), held)
        counts[group] = held
    neighbours = jnp.minimum(section, 1) + jnp.minimum(sections - 1 - section, 1)
    pl.semaphore_wait(barrier, greeted + cores * neighbours)
    if spare > 0:
        for step in range(1, groups):
            count_copy(step, group).start()

    handed = mig_req[inst]
    for which, stored in enumerate((k_all, v_all)):
        for i in range(LOADS):
            loads[which * LOADS + i].wait()

        def gather(c, carry, which=which, stored=stored):
            u = KINDS * c + which
            span = pl.ds(pl.multiple_of(lax.rem(c, split) * unit, unit), unit)
            send[u] = stored[tables[0, handed, lax.div(c, split)], span, :]

            @pl.when(u < lead)
            def _():
                own_copy(u).start()
            if spare > 0:
                @pl.when(u >= levels[0])
                def _():
                    moved_copy(u - levels[0]).start()
            return carry
        lax.fori_loop(0, chunks, gather, 0)
    for copy in small[3:]:
        copy.wait()

    for i in range(heads):
        lanes = slice(i * HD, (i + 1) * HD)
        span = slice(i * steps, (i + 1) * steps)
        gain_q[span, :] = jnp.broadcast_to(gain_attn[0:1, lanes], (steps, HD))
        gain_o[span, :] = jnp.broadcast_to(gain_out[0:1, lanes], (steps, HD))

    tile = 2 * steps

    def row_sums(a):
        a = jnp.sum((a * a).reshape(rows // tile, tile, HD), axis=0)
        a = a[:steps] + a[steps:]
        a = jnp.broadcast_to(jnp.sum(a, axis=-1, keepdims=True), (steps, HD))
        return jnp.concatenate([a, a], axis=0)

    @pl.when(section == 0)
    def _():
        def spread(t, carry):
            e = emb[t].astype(jnp.float32)
            for i in range(heads):
                h_rows[pl.ds(i * steps + t, requests, stride=rows), :] = e[:, i * HD:(i + 1) * HD]
            return carry
        lax.fori_loop(0, steps, spread, 0)

        def first_sums(r, carry):
            ss_all[core, r] = row_sums(h_rows[pl.ds(pl.multiple_of(r * rows, rows), rows), :])
            return carry
        lax.fori_loop(0, requests, first_sums, 0)
        for step in range(1, cores):
            peer_copy(step).start()

    fk[...] = jnp.zeros_like(fk)
    fv[...] = jnp.zeros_like(fv)
    q_diag[...] = jnp.zeros_like(q_diag)

    @pl.when(section == 0)
    def _():
        for step in range(1, cores):
            peer_arrival(lax.rem(core + step, cores)).wait_recv()

    def one_request(r, carry):
        @pl.when(section > 0)
        def _():
            next_copy(r).wait_recv()
            for other in range(cores):
                sum_arrival(r, other).wait_recv()
            h_rows[pl.ds(pl.multiple_of(r * rows, rows), rows), :] = h_in[r].astype(jnp.float32)

        squares = ss_all[0, r]
        for other in range(1, cores):
            squares = squares + ss_all[other, r]
        ratio = lax.rsqrt(squares / total_width + 1e-05)
        length = lens[inst, r]
        h = h_rows[pl.ds(pl.multiple_of(r * rows, rows), rows), :]
        x = h.reshape(rows // tile, tile, HD) * ratio[None] * gain_q[...].reshape(rows // tile, tile, HD)
        x = x.reshape(rows, HD)
        for g in range(heads_kv):
            lanes = slice(g * HD, (g + 1) * HD)
            span = slice(g * part, (g + 1) * part)
            key_sum = jnp.sum(x[span].reshape(part // tile, tile, HD), axis=0)
            value_sum = jnp.sum(h[span].reshape(part // tile, tile, HD), axis=0)
            fk[r, 0:steps, lanes] = (key_sum[:steps] + key_sum[steps:]) * (1.0 / share)
            fv[r, 0:steps, lanes] = (value_sum[:steps] + value_sum[steps:]) * (1.0 / share)
            q_diag[span, lanes] = x[span].astype(jnp.bfloat16)
        q = q_diag[...]
        row = lax.broadcasted_iota(jnp.int32, (blk, rows), 0)
        new_row = lax.broadcasted_iota(jnp.int32, (PAD, rows), 0)
        new_step = lax.rem(lax.broadcasted_iota(jnp.int32, (PAD, rows), 1), steps)
        scores = []
        for b in range(maxblk):
            s = lax.dot_general(k_all[tables[0, r, b]], q, NT, preferred_element_type=jnp.float32) * scale
            scores.append(jnp.where(row + b * blk < length, s, -jnp.inf))
        new = lax.dot_general(fk[r].astype(jnp.bfloat16), q, NT, preferred_element_type=jnp.float32) * scale
        new = jnp.where(new_row <= new_step, new, -jnp.inf)
        top = functools.reduce(jnp.maximum, scores)
        top = jnp.maximum(jnp.max(top, axis=0, keepdims=True), jnp.max(new, axis=0, keepdims=True))
        expo = [jnp.exp(s - top) for s in scores]
        expo_new = jnp.exp(new - top)
        total_weight = jnp.sum(functools.reduce(jnp.add, expo), axis=0, keepdims=True)
        total_weight = total_weight + jnp.sum(expo_new, axis=0, keepdims=True)
        inverse = 1.0 / total_weight
        weights = jnp.concatenate([(e * inverse).astype(jnp.bfloat16).T for e in expo], axis=1)
        weights_new = (expo_new * inverse).T.astype(jnp.bfloat16)
        values = [v_all[tables[0, r, b]] for b in range(maxblk)]
        fresh_values = fv[r].astype(jnp.bfloat16)
        outs = []
        for g in range(heads_kv):
            lanes = slice(g * HD, (g + 1) * HD)
            span = slice(g * part, (g + 1) * part)
            o = jnp.dot(weights[span], jnp.concatenate([v[:, lanes] for v in values], axis=0),
                        preferred_element_type=jnp.float32)
            o = o + jnp.dot(weights_new[span], fresh_values[:, lanes], preferred_element_type=jnp.float32)
            o = o * lax.rsqrt(jnp.mean(o * o, axis=-1, keepdims=True) + 1e-05)
            outs.append(o)
        y = (h + jnp.concatenate(outs, axis=0) * gain_o[...]).astype(jnp.bfloat16)
        res[r] = y
        y = y.astype(jnp.float32)
        y_rows[pl.ds(pl.multiple_of(r * rows, rows), rows), :] = y
        ss_out[r] = row_sums(y)

        @pl.when(section < sections - 1)
        def _():
            next_copy(r).start()
            for other in range(cores):
                next_sum(r, other).start()
        return carry

    lax.fori_loop(0, requests, one_request, 0)

    fresh_send[0] = fk[handed].astype(jnp.bfloat16)
    fresh_send[1] = fv[handed].astype(jnp.bfloat16)
    fresh_copy.start()

    if spare > 0:
        for step in range(1, groups):
            count_copy(step, lax.rem(group + step, groups)).wait_recv()
        most = jnp.zeros(counts.shape[1:], jnp.int32)
        for pair in range(0, groups, 2):
            most = jnp.maximum(most, counts[pair] + counts[pair + 1])
        lane = lax.broadcasted_iota(jnp.int32, most.shape, 1)
        choice = 0
        for members in classes:
            own = functools.reduce(jnp.logical_or, [lane == i for i in members])
            need = jnp.max(jnp.where(own, most, 0))
            choice = choice * len(levels)
            for level in levels[:-1]:
                choice = choice + jnp.where(need > level, 1, 0)
        pick[0] = choice
    else:
        pick[0] = 0

    def collect(t, carry):
        for i in range(heads):
            turn[t, :, i * HD:(i + 1) * HD] = y_rows[pl.ds(i * steps + t, requests, stride=rows), :]
        out[0, t] = turn[t].astype(jnp.bfloat16)
        return carry
    lax.fori_loop(0, steps, collect, 0)

    fresh_copy.wait_recv()
    source_len = lens[source, mig_req[source]]

    for which in range(KINDS):
        def settle(c, carry, which=which):
            u = KINDS * c + which
            own_copy(u).wait_recv()
            front[which, c] = place(recv[u], fresh_recv[which], c * unit, source_len)
            return carry
        lax.fori_loop(0, lead // KINDS, settle, 0)

    if spare > 0:
        for j in range(spare):
            moved_copy(j).wait_recv()
        for j in range(spare):
            moved_copy(j).wait_send()
        for step in range(1, groups):
            count_copy(step, group).wait_send()
    for u in range(lead):
        own_copy(u).wait_send()
    fresh_copy.wait_send()

    @pl.when(section == 0)
    def _():
        for step in range(1, cores):
            peer_copy(step).wait_send()

    @pl.when(section < sections - 1)
    def _():
        for r in range(requests):
            next_copy(r).wait_send()
            for other in range(cores):
                next_sum(r, other).wait_send()


def finish(offset, classes, chosen, lowest, lens_hbm, mig_hbm, send, moved, fresh,
           back,
           lens, mig_req, recv, mix, small_sem, mig_send, mig_recv, back_send):
    inst = lax.axis_index("inst")
    group = lax.axis_index("groups")
    total, unit, _ = send.shape
    lead = total - KINDS * back.shape[1]
    source = jnp.bitwise_xor(inst, offset)
    beside = jnp.bitwise_xor(group, 1)
    balanced = lowest < total

    def slots_of(i):
        if len(chosen) == 1:
            return chosen[0]
        slots = chosen[-1]
        for members, level in zip(classes[:-1], chosen[:-1]):
            for member in members:
                slots = jnp.where(i == member, level, slots)
        return slots

    going, coming = slots_of(inst), slots_of(source)
    sends, comes = going - lead, coming - lead
    mixed_out, mixed_in = total - going, total - coming

    small = [pltpu.make_async_copy(mig_hbm, mig_req, small_sem.at[0]), pltpu.make_async_copy(lens_hbm, lens, small_sem.at[1])]
    for copy in small:
        copy.start()
    barrier = pltpu.get_barrier_semaphore()
    pl.semaphore_signal(barrier, inc=1, device_id={"inst": source}, device_id_type=MESH)
    if balanced:
        pl.semaphore_signal(barrier, inc=1, device_id={"groups": beside}, device_id_type=MESH)
    for copy in small:
        copy.wait()
    pl.semaphore_wait(barrier, 2 if balanced else 1)

    def out_slot(i):
        return jnp.where(i < mixed_out, going - 1 - i, lead + i - mixed_out)

    def copy_from(ref, u):
        return pltpu.make_async_remote_copy(
            src_ref=ref, dst_ref=recv.at[u - lead],
            send_sem=mig_send.at[u - lead], recv_sem=mig_recv.at[u - lead],
            device_id={"inst": source}, device_id_type=MESH)

    def back_copy(j):
        return pltpu.make_async_remote_copy(
            src_ref=recv.at[coming - 1 - j - lead], dst_ref=recv.at[coming + j - lead],
            send_sem=back_send.at[j], recv_sem=mig_recv.at[coming + j - lead],
            device_id={"groups": beside}, device_id_type=MESH)

    handed_chunks = lax.div(lens[inst, mig_req[inst]] + (unit - 1), unit)
    source_len = lens[source, mig_req[source]]

    def put(i):
        u = out_slot(i)
        if balanced:
            @pl.when(i < mixed_out)
            def _():
                mix[i] = jnp.where(lax.div(u, KINDS) < handed_chunks, send[u], moved[going + i - lowest])
                copy_from(mix.at[i], u).start()

        @pl.when(i >= mixed_out)
        def _():
            copy_from(send.at[u], u).start()

    def step(i, carry):
        @pl.when(i >= WINDOW)
        def _():
            k = i - WINDOW
            u = jnp.where(k < comes, jnp.where(k < mixed_in, coming - 1 - k, lead + k - mixed_in), coming + k - comes)
            copy_from(send.at[u], u).wait_recv()
            if balanced:
                @pl.when(k < mixed_in)
                def _():
                    back_copy(k).start()

            @pl.when(k < sends)
            def _():
                s = out_slot(k)
                copy_from(send.at[s], s).wait_send()
            which, c = lax.rem(u, KINDS), lax.div(u, KINDS)
            back[which, c - lead // KINDS] = place(recv[u - lead], fresh[which], c * unit, source_len)

        @pl.when(i < sends)
        def _():
            put(i)
        return carry
    lax.fori_loop(0, total - lead + WINDOW, step, 0)

    if balanced:
        def returned(j, carry):
            back_copy(j).wait_send()
            return carry
        lax.fori_loop(0, mixed_in, returned, 0)


def store(res, front, back, res_out, k_out, v_out, sems, res_sem):
    copies = [pltpu.make_async_copy(res, res_out, res_sem)]
    for which, dst in enumerate((k_out, v_out)):
        for i, src in enumerate((back, front)):
            first = 0 if i == 1 else front.shape[1]
            span = pl.ds(first, src.shape[1])
            copies.append(pltpu.make_async_copy(src.at[which], dst.at[span], sems.at[which, i]))
    for copy in copies:
        copy.start()
    for copy in copies:
        copy.wait()


def local(emb, attn_gain, out_gain, k_cache, v_cache, tables, lens, partner, mig_req):
    steps, requests, width = emb.shape
    _, _, pool, blk, kv_local = k_cache.shape
    maxblk = tables.shape[2]
    total = KINDS * SPLIT * maxblk
    cores = lax.axis_size("tp")
    groups = lax.axis_size("groups")
    context = maxblk * blk
    heads_kv = kv_local // HD
    rows = width // HD * steps
    bf16, f32 = jnp.bfloat16, jnp.float32
    vmem = pl.BlockSpec(memory_space=pltpu.VMEM)
    smem = pl.BlockSpec(memory_space=pltpu.SMEM)
    hbm = pl.BlockSpec(memory_space=pltpu.HBM)
    anywhere = pl.BlockSpec(memory_space=pl.ANY)
    dma = pltpu.SemaphoreType.DMA
    offsets = lax.axis_size("inst") - 1
    instances = lax.axis_size("inst")
    lead = total // 4

    def plan(offset):
        together = [tuple(range(instances))]
        if groups % 2 != 0:
            return together, [total]
        if offsets > FEW:
            return together, [total - lead, total]
        if offsets == FEW and offset > 1:
            return [(0, 3), (1, 2)], list(range(total - total // 3, total + 1, total // 6))
        step = total // 12
        return together, [total - lead, total - lead + step // 2] + list(range(total - lead + step, total + 1, step))


    chunk = blk // SPLIT

    def unit(*count):
        return jax.ShapeDtypeStruct((*count, chunk, kv_local), bf16)

    def call_begin(offset):
        classes, levels = plan(offset)
        return pl.pallas_call(
            functools.partial(begin, offset, classes, levels),
            out_shape=(
                jax.ShapeDtypeStruct((1,), jnp.int32),
                jax.ShapeDtypeStruct((1, steps, requests, width), bf16),
                unit(total),
                unit(max(total - levels[0], 1)),
                jax.ShapeDtypeStruct((KINDS, PAD, kv_local), bf16),
                unit(KINDS, lead // KINDS),
            ),
            in_specs=[hbm] * 8,
            out_specs=(smem, vmem, vmem, vmem, vmem, vmem),
            scratch_shapes=[
                pltpu.SMEM(tables.shape, jnp.int32),
                pltpu.SMEM(lens.shape, jnp.int32),
                pltpu.SMEM(mig_req.shape, jnp.int32),
                pltpu.VMEM(emb.shape, bf16),
                pltpu.VMEM(attn_gain.shape, f32),
                pltpu.VMEM(out_gain.shape, f32),
                pltpu.VMEM((rows, HD), f32),
                pltpu.VMEM((rows, HD), f32),
                pltpu.VMEM((steps, requests, width), f32),
                pltpu.VMEM((pool, blk, kv_local), bf16),
                pltpu.VMEM((pool, blk, kv_local), bf16),
                pltpu.VMEM((lead, chunk, kv_local), bf16),
                pltpu.VMEM((groups, 8, 128), jnp.int32),
                pltpu.VMEM((KINDS, PAD, kv_local), bf16),
                pltpu.VMEM((requests * rows, HD), f32),
                pltpu.VMEM((requests * rows, HD), f32),
                pltpu.VMEM((requests, rows, HD), bf16),
                pltpu.VMEM((requests, rows, HD), bf16),
                pltpu.VMEM((cores, requests, 2 * steps, HD), f32),
                pltpu.VMEM((requests, 2 * steps, HD), f32),
                pltpu.VMEM((requests, PAD, kv_local), f32),
                pltpu.VMEM((requests, PAD, kv_local), f32),
                pltpu.VMEM((rows, heads_kv * HD), bf16),
                dma((6,)),
                dma((KINDS, LOADS)),
                dma((lead,)),
                dma((lead,)),
                dma((max(total - levels[0], 1),)),
                dma((max(total - levels[0], 1),)),
                dma((groups,)),
                dma((groups,)),
                dma,
                dma,
                dma((requests,)),
                dma((requests,)),
                dma((requests, cores)),
                dma((requests, cores)),
                dma((2, cores)),
            ],
            compiler_params=pltpu.CompilerParams(
                collective_id=offset - 1, has_side_effects=True, vmem_limit_bytes=LIMIT),
        )

    numbers = itertools.count(offsets)

    def call_finish(offset, chosen):
        classes, levels = plan(offset)
        return pl.pallas_call(
            functools.partial(finish, offset, classes, chosen, levels[0]),
            out_shape=unit(KINDS, (total - lead) // KINDS),
            in_specs=[hbm] * 2 + [vmem] * 3,
            out_specs=vmem,
            scratch_shapes=[
                pltpu.SMEM(lens.shape, jnp.int32),
                pltpu.SMEM(mig_req.shape, jnp.int32),
                pltpu.VMEM((total - lead, chunk, kv_local), bf16),
                pltpu.VMEM((max(total - levels[0], 1), chunk, kv_local), bf16),
                dma((2,)),
                dma((total - lead,)),
                dma((total - lead,)),
                dma((max(total - levels[0], 1),)),
            ],
            compiler_params=pltpu.CompilerParams(
                collective_id=next(numbers), has_side_effects=True, vmem_limit_bytes=LIMIT),
        )

    call_store = pl.pallas_call(
        store,
        out_shape=(
            jax.ShapeDtypeStruct((1, steps, requests, width), bf16),
            unit(total // KINDS),
            unit(total // KINDS),
        ),
        in_specs=[anywhere] * 3,
        out_specs=(hbm,) * 3,
        scratch_shapes=[dma((KINDS, 2)), dma],
        compiler_params=pltpu.CompilerParams(vmem_limit_bytes=LIMIT),
    )

    def way(offset):
        def run(*operands):
            pick, out, send, moved, fresh, front = call_begin(offset)(*operands)

            classes, levels = plan(offset)
            combos = list(itertools.product(levels, repeat=len(classes)))

            def rest(chosen):
                def run_rest(lens, mig_req, out, send, moved, fresh, front):
                    return call_store(out, front, call_finish(offset, chosen)(lens, mig_req, send, moved, fresh))
                return run_rest
            res, k, v = lax.switch(
                pick[0], [rest(chosen) for chosen in combos],
                operands[1], operands[2], out, send, moved, fresh, front)
            return res, k.reshape(1, 1, context, kv_local), v.reshape(1, 1, context, kv_local)
        return run

    return tuple(lax.switch(
        partner[0] - 1, [way(offset) for offset in range(1, offsets + 1)],
        tables, lens, mig_req, emb, attn_gain, out_gain, k_cache, v_cache))


def solution(mesh):
    return jax.shard_map(
        local,
        mesh=mesh,
        in_specs=(
            P(None, ("groups", "inst"), "tp"),
            P("section", "tp"),
            P("section", "tp"),
            P(("groups", "inst"), "section", None, None, "tp"),
            P(("groups", "inst"), "section", None, None, "tp"),
            P(("groups", "inst"), None, None),
            P("groups", None),
            P(),
            P("groups"),
        ),
        out_specs=(
            P("section", None, ("groups", "inst"), "tp"),
            P(("groups", "inst"), "section", None, "tp"),
            P(("groups", "inst"), "section", None, "tp"),
        ),
        check_vma=False,
    )
```

```python
import functools
import itertools

import jax
import jax.numpy as jnp
from jax import lax
from jax.experimental import pallas as pl
from jax.experimental.pallas import tpu as pltpu
from jax.sharding import PartitionSpec as P

QH = 64
KVH = 8
HD = 128
LOADS = 3
STORES = 2
PAD = 8
KINDS = 2
SPLIT = 2
WINDOW = 4
LIMIT = 20 << 20
FEW = 3
MESH = pl.DeviceIdType.MESH
NT = (((1,), (1,)), ((), ()))


def place(block, fresh, first_row, source_len):
    blk, width = block.shape
    pos = lax.broadcasted_iota(jnp.int32, (blk, PAD), 0) + first_row - source_len
    hit = jnp.where(pos == lax.broadcasted_iota(jnp.int32, (blk, PAD), 1), 1.0, 0.0).astype(jnp.bfloat16)
    placed = jnp.dot(hit, fresh, preferred_element_type=jnp.float32)
    row = lax.broadcasted_iota(jnp.int32, (blk, width), 0) + first_row
    return jnp.where(row < source_len, block.astype(jnp.float32), placed).astype(jnp.bfloat16)


def begin(offset, classes, levels, tables_hbm, lens_hbm, mig_hbm, emb_hbm, gain_attn_hbm, gain_out_hbm, k_hbm, v_hbm,
          pick, out, send, moved, fresh, recv,
          tables, lens, mig_req, emb, gain_attn, gain_out, gain_q, gain_o, turn,
          k_all, v_all, counts,
          h_rows, y_rows, res, h_in, ss_all, ss_out, fk, fv, q_diag,
          small_sem, load_sem, mig_send, mig_recv, moved_send, moved_recv, count_ssem, count_rsem,
          h_ssem, h_rsem, ss_ssem, ss_rsem, peer_sem):
    sections = lax.axis_size("section")
    cores = lax.axis_size("tp")
    groups = lax.axis_size("groups")
    section = lax.axis_index("section")
    core = lax.axis_index("tp")
    inst = lax.axis_index("inst")
    group = lax.axis_index("groups")
    steps, requests, width = emb.shape
    pool, blk, kv_local = k_all.shape
    instances = lens.shape[0]
    total, unit, _ = send.shape
    chunks = total // KINDS
    split = blk // unit
    maxblk = chunks // split
    spare = total - levels[0]
    lead = recv.shape[0]
    heads_kv = kv_local // HD
    heads = width // HD
    share = QH // KVH
    rows = heads * steps
    part = share * steps
    scale = HD ** (-0.5)
    total_width = width * cores
    source = jnp.bitwise_xor(inst, offset)
    beside = jnp.bitwise_xor(group, 1)

    small = []
    for i, (src, dst) in enumerate((
            (mig_hbm, mig_req), (tables_hbm, tables), (lens_hbm, lens),
            (emb_hbm, emb), (gain_attn_hbm, gain_attn), (gain_out_hbm, gain_out))):
        small.append(pltpu.make_async_copy(src, dst, small_sem.at[i]))
    loads = []
    piece = pool // LOADS
    for which, (src, dst) in enumerate(((k_hbm, k_all), (v_hbm, v_all))):
        for i in range(LOADS):
            loads.append(pltpu.make_async_copy(
                src.at[0, 0, pl.ds(i * piece, piece)], dst.at[pl.ds(i * piece, piece)], load_sem.at[which, i]))
    for copy in small[:3] + loads[:LOADS] + small[3:] + loads[LOADS:]:
        copy.start()

    barrier = pltpu.get_barrier_semaphore()
    pl.semaphore_signal(barrier, inc=1, device_id={"inst": source}, device_id_type=MESH)
    greeted = cores
    if spare > 0:
        for step in range(1, groups):
            pl.semaphore_signal(barrier, inc=1, device_id={"groups": lax.rem(group + step, groups)}, device_id_type=MESH)
        greeted = greeted + groups - 1
    for step in range(1, cores):
        pl.semaphore_signal(barrier, inc=1, device_id={"tp": lax.rem(core + step, cores)}, device_id_type=MESH)

    @pl.when(section > 0)
    def _():
        for other in range(cores):
            pl.semaphore_signal(barrier, inc=1, device_id={"section": section - 1, "tp": other}, device_id_type=MESH)

    @pl.when(section < sections - 1)
    def _():
        for other in range(cores):
            pl.semaphore_signal(barrier, inc=1, device_id={"section": section + 1, "tp": other}, device_id_type=MESH)

    def peer_copy(step):
        return pltpu.make_async_remote_copy(
            src_ref=ss_all.at[core], dst_ref=ss_all.at[core],
            send_sem=peer_sem.at[0, step], recv_sem=peer_sem.at[1, core],
            device_id={"tp": lax.rem(core + step, cores)}, device_id_type=MESH)

    def peer_arrival(other):
        return pltpu.make_async_remote_copy(
            src_ref=ss_all.at[other], dst_ref=ss_all.at[other],
            send_sem=peer_sem.at[0, 0], recv_sem=peer_sem.at[1, other],
            device_id={"tp": lax.rem(core + 1, cores)}, device_id_type=MESH)

    def next_copy(r):
        return pltpu.make_async_remote_copy(
            src_ref=res.at[r], dst_ref=h_in.at[r],
            send_sem=h_ssem.at[r], recv_sem=h_rsem.at[r],
            device_id={"section": section + 1}, device_id_type=MESH)

    def next_sum(r, other):
        return pltpu.make_async_remote_copy(
            src_ref=ss_out.at[r], dst_ref=ss_all.at[core, r],
            send_sem=ss_ssem.at[r, other], recv_sem=ss_rsem.at[r, core],
            device_id={"section": section + 1, "tp": other}, device_id_type=MESH)

    def sum_arrival(r, other):
        return pltpu.make_async_remote_copy(
            src_ref=ss_out.at[r], dst_ref=ss_all.at[other, r],
            send_sem=ss_ssem.at[r, other], recv_sem=ss_rsem.at[r, other],
            device_id={"tp": lax.rem(core + 1, cores)}, device_id_type=MESH)

    def own_copy(u):
        return pltpu.make_async_remote_copy(
            src_ref=send.at[u], dst_ref=recv.at[u],
            send_sem=mig_send.at[u], recv_sem=mig_recv.at[u],
            device_id={"inst": source}, device_id_type=MESH)

    def moved_copy(j):
        return pltpu.make_async_remote_copy(
            src_ref=send.at[levels[0] + j], dst_ref=moved.at[j],
            send_sem=moved_send.at[j], recv_sem=moved_recv.at[j],
            device_id={"groups": beside}, device_id_type=MESH)

    def count_copy(step, slot):
        return pltpu.make_async_remote_copy(
            src_ref=counts.at[slot], dst_ref=counts.at[slot],
            send_sem=count_ssem.at[step], recv_sem=count_rsem.at[slot],
            device_id={"groups": lax.rem(group + step, groups)}, device_id_type=MESH)

    for copy in small[:3]:
        copy.wait()
    if spare > 0:
        lane = lax.broadcasted_iota(jnp.int32, counts.shape[1:], 1)
        held = jnp.zeros(counts.shape[1:], jnp.int32)
        for i in range(instances):
            held = jnp.where(lane == i, lax.div(lens[i, mig_req[i]] + (unit - 1), unit), held)
        counts[group] = held
    neighbours = jnp.minimum(section, 1) + jnp.minimum(sections - 1 - section, 1)
    pl.semaphore_wait(barrier, greeted + cores * neighbours)
    if spare > 0:
        for step in range(1, groups):
            count_copy(step, group).start()

    handed = mig_req[inst]
    def hand_over(which, stored):
        for i in range(LOADS):
            loads[which * LOADS + i].wait()

        def gather(c, carry):
            u = KINDS * c + which
            span = pl.ds(pl.multiple_of(lax.rem(c, split) * unit, unit), unit)
            send[u] = stored[tables[0, handed, lax.div(c, split)], span, :]

            @pl.when(u < lead)
            def _():
                own_copy(u).start()
            if spare > 0:
                @pl.when(u >= levels[0])
                def _():
                    moved_copy(u - levels[0]).start()
            return carry
        lax.fori_loop(0, chunks, gather, 0)

    hand_over(0, k_all)
    for copy in small[3:]:
        copy.wait()

    for i in range(heads):
        lanes = slice(i * HD, (i + 1) * HD)
        span = slice(i * steps, (i + 1) * steps)
        gain_q[span, :] = jnp.broadcast_to(gain_attn[0:1, lanes], (steps, HD))
        gain_o[span, :] = jnp.broadcast_to(gain_out[0:1, lanes], (steps, HD))

    tile = 2 * steps

    def row_sums(a):
        a = jnp.sum((a * a).reshape(rows // tile, tile, HD), axis=0)
        a = a[:steps] + a[steps:]
        a = jnp.broadcast_to(jnp.sum(a, axis=-1, keepdims=True), (steps, HD))
        return jnp.concatenate([a, a], axis=0)

    @pl.when(section == 0)
    def _():
        def spread(t, carry):
            e = emb[t].astype(jnp.float32)
            for i in range(heads):
                h_rows[pl.ds(i * steps + t, requests, stride=rows), :] = e[:, i * HD:(i + 1) * HD]
            return carry
        lax.fori_loop(0, steps, spread, 0)

        def first_sums(r, carry):
            ss_all[core, r] = row_sums(h_rows[pl.ds(pl.multiple_of(r * rows, rows), rows), :])
            return carry
        lax.fori_loop(0, requests, first_sums, 0)

    fk[...] = jnp.zeros_like(fk)
    fv[...] = jnp.zeros_like(fv)
    q_diag[...] = jnp.zeros_like(q_diag)

    @pl.when(section == 0)
    def _():
        for step in range(1, cores):
            peer_copy(step).start()

    hand_over(1, v_all)
    @pl.when(section == 0)
    def _():
        for step in range(1, cores):
            peer_arrival(lax.rem(core + step, cores)).wait_recv()

    def one_request(r, carry):
        @pl.when(section > 0)
        def _():
            next_copy(r).wait_recv()
            for other in range(cores):
                sum_arrival(r, other).wait_recv()
            h_rows[pl.ds(pl.multiple_of(r * rows, rows), rows), :] = h_in[r].astype(jnp.float32)

        squares = ss_all[0, r]
        for other in range(1, cores):
            squares = squares + ss_all[other, r]
        ratio = lax.rsqrt(squares / total_width + 1e-05)
        length = lens[inst, r]
        h = h_rows[pl.ds(pl.multiple_of(r * rows, rows), rows), :]
        x = h.reshape(rows // tile, tile, HD) * ratio[None] * gain_q[...].reshape(rows // tile, tile, HD)
        x = x.reshape(rows, HD)
        for g in range(heads_kv):
            lanes = slice(g * HD, (g + 1) * HD)
            span = slice(g * part, (g + 1) * part)
            key_sum = jnp.sum(x[span].reshape(part // tile, tile, HD), axis=0)
            value_sum = jnp.sum(h[span].reshape(part // tile, tile, HD), axis=0)
            fk[r, 0:steps, lanes] = (key_sum[:steps] + key_sum[steps:]) * (1.0 / share)
            fv[r, 0:steps, lanes] = (value_sum[:steps] + value_sum[steps:]) * (1.0 / share)
            q_diag[span, lanes] = x[span].astype(jnp.bfloat16)
        q = q_diag[...]
        row = lax.broadcasted_iota(jnp.int32, (blk, rows), 0)
        new_row = lax.broadcasted_iota(jnp.int32, (PAD, rows), 0)
        new_step = lax.rem(lax.broadcasted_iota(jnp.int32, (PAD, rows), 1), steps)
        scores = []
        for b in range(maxblk):
            s = lax.dot_general(k_all[tables[0, r, b]], q, NT, preferred_element_type=jnp.float32) * scale
            scores.append(jnp.where(row + b * blk < length, s, -jnp.inf))
        new = lax.dot_general(fk[r].astype(jnp.bfloat16), q, NT, preferred_element_type=jnp.float32) * scale
        new = jnp.where(new_row <= new_step, new, -jnp.inf)
        top = functools.reduce(jnp.maximum, scores)
        top = jnp.maximum(jnp.max(top, axis=0, keepdims=True), jnp.max(new, axis=0, keepdims=True))
        expo = [jnp.exp(s - top) for s in scores]
        expo_new = jnp.exp(new - top)
        total_weight = jnp.sum(functools.reduce(jnp.add, expo), axis=0, keepdims=True)
        total_weight = total_weight + jnp.sum(expo_new, axis=0, keepdims=True)
        inverse = 1.0 / total_weight
        weights = jnp.concatenate([(e * inverse).astype(jnp.bfloat16).T for e in expo], axis=1)
        weights_new = (expo_new * inverse).T.astype(jnp.bfloat16)
        values = [v_all[tables[0, r, b]] for b in range(maxblk)]
        fresh_values = fv[r].astype(jnp.bfloat16)
        outs = []
        for g in range(heads_kv):
            lanes = slice(g * HD, (g + 1) * HD)
            span = slice(g * part, (g + 1) * part)
            o = jnp.dot(weights[span], jnp.concatenate([v[:, lanes] for v in values], axis=0),
                        preferred_element_type=jnp.float32)
            o = o + jnp.dot(weights_new[span], fresh_values[:, lanes], preferred_element_type=jnp.float32)
            o = o * lax.rsqrt(jnp.mean(o * o, axis=-1, keepdims=True) + 1e-05)
            outs.append(o)
        y = (h + jnp.concatenate(outs, axis=0) * gain_o[...]).astype(jnp.bfloat16)
        res[r] = y
        y = y.astype(jnp.float32)
        y_rows[pl.ds(pl.multiple_of(r * rows, rows), rows), :] = y
        ss_out[r] = row_sums(y)

        @pl.when(section < sections - 1)
        def _():
            next_copy(r).start()
            for other in range(cores):
                next_sum(r, other).start()
        return carry

    lax.fori_loop(0, requests, one_request, 0)

    fresh[0] = fk[handed].astype(jnp.bfloat16)
    fresh[1] = fv[handed].astype(jnp.bfloat16)

    if spare > 0:
        for step in range(1, groups):
            count_copy(step, lax.rem(group + step, groups)).wait_recv()
        most = jnp.zeros(counts.shape[1:], jnp.int32)
        for pair in range(0, groups, 2):
            most = jnp.maximum(most, counts[pair] + counts[pair + 1])
        lane = lax.broadcasted_iota(jnp.int32, most.shape, 1)
        choice = 0
        for members in classes:
            own = functools.reduce(jnp.logical_or, [lane == i for i in members])
            need = jnp.max(jnp.where(own, most, 0))
            choice = choice * len(levels)
            for level in levels[:-1]:
                choice = choice + jnp.where(need > level, 1, 0)
        pick[0] = choice
    else:
        pick[0] = 0

    def collect(t, carry):
        for i in range(heads):
            turn[t, :, i * HD:(i + 1) * HD] = y_rows[pl.ds(i * steps + t, requests, stride=rows), :]
        out[0, t] = turn[t].astype(jnp.bfloat16)
        return carry
    lax.fori_loop(0, steps, collect, 0)

    for u in range(lead):
        own_copy(u).wait_recv()
    if spare > 0:
        for j in range(spare):
            moved_copy(j).wait_recv()
        for j in range(spare):
            moved_copy(j).wait_send()
        for step in range(1, groups):
            count_copy(step, group).wait_send()
    for u in range(lead):
        own_copy(u).wait_send()

    @pl.when(section == 0)
    def _():
        for step in range(1, cores):
            peer_copy(step).wait_send()

    @pl.when(section < sections - 1)
    def _():
        for r in range(requests):
            next_copy(r).wait_send()
            for other in range(cores):
                next_sum(r, other).wait_send()


def finish(offset, classes, chosen, lowest, lens_hbm, mig_hbm, send, moved, front, fresh_send,
           done,
           lens, mig_req, recv, mix, fresh, small_sem, mig_send, mig_recv, back_send, fresh_sem):
    inst = lax.axis_index("inst")
    group = lax.axis_index("groups")
    total, unit, _ = send.shape
    lead = front.shape[0]
    source = jnp.bitwise_xor(inst, offset)
    beside = jnp.bitwise_xor(group, 1)
    balanced = lowest < total

    def slots_of(i):
        if len(chosen) == 1:
            return chosen[0]
        slots = chosen[-1]
        for members, level in zip(classes[:-1], chosen[:-1]):
            for member in members:
                slots = jnp.where(i == member, level, slots)
        return slots

    going, coming = slots_of(inst), slots_of(source)
    sends, comes = going - lead, coming - lead
    mixed_out, mixed_in = total - going, total - coming

    small = [pltpu.make_async_copy(mig_hbm, mig_req, small_sem.at[0]), pltpu.make_async_copy(lens_hbm, lens, small_sem.at[1])]
    for copy in small:
        copy.start()
    barrier = pltpu.get_barrier_semaphore()
    pl.semaphore_signal(barrier, inc=1, device_id={"inst": source}, device_id_type=MESH)
    if balanced:
        pl.semaphore_signal(barrier, inc=1, device_id={"groups": beside}, device_id_type=MESH)
    for copy in small:
        copy.wait()
    pl.semaphore_wait(barrier, 2 if balanced else 1)

    def out_slot(i):
        return jnp.where(i < mixed_out, going - 1 - i, lead + i - mixed_out)

    def copy_from(ref, u):
        return pltpu.make_async_remote_copy(
            src_ref=ref, dst_ref=recv.at[u - lead],
            send_sem=mig_send.at[u - lead], recv_sem=mig_recv.at[u - lead],
            device_id={"inst": source}, device_id_type=MESH)

    def back_copy(j):
        return pltpu.make_async_remote_copy(
            src_ref=recv.at[coming - 1 - j - lead], dst_ref=recv.at[coming + j - lead],
            send_sem=back_send.at[j], recv_sem=mig_recv.at[coming + j - lead],
            device_id={"groups": beside}, device_id_type=MESH)

    fresh_copy = pltpu.make_async_remote_copy(
        src_ref=fresh_send, dst_ref=fresh, send_sem=fresh_sem.at[0], recv_sem=fresh_sem.at[1],
        device_id={"inst": source}, device_id_type=MESH)
    fresh_copy.start()
    handed_chunks = lax.div(lens[inst, mig_req[inst]] + (unit - 1), unit)
    source_len = lens[source, mig_req[source]]

    def put(i):
        u = out_slot(i)
        if balanced:
            @pl.when(i < mixed_out)
            def _():
                mix[i] = jnp.where(lax.div(u, KINDS) < handed_chunks, send[u], moved[going + i - lowest])
                copy_from(mix.at[i], u).start()

        @pl.when(i >= mixed_out)
        def _():
            copy_from(send.at[u], u).start()

    def settle(u, block):
        which, c = lax.rem(u, KINDS), lax.div(u, KINDS)
        done[which, c] = place(block, fresh[which], c * unit, source_len)

    def launch(i, carry):
        put(i)
        return carry
    lax.fori_loop(0, jnp.minimum(WINDOW, sends), launch, 0)
    fresh_copy.wait_recv()

    def settle_front(u, carry):
        settle(u, front[u])
        return carry
    lax.fori_loop(0, lead, settle_front, 0)

    def step(i, carry):
        u = jnp.where(i < comes, jnp.where(i < mixed_in, coming - 1 - i, lead + i - mixed_in), coming + i - comes)
        copy_from(send.at[u], u).wait_recv()
        if balanced:
            @pl.when(i < mixed_in)
            def _():
                back_copy(i).start()

        @pl.when(i < sends)
        def _():
            s = out_slot(i)
            copy_from(send.at[s], s).wait_send()

        @pl.when(i + WINDOW < sends)
        def _():
            put(i + WINDOW)
        settle(u, recv[u - lead])
        return carry
    lax.fori_loop(0, total - lead, step, 0)
    fresh_copy.wait_send()

    if balanced:
        def returned(j, carry):
            back_copy(j).wait_send()
            return carry
        lax.fori_loop(0, mixed_in, returned, 0)


def store(res, done, res_out, k_out, v_out, sems, res_sem):
    copies = [pltpu.make_async_copy(res, res_out, res_sem)]
    part = done.shape[1] // STORES
    for which, dst in enumerate((k_out, v_out)):
        for i in range(STORES):
            span = pl.ds(i * part, part)
            copies.append(pltpu.make_async_copy(done.at[which, span], dst.at[span], sems.at[which, i]))
    for copy in copies:
        copy.start()
    for copy in copies:
        copy.wait()


def local(emb, attn_gain, out_gain, k_cache, v_cache, tables, lens, partner, mig_req):
    steps, requests, width = emb.shape
    _, _, pool, blk, kv_local = k_cache.shape
    maxblk = tables.shape[2]
    total = KINDS * SPLIT * maxblk
    cores = lax.axis_size("tp")
    groups = lax.axis_size("groups")
    context = maxblk * blk
    heads_kv = kv_local // HD
    rows = width // HD * steps
    bf16, f32 = jnp.bfloat16, jnp.float32
    vmem = pl.BlockSpec(memory_space=pltpu.VMEM)
    smem = pl.BlockSpec(memory_space=pltpu.SMEM)
    hbm = pl.BlockSpec(memory_space=pltpu.HBM)
    anywhere = pl.BlockSpec(memory_space=pl.ANY)
    dma = pltpu.SemaphoreType.DMA
    offsets = lax.axis_size("inst") - 1
    instances = lax.axis_size("inst")
    lead = total // 4

    def plan(offset):
        together = [tuple(range(instances))]
        if groups % 2 != 0:
            return together, [total]
        if offsets > FEW:
            return together, [total - lead, total]
        if offsets == FEW and offset > 1:
            return [(0, 3), (1, 2)], list(range(total - total // 3, total + 1, total // 6))
        step = total // 12
        return together, [total - lead, total - lead + step // 2] + list(range(total - lead + step, total + 1, step))


    chunk = blk // SPLIT

    def unit(*count):
        return jax.ShapeDtypeStruct((*count, chunk, kv_local), bf16)

    def call_begin(offset):
        classes, levels = plan(offset)
        return pl.pallas_call(
            functools.partial(begin, offset, classes, levels),
            out_shape=(
                jax.ShapeDtypeStruct((1,), jnp.int32),
                jax.ShapeDtypeStruct((1, steps, requests, width), bf16),
                unit(total),
                unit(max(total - levels[0], 1)),
                jax.ShapeDtypeStruct((KINDS, PAD, kv_local), bf16),
                unit(lead),
            ),
            in_specs=[hbm] * 8,
            out_specs=(smem, vmem, vmem, vmem, vmem, vmem),
            scratch_shapes=[
                pltpu.SMEM(tables.shape, jnp.int32),
                pltpu.SMEM(lens.shape, jnp.int32),
                pltpu.SMEM(mig_req.shape, jnp.int32),
                pltpu.VMEM(emb.shape, bf16),
                pltpu.VMEM(attn_gain.shape, f32),
                pltpu.VMEM(out_gain.shape, f32),
                pltpu.VMEM((rows, HD), f32),
                pltpu.VMEM((rows, HD), f32),
                pltpu.VMEM((steps, requests, width), f32),
                pltpu.VMEM((pool, blk, kv_local), bf16),
                pltpu.VMEM((pool, blk, kv_local), bf16),
                pltpu.VMEM((groups, 8, 128), jnp.int32),
                pltpu.VMEM((requests * rows, HD), f32),
                pltpu.VMEM((requests * rows, HD), f32),
                pltpu.VMEM((requests, rows, HD), bf16),
                pltpu.VMEM((requests, rows, HD), bf16),
                pltpu.VMEM((cores, requests, 2 * steps, HD), f32),
                pltpu.VMEM((requests, 2 * steps, HD), f32),
                pltpu.VMEM((requests, PAD, kv_local), f32),
                pltpu.VMEM((requests, PAD, kv_local), f32),
                pltpu.VMEM((rows, heads_kv * HD), bf16),
                dma((6,)),
                dma((KINDS, LOADS)),
                dma((lead,)),
                dma((lead,)),
                dma((max(total - levels[0], 1),)),
                dma((max(total - levels[0], 1),)),
                dma((groups,)),
                dma((groups,)),
                dma((requests,)),
                dma((requests,)),
                dma((requests, cores)),
                dma((requests, cores)),
                dma((2, cores)),
            ],
            compiler_params=pltpu.CompilerParams(
                collective_id=offset - 1, has_side_effects=True, vmem_limit_bytes=LIMIT),
        )

    numbers = itertools.count(offsets)

    def call_finish(offset, chosen):
        classes, levels = plan(offset)
        return pl.pallas_call(
            functools.partial(finish, offset, classes, chosen, levels[0]),
            out_shape=unit(KINDS, total // KINDS),
            in_specs=[hbm] * 2 + [vmem] * 4,
            out_specs=vmem,
            scratch_shapes=[
                pltpu.SMEM(lens.shape, jnp.int32),
                pltpu.SMEM(mig_req.shape, jnp.int32),
                pltpu.VMEM((total - lead, chunk, kv_local), bf16),
                pltpu.VMEM((max(total - levels[0], 1), chunk, kv_local), bf16),
                pltpu.VMEM((KINDS, PAD, kv_local), bf16),
                dma((2,)),
                dma((total - lead,)),
                dma((total - lead,)),
                dma((max(total - levels[0], 1),)),
                dma((2,)),
            ],
            compiler_params=pltpu.CompilerParams(
                collective_id=next(numbers), has_side_effects=True, vmem_limit_bytes=LIMIT),
        )

    call_store = pl.pallas_call(
        store,
        out_shape=(
            jax.ShapeDtypeStruct((1, steps, requests, width), bf16),
            unit(total // KINDS),
            unit(total // KINDS),
        ),
        in_specs=[anywhere] * 2,
        out_specs=(hbm,) * 3,
        scratch_shapes=[dma((KINDS, STORES)), dma],
        compiler_params=pltpu.CompilerParams(vmem_limit_bytes=LIMIT),
    )

    def way(offset):
        def run(*operands):
            pick, out, send, moved, fresh, front = call_begin(offset)(*operands)

            classes, levels = plan(offset)
            combos = list(itertools.product(levels, repeat=len(classes)))

            def rest(chosen):
                def run_rest(lens, mig_req, out, send, moved, fresh, front):
                    return call_store(out, call_finish(offset, chosen)(lens, mig_req, send, moved, front, fresh))
                return run_rest
            res, k, v = lax.switch(
                pick[0], [rest(chosen) for chosen in combos],
                operands[1], operands[2], out, send, moved, fresh, front)
            return res, k.reshape(1, 1, context, kv_local), v.reshape(1, 1, context, kv_local)
        return run

    return tuple(lax.switch(
        partner[0] - 1, [way(offset) for offset in range(1, offsets + 1)],
        tables, lens, mig_req, emb, attn_gain, out_gain, k_cache, v_cache))


def solution(mesh):
    return jax.shard_map(
        local,
        mesh=mesh,
        in_specs=(
            P(None, ("groups", "inst"), "tp"),
            P("section", "tp"),
            P("section", "tp"),
            P(("groups", "inst"), "section", None, None, "tp"),
            P(("groups", "inst"), "section", None, None, "tp"),
            P(("groups", "inst"), None, None),
            P("groups", None),
            P(),
            P("groups"),
        ),
        out_specs=(
            P("section", None, ("groups", "inst"), "tp"),
            P(("groups", "inst"), "section", None, "tp"),
            P(("groups", "inst"), "section", None, "tp"),
        ),
        check_vma=False,
    )
```

```python
import functools
import itertools

import jax
import jax.numpy as jnp
from jax import lax
from jax.experimental import pallas as pl
from jax.experimental.pallas import tpu as pltpu
from jax.sharding import PartitionSpec as P

QH = 64
KVH = 8
HD = 128
LOADS = 3
STORES = 2
PAD = 8
KINDS = 2
SPLIT = 2
WINDOW = 4
LIMIT = 20 << 20
FEW = 3
EXTRA = 1
MESH = pl.DeviceIdType.MESH
NT = (((1,), (1,)), ((), ()))


def by_instance(i, values):
    chosen = values[-1]
    if len(set(values)) > 1:
        for k, value in enumerate(values[:-1]):
            chosen = jnp.where(i == k, value, chosen)
    return chosen


def place(block, fresh, first_row, source_len):
    blk, width = block.shape
    pos = lax.broadcasted_iota(jnp.int32, (blk, PAD), 0) + first_row - source_len
    hit = jnp.where(pos == lax.broadcasted_iota(jnp.int32, (blk, PAD), 1), 1.0, 0.0).astype(jnp.bfloat16)
    placed = jnp.dot(hit, fresh, preferred_element_type=jnp.float32)
    row = lax.broadcasted_iota(jnp.int32, (blk, width), 0) + first_row
    return jnp.where(row < source_len, block.astype(jnp.float32), placed).astype(jnp.bfloat16)


def begin(offset, classes, levels, leads, tables_hbm, lens_hbm, mig_hbm, emb_hbm, gain_attn_hbm, gain_out_hbm, k_hbm, v_hbm,
          pick, out, send, moved, fresh, recv,
          tables, lens, mig_req, emb, gain_attn, gain_out, gain_q, gain_o, turn,
          k_all, v_all, counts,
          h_rows, y_rows, res, h_in, ss_all, ss_out, fk, fv, q_diag,
          small_sem, load_sem, mig_send, mig_recv, moved_send, moved_recv, count_ssem, count_rsem,
          h_ssem, h_rsem, ss_ssem, ss_rsem, peer_sem):
    sections = lax.axis_size("section")
    cores = lax.axis_size("tp")
    groups = lax.axis_size("groups")
    section = lax.axis_index("section")
    core = lax.axis_index("tp")
    inst = lax.axis_index("inst")
    group = lax.axis_index("groups")
    steps, requests, width = emb.shape
    pool, blk, kv_local = k_all.shape
    instances = lens.shape[0]
    total, unit, _ = send.shape
    chunks = total // KINDS
    split = blk // unit
    maxblk = chunks // split
    spare = total - levels[0]
    lead = by_instance(inst, leads)
    heads_kv = kv_local // HD
    heads = width // HD
    share = QH // KVH
    rows = heads * steps
    part = share * steps
    scale = HD ** (-0.5)
    total_width = width * cores
    source = jnp.bitwise_xor(inst, offset)
    beside = jnp.bitwise_xor(group, 1)

    small = []
    for i, (src, dst) in enumerate((
            (mig_hbm, mig_req), (tables_hbm, tables), (lens_hbm, lens),
            (emb_hbm, emb), (gain_attn_hbm, gain_attn), (gain_out_hbm, gain_out))):
        small.append(pltpu.make_async_copy(src, dst, small_sem.at[i]))
    loads = []
    piece = pool // LOADS
    for which, (src, dst) in enumerate(((k_hbm, k_all), (v_hbm, v_all))):
        for i in range(LOADS):
            loads.append(pltpu.make_async_copy(
                src.at[0, 0, pl.ds(i * piece, piece)], dst.at[pl.ds(i * piece, piece)], load_sem.at[which, i]))
    for copy in small[:3] + loads[:LOADS] + small[3:] + loads[LOADS:]:
        copy.start()

    barrier = pltpu.get_barrier_semaphore()
    pl.semaphore_signal(barrier, inc=1, device_id={"inst": source}, device_id_type=MESH)
    greeted = cores
    if spare > 0:
        for step in range(1, groups):
            pl.semaphore_signal(barrier, inc=1, device_id={"groups": lax.rem(group + step, groups)}, device_id_type=MESH)
        greeted = greeted + groups - 1
    for step in range(1, cores):
        pl.semaphore_signal(barrier, inc=1, device_id={"tp": lax.rem(core + step, cores)}, device_id_type=MESH)

    @pl.when(section > 0)
    def _():
        for other in range(cores):
            pl.semaphore_signal(barrier, inc=1, device_id={"section": section - 1, "tp": other}, device_id_type=MESH)

    @pl.when(section < sections - 1)
    def _():
        for other in range(cores):
            pl.semaphore_signal(barrier, inc=1, device_id={"section": section + 1, "tp": other}, device_id_type=MESH)

    def peer_copy(step):
        return pltpu.make_async_remote_copy(
            src_ref=ss_all.at[core], dst_ref=ss_all.at[core],
            send_sem=peer_sem.at[0, step], recv_sem=peer_sem.at[1, core],
            device_id={"tp": lax.rem(core + step, cores)}, device_id_type=MESH)

    def peer_arrival(other):
        return pltpu.make_async_remote_copy(
            src_ref=ss_all.at[other], dst_ref=ss_all.at[other],
            send_sem=peer_sem.at[0, 0], recv_sem=peer_sem.at[1, other],
            device_id={"tp": lax.rem(core + 1, cores)}, device_id_type=MESH)

    def next_copy(r):
        return pltpu.make_async_remote_copy(
            src_ref=res.at[r], dst_ref=h_in.at[r],
            send_sem=h_ssem.at[r], recv_sem=h_rsem.at[r],
            device_id={"section": section + 1}, device_id_type=MESH)

    def next_sum(r, other):
        return pltpu.make_async_remote_copy(
            src_ref=ss_out.at[r], dst_ref=ss_all.at[core, r],
            send_sem=ss_ssem.at[r, other], recv_sem=ss_rsem.at[r, core],
            device_id={"section": section + 1, "tp": other}, device_id_type=MESH)

    def sum_arrival(r, other):
        return pltpu.make_async_remote_copy(
            src_ref=ss_out.at[r], dst_ref=ss_all.at[other, r],
            send_sem=ss_ssem.at[r, other], recv_sem=ss_rsem.at[r, other],
            device_id={"tp": lax.rem(core + 1, cores)}, device_id_type=MESH)

    def own_copy(u):
        return pltpu.make_async_remote_copy(
            src_ref=send.at[u], dst_ref=recv.at[u],
            send_sem=mig_send.at[u], recv_sem=mig_recv.at[u],
            device_id={"inst": source}, device_id_type=MESH)

    def moved_copy(j):
        return pltpu.make_async_remote_copy(
            src_ref=send.at[levels[0] + j], dst_ref=moved.at[j],
            send_sem=moved_send.at[j], recv_sem=moved_recv.at[j],
            device_id={"groups": beside}, device_id_type=MESH)

    def count_copy(step, slot):
        return pltpu.make_async_remote_copy(
            src_ref=counts.at[slot], dst_ref=counts.at[slot],
            send_sem=count_ssem.at[step], recv_sem=count_rsem.at[slot],
            device_id={"groups": lax.rem(group + step, groups)}, device_id_type=MESH)

    for copy in small[:3]:
        copy.wait()
    if spare > 0:
        lane = lax.broadcasted_iota(jnp.int32, counts.shape[1:], 1)
        held = jnp.zeros(counts.shape[1:], jnp.int32)
        for i in range(instances):
            held = jnp.where(lane == i, lax.div(lens[i, mig_req[i]] + (unit - 1), unit), held)
        counts[group] = held
    neighbours = jnp.minimum(section, 1) + jnp.minimum(sections - 1 - section, 1)
    pl.semaphore_wait(barrier, greeted + cores * neighbours)
    if spare > 0:
        for step in range(1, groups):
            count_copy(step, group).start()

    handed = mig_req[inst]
    def hand_over(which, stored):
        for i in range(LOADS):
            loads[which * LOADS + i].wait()

        def gather(c, carry):
            u = KINDS * c + which
            span = pl.ds(pl.multiple_of(lax.rem(c, split) * unit, unit), unit)
            send[u] = stored[tables[0, handed, lax.div(c, split)], span, :]

            @pl.when(u < lead)
            def _():
                own_copy(u).start()
            if spare > 0:
                @pl.when(u >= levels[0])
                def _():
                    moved_copy(u - levels[0]).start()
            return carry
        lax.fori_loop(0, chunks, gather, 0)

    hand_over(0, k_all)
    for copy in small[3:]:
        copy.wait()

    for i in range(heads):
        lanes = slice(i * HD, (i + 1) * HD)
        span = slice(i * steps, (i + 1) * steps)
        gain_q[span, :] = jnp.broadcast_to(gain_attn[0:1, lanes], (steps, HD))
        gain_o[span, :] = jnp.broadcast_to(gain_out[0:1, lanes], (steps, HD))

    tile = 2 * steps

    def row_sums(a):
        a = jnp.sum((a * a).reshape(rows // tile, tile, HD), axis=0)
        a = a[:steps] + a[steps:]
        a = jnp.broadcast_to(jnp.sum(a, axis=-1, keepdims=True), (steps, HD))
        return jnp.concatenate([a, a], axis=0)

    @pl.when(section == 0)
    def _():
        def spread(t, carry):
            e = emb[t].astype(jnp.float32)
            for i in range(heads):
                h_rows[pl.ds(i * steps + t, requests, stride=rows), :] = e[:, i * HD:(i + 1) * HD]
            return carry
        lax.fori_loop(0, steps, spread, 0)

        def first_sums(r, carry):
            ss_all[core, r] = row_sums(h_rows[pl.ds(pl.multiple_of(r * rows, rows), rows), :])
            return carry
        lax.fori_loop(0, requests, first_sums, 0)

    fk[...] = jnp.zeros_like(fk)
    fv[...] = jnp.zeros_like(fv)
    q_diag[...] = jnp.zeros_like(q_diag)

    @pl.when(section == 0)
    def _():
        for step in range(1, cores):
            peer_copy(step).start()

    hand_over(1, v_all)
    @pl.when(section == 0)
    def _():
        for step in range(1, cores):
            peer_arrival(lax.rem(core + step, cores)).wait_recv()

    def one_request(r, carry):
        @pl.when(section > 0)
        def _():
            next_copy(r).wait_recv()
            for other in range(cores):
                sum_arrival(r, other).wait_recv()
            h_rows[pl.ds(pl.multiple_of(r * rows, rows), rows), :] = h_in[r].astype(jnp.float32)

        squares = ss_all[0, r]
        for other in range(1, cores):
            squares = squares + ss_all[other, r]
        ratio = lax.rsqrt(squares / total_width + 1e-05)
        length = lens[inst, r]
        h = h_rows[pl.ds(pl.multiple_of(r * rows, rows), rows), :]
        x = h.reshape(rows // tile, tile, HD) * ratio[None] * gain_q[...].reshape(rows // tile, tile, HD)
        x = x.reshape(rows, HD)
        for g in range(heads_kv):
            lanes = slice(g * HD, (g + 1) * HD)
            span = slice(g * part, (g + 1) * part)
            key_sum = jnp.sum(x[span].reshape(part // tile, tile, HD), axis=0)
            value_sum = jnp.sum(h[span].reshape(part // tile, tile, HD), axis=0)
            fk[r, 0:steps, lanes] = (key_sum[:steps] + key_sum[steps:]) * (1.0 / share)
            fv[r, 0:steps, lanes] = (value_sum[:steps] + value_sum[steps:]) * (1.0 / share)
            q_diag[span, lanes] = x[span].astype(jnp.bfloat16)
        q = q_diag[...]
        row = lax.broadcasted_iota(jnp.int32, (blk, rows), 0)
        new_row = lax.broadcasted_iota(jnp.int32, (PAD, rows), 0)
        new_step = lax.rem(lax.broadcasted_iota(jnp.int32, (PAD, rows), 1), steps)
        scores = []
        for b in range(maxblk):
            s = lax.dot_general(k_all[tables[0, r, b]], q, NT, preferred_element_type=jnp.float32) * scale
            scores.append(jnp.where(row + b * blk < length, s, -jnp.inf))
        new = lax.dot_general(fk[r].astype(jnp.bfloat16), q, NT, preferred_element_type=jnp.float32) * scale
        new = jnp.where(new_row <= new_step, new, -jnp.inf)
        top = functools.reduce(jnp.maximum, scores)
        top = jnp.maximum(jnp.max(top, axis=0, keepdims=True), jnp.max(new, axis=0, keepdims=True))
        expo = [jnp.exp(s - top) for s in scores]
        expo_new = jnp.exp(new - top)
        total_weight = jnp.sum(functools.reduce(jnp.add, expo), axis=0, keepdims=True)
        total_weight = total_weight + jnp.sum(expo_new, axis=0, keepdims=True)
        inverse = 1.0 / total_weight
        weights = jnp.concatenate([(e * inverse).astype(jnp.bfloat16).T for e in expo], axis=1)
        weights_new = (expo_new * inverse).T.astype(jnp.bfloat16)
        values = [v_all[tables[0, r, b]] for b in range(maxblk)]
        fresh_values = fv[r].astype(jnp.bfloat16)
        outs = []
        for g in range(heads_kv):
            lanes = slice(g * HD, (g + 1) * HD)
            span = slice(g * part, (g + 1) * part)
            o = jnp.dot(weights[span], jnp.concatenate([v[:, lanes] for v in values], axis=0),
                        preferred_element_type=jnp.float32)
            o = o + jnp.dot(weights_new[span], fresh_values[:, lanes], preferred_element_type=jnp.float32)
            o = o * lax.rsqrt(jnp.mean(o * o, axis=-1, keepdims=True) + 1e-05)
            outs.append(o)
        y = (h + jnp.concatenate(outs, axis=0) * gain_o[...]).astype(jnp.bfloat16)
        res[r] = y
        y = y.astype(jnp.float32)
        y_rows[pl.ds(pl.multiple_of(r * rows, rows), rows), :] = y
        ss_out[r] = row_sums(y)

        @pl.when(section < sections - 1)
        def _():
            next_copy(r).start()
            for other in range(cores):
                next_sum(r, other).start()
        return carry

    lax.fori_loop(0, requests, one_request, 0)

    fresh[0] = fk[handed].astype(jnp.bfloat16)
    fresh[1] = fv[handed].astype(jnp.bfloat16)

    if spare > 0:
        for step in range(1, groups):
            count_copy(step, lax.rem(group + step, groups)).wait_recv()
        most = jnp.zeros(counts.shape[1:], jnp.int32)
        for pair in range(0, groups, 2):
            most = jnp.maximum(most, counts[pair] + counts[pair + 1])
        lane = lax.broadcasted_iota(jnp.int32, most.shape, 1)
        choice = 0
        for members in classes:
            own = functools.reduce(jnp.logical_or, [lane == i for i in members])
            need = jnp.max(jnp.where(own, most, 0))
            choice = choice * len(levels)
            for level in levels[:-1]:
                choice = choice + jnp.where(need > level, 1, 0)
        pick[0] = choice
    else:
        pick[0] = 0

    def collect(t, carry):
        for i in range(heads):
            turn[t, :, i * HD:(i + 1) * HD] = y_rows[pl.ds(i * steps + t, requests, stride=rows), :]
        out[0, t] = turn[t].astype(jnp.bfloat16)
        return carry
    lax.fori_loop(0, steps, collect, 0)

    def taken(u, carry):
        own_copy(u).wait_recv()
        return carry
    lax.fori_loop(0, lead, taken, 0)

    def given(u, carry):
        own_copy(u).wait_send()
        return carry
    lax.fori_loop(0, lead, given, 0)
    if spare > 0:
        for j in range(spare):
            moved_copy(j).wait_recv()
        for j in range(spare):
            moved_copy(j).wait_send()
        for step in range(1, groups):
            count_copy(step, group).wait_send()

    @pl.when(section == 0)
    def _():
        for step in range(1, cores):
            peer_copy(step).wait_send()

    @pl.when(section < sections - 1)
    def _():
        for r in range(requests):
            next_copy(r).wait_send()
            for other in range(cores):
                next_sum(r, other).wait_send()


def finish(offset, classes, chosen, lowest, leads, lens_hbm, mig_hbm, send, moved, front, fresh_send,
           done,
           lens, mig_req, recv, mix, fresh, small_sem, mig_send, mig_recv, back_send, fresh_sem):
    inst = lax.axis_index("inst")
    group = lax.axis_index("groups")
    total, unit, _ = send.shape
    lead, least = by_instance(inst, leads), min(leads)
    source = jnp.bitwise_xor(inst, offset)
    beside = jnp.bitwise_xor(group, 1)
    balanced = lowest < total

    def slots_of(i):
        return by_instance(i, [
            level for k in range(len(leads)) for members, level in zip(classes, chosen) if k in members])

    going, coming = slots_of(inst), slots_of(source)
    sends, comes = going - lead, coming - lead
    mixed_out, mixed_in = total - going, total - coming

    small = [pltpu.make_async_copy(mig_hbm, mig_req, small_sem.at[0]), pltpu.make_async_copy(lens_hbm, lens, small_sem.at[1])]
    for copy in small:
        copy.start()
    barrier = pltpu.get_barrier_semaphore()
    pl.semaphore_signal(barrier, inc=1, device_id={"inst": source}, device_id_type=MESH)
    if balanced:
        pl.semaphore_signal(barrier, inc=1, device_id={"groups": beside}, device_id_type=MESH)
    for copy in small:
        copy.wait()
    pl.semaphore_wait(barrier, 2 if balanced else 1)

    def out_slot(i):
        return jnp.where(i < mixed_out, going - 1 - i, lead + i - mixed_out)

    def copy_from(ref, u):
        return pltpu.make_async_remote_copy(
            src_ref=ref, dst_ref=recv.at[u - least],
            send_sem=mig_send.at[u - least], recv_sem=mig_recv.at[u - least],
            device_id={"inst": source}, device_id_type=MESH)

    def back_copy(j):
        return pltpu.make_async_remote_copy(
            src_ref=recv.at[coming - 1 - j - least], dst_ref=recv.at[coming + j - least],
            send_sem=back_send.at[j], recv_sem=mig_recv.at[coming + j - least],
            device_id={"groups": beside}, device_id_type=MESH)

    fresh_copy = pltpu.make_async_remote_copy(
        src_ref=fresh_send, dst_ref=fresh, send_sem=fresh_sem.at[0], recv_sem=fresh_sem.at[1],
        device_id={"inst": source}, device_id_type=MESH)
    fresh_copy.start()
    handed_chunks = lax.div(lens[inst, mig_req[inst]] + (unit - 1), unit)
    source_len = lens[source, mig_req[source]]

    def put(i):
        u = out_slot(i)
        if balanced:
            @pl.when(i < mixed_out)
            def _():
                mix[i] = jnp.where(lax.div(u, KINDS) < handed_chunks, send[u], moved[going + i - lowest])
                copy_from(mix.at[i], u).start()

        @pl.when(i >= mixed_out)
        def _():
            copy_from(send.at[u], u).start()

    def settle(u, block):
        which, c = lax.rem(u, KINDS), lax.div(u, KINDS)
        done[which, c] = place(block, fresh[which], c * unit, source_len)

    def launch(i, carry):
        put(i)
        return carry
    lax.fori_loop(0, jnp.minimum(WINDOW, sends), launch, 0)
    fresh_copy.wait_recv()

    def settle_front(u, carry):
        settle(u, front[u])
        return carry
    lax.fori_loop(0, lead, settle_front, 0)

    def step(i, carry):
        u = jnp.where(i < comes, jnp.where(i < mixed_in, coming - 1 - i, lead + i - mixed_in), coming + i - comes)
        copy_from(send.at[u], u).wait_recv()
        if balanced:
            @pl.when(i < mixed_in)
            def _():
                back_copy(i).start()

        @pl.when(i < sends)
        def _():
            s = out_slot(i)
            copy_from(send.at[s], s).wait_send()

        @pl.when(i + WINDOW < sends)
        def _():
            put(i + WINDOW)
        settle(u, recv[u - least])
        return carry
    lax.fori_loop(0, total - lead, step, 0)
    fresh_copy.wait_send()

    if balanced:
        def returned(j, carry):
            back_copy(j).wait_send()
            return carry
        lax.fori_loop(0, mixed_in, returned, 0)


def store(res, done, res_out, k_out, v_out, sems, res_sem):
    copies = [pltpu.make_async_copy(res, res_out, res_sem)]
    part = done.shape[1] // STORES
    for which, dst in enumerate((k_out, v_out)):
        for i in range(STORES):
            span = pl.ds(i * part, part)
            copies.append(pltpu.make_async_copy(done.at[which, span], dst.at[span], sems.at[which, i]))
    for copy in copies:
        copy.start()
    for copy in copies:
        copy.wait()


def local(emb, attn_gain, out_gain, k_cache, v_cache, tables, lens, partner, mig_req):
    steps, requests, width = emb.shape
    _, _, pool, blk, kv_local = k_cache.shape
    maxblk = tables.shape[2]
    total = KINDS * SPLIT * maxblk
    cores = lax.axis_size("tp")
    groups = lax.axis_size("groups")
    context = maxblk * blk
    heads_kv = kv_local // HD
    rows = width // HD * steps
    bf16, f32 = jnp.bfloat16, jnp.float32
    vmem = pl.BlockSpec(memory_space=pltpu.VMEM)
    smem = pl.BlockSpec(memory_space=pltpu.SMEM)
    hbm = pl.BlockSpec(memory_space=pltpu.HBM)
    anywhere = pl.BlockSpec(memory_space=pl.ANY)
    dma = pltpu.SemaphoreType.DMA
    offsets = lax.axis_size("inst") - 1
    instances = lax.axis_size("inst")
    lead = total // 4

    def first_units(offset):
        return [lead + EXTRA if offsets == FEW and offset == 1 else lead] * instances

    def plan(offset):
        together = [tuple(range(instances))]
        if groups % 2 != 0:
            return together, [total]
        if offsets > FEW:
            return together, [total - lead, total]
        if offsets == FEW and offset > 1:
            return [(0, 3), (1, 2)], list(range(total - total // 3, total + 1, total // 6))
        step = total // 12
        return together, [total - lead, total - lead + step // 2] + list(range(total - lead + step, total + 1, step))


    chunk = blk // SPLIT

    def unit(*count):
        return jax.ShapeDtypeStruct((*count, chunk, kv_local), bf16)

    def call_begin(offset):
        classes, levels = plan(offset)
        leads = first_units(offset)
        return pl.pallas_call(
            functools.partial(begin, offset, classes, levels, leads),
            out_shape=(
                jax.ShapeDtypeStruct((1,), jnp.int32),
                jax.ShapeDtypeStruct((1, steps, requests, width), bf16),
                unit(total),
                unit(max(total - levels[0], 1)),
                jax.ShapeDtypeStruct((KINDS, PAD, kv_local), bf16),
                unit(max(leads)),
            ),
            in_specs=[hbm] * 8,
            out_specs=(smem, vmem, vmem, vmem, vmem, vmem),
            scratch_shapes=[
                pltpu.SMEM(tables.shape, jnp.int32),
                pltpu.SMEM(lens.shape, jnp.int32),
                pltpu.SMEM(mig_req.shape, jnp.int32),
                pltpu.VMEM(emb.shape, bf16),
                pltpu.VMEM(attn_gain.shape, f32),
                pltpu.VMEM(out_gain.shape, f32),
                pltpu.VMEM((rows, HD), f32),
                pltpu.VMEM((rows, HD), f32),
                pltpu.VMEM((steps, requests, width), f32),
                pltpu.VMEM((pool, blk, kv_local), bf16),
                pltpu.VMEM((pool, blk, kv_local), bf16),
                pltpu.VMEM((groups, 8, 128), jnp.int32),
                pltpu.VMEM((requests * rows, HD), f32),
                pltpu.VMEM((requests * rows, HD), f32),
                pltpu.VMEM((requests, rows, HD), bf16),
                pltpu.VMEM((requests, rows, HD), bf16),
                pltpu.VMEM((cores, requests, 2 * steps, HD), f32),
                pltpu.VMEM((requests, 2 * steps, HD), f32),
                pltpu.VMEM((requests, PAD, kv_local), f32),
                pltpu.VMEM((requests, PAD, kv_local), f32),
                pltpu.VMEM((rows, heads_kv * HD), bf16),
                dma((6,)),
                dma((KINDS, LOADS)),
                dma((max(leads),)),
                dma((max(leads),)),
                dma((max(total - levels[0], 1),)),
                dma((max(total - levels[0], 1),)),
                dma((groups,)),
                dma((groups,)),
                dma((requests,)),
                dma((requests,)),
                dma((requests, cores)),
                dma((requests, cores)),
                dma((2, cores)),
            ],
            compiler_params=pltpu.CompilerParams(
                collective_id=offset - 1, has_side_effects=True, vmem_limit_bytes=LIMIT),
        )

    numbers = itertools.count(offsets)

    def call_finish(offset, chosen):
        classes, levels = plan(offset)
        leads = first_units(offset)
        return pl.pallas_call(
            functools.partial(finish, offset, classes, chosen, levels[0], leads),
            out_shape=unit(KINDS, total // KINDS),
            in_specs=[hbm] * 2 + [vmem] * 4,
            out_specs=vmem,
            scratch_shapes=[
                pltpu.SMEM(lens.shape, jnp.int32),
                pltpu.SMEM(mig_req.shape, jnp.int32),
                pltpu.VMEM((total - min(leads), chunk, kv_local), bf16),
                pltpu.VMEM((max(total - levels[0], 1), chunk, kv_local), bf16),
                pltpu.VMEM((KINDS, PAD, kv_local), bf16),
                dma((2,)),
                dma((total - min(leads),)),
                dma((total - min(leads),)),
                dma((max(total - levels[0], 1),)),
                dma((2,)),
            ],
            compiler_params=pltpu.CompilerParams(
                collective_id=next(numbers), has_side_effects=True, vmem_limit_bytes=LIMIT),
        )

    call_store = pl.pallas_call(
        store,
        out_shape=(
            jax.ShapeDtypeStruct((1, steps, requests, width), bf16),
            unit(total // KINDS),
            unit(total // KINDS),
        ),
        in_specs=[anywhere] * 2,
        out_specs=(hbm,) * 3,
        scratch_shapes=[dma((KINDS, STORES)), dma],
        compiler_params=pltpu.CompilerParams(vmem_limit_bytes=LIMIT),
    )

    def way(offset):
        def run(*operands):
            pick, out, send, moved, fresh, front = call_begin(offset)(*operands)

            classes, levels = plan(offset)
            combos = list(itertools.product(levels, repeat=len(classes)))

            def rest(chosen):
                def run_rest(lens, mig_req, out, send, moved, fresh, front):
                    return call_store(out, call_finish(offset, chosen)(lens, mig_req, send, moved, front, fresh))
                return run_rest
            res, k, v = lax.switch(
                pick[0], [rest(chosen) for chosen in combos],
                operands[1], operands[2], out, send, moved, fresh, front)
            return res, k.reshape(1, 1, context, kv_local), v.reshape(1, 1, context, kv_local)
        return run

    return tuple(lax.switch(
        partner[0] - 1, [way(offset) for offset in range(1, offsets + 1)],
        tables, lens, mig_req, emb, attn_gain, out_gain, k_cache, v_cache))


def solution(mesh):
    return jax.shard_map(
        local,
        mesh=mesh,
        in_specs=(
            P(None, ("groups", "inst"), "tp"),
            P("section", "tp"),
            P("section", "tp"),
            P(("groups", "inst"), "section", None, None, "tp"),
            P(("groups", "inst"), "section", None, None, "tp"),
            P(("groups", "inst"), None, None),
            P("groups", None),
            P(),
            P("groups"),
        ),
        out_specs=(
            P("section", None, ("groups", "inst"), "tp"),
            P(("groups", "inst"), "section", None, "tp"),
            P(("groups", "inst"), "section", None, "tp"),
        ),
        check_vma=False,
    )
```

```python
import functools
import itertools

import jax
import jax.numpy as jnp
from jax import lax
from jax.experimental import pallas as pl
from jax.experimental.pallas import tpu as pltpu
from jax.sharding import PartitionSpec as P

QH = 64
KVH = 8
HD = 128
LOADS = 3
STORES = 2
PAD = 8
KINDS = 2
SPLIT = 2
WINDOW = 4
LIMIT = 20 << 20
FEW = 3
EXTRA = 1
MESH = pl.DeviceIdType.MESH
NT = (((1,), (1,)), ((), ()))


def by_instance(i, values):
    chosen = values[-1]
    if len(set(values)) > 1:
        for k, value in enumerate(values[:-1]):
            chosen = jnp.where(i == k, value, chosen)
    return chosen


def place(block, fresh, first_row, source_len):
    blk, width = block.shape
    pos = lax.broadcasted_iota(jnp.int32, (blk, PAD), 0) + first_row - source_len
    hit = jnp.where(pos == lax.broadcasted_iota(jnp.int32, (blk, PAD), 1), 1.0, 0.0).astype(jnp.bfloat16)
    placed = jnp.dot(hit, fresh, preferred_element_type=jnp.float32)
    row = lax.broadcasted_iota(jnp.int32, (blk, width), 0) + first_row
    return jnp.where(row < source_len, block.astype(jnp.float32), placed).astype(jnp.bfloat16)


def begin(offset, classes, levels, leads, tables_hbm, lens_hbm, mig_hbm, emb_hbm, gain_attn_hbm, gain_out_hbm, k_hbm, v_hbm,
          pick, out, send, moved, fresh, recv,
          tables, lens, mig_req, emb, gain_attn, gain_out, gain_q, gain_o, turn,
          k_all, v_all, counts,
          h_rows, y_rows, res, h_in, ss_all, ss_out, fk, fv, q_diag,
          small_sem, load_sem, mig_send, mig_recv, moved_send, moved_recv, count_ssem, count_rsem,
          h_ssem, h_rsem, ss_ssem, ss_rsem, peer_sem):
    sections = lax.axis_size("section")
    cores = lax.axis_size("tp")
    groups = lax.axis_size("groups")
    section = lax.axis_index("section")
    core = lax.axis_index("tp")
    inst = lax.axis_index("inst")
    group = lax.axis_index("groups")
    steps, requests, width = emb.shape
    pool, blk, kv_local = k_all.shape
    instances = lens.shape[0]
    total, unit, _ = send.shape
    chunks = total // KINDS
    split = blk // unit
    maxblk = chunks // split
    spare = total - levels[0]
    lead = by_instance(inst, leads)
    heads_kv = kv_local // HD
    heads = width // HD
    share = QH // KVH
    rows = heads * steps
    part = share * steps
    scale = HD ** (-0.5)
    total_width = width * cores
    source = jnp.bitwise_xor(inst, offset)
    beside = jnp.bitwise_xor(group, 1)

    small = []
    for i, (src, dst) in enumerate((
            (mig_hbm, mig_req), (tables_hbm, tables), (lens_hbm, lens),
            (emb_hbm, emb), (gain_attn_hbm, gain_attn), (gain_out_hbm, gain_out))):
        small.append(pltpu.make_async_copy(src, dst, small_sem.at[i]))
    loads = []
    piece = pool // LOADS
    for which, (src, dst) in enumerate(((k_hbm, k_all), (v_hbm, v_all))):
        for i in range(LOADS):
            loads.append(pltpu.make_async_copy(
                src.at[0, 0, pl.ds(i * piece, piece)], dst.at[pl.ds(i * piece, piece)], load_sem.at[which, i]))
    for copy in small[:3] + loads[:LOADS] + small[3:] + loads[LOADS:]:
        copy.start()

    barrier = pltpu.get_barrier_semaphore()
    pl.semaphore_signal(barrier, inc=1, device_id={"inst": source}, device_id_type=MESH)
    greeted = cores
    if spare > 0:
        for step in range(1, groups):
            pl.semaphore_signal(barrier, inc=1, device_id={"groups": lax.rem(group + step, groups)}, device_id_type=MESH)
        greeted = greeted + groups - 1
    for step in range(1, cores):
        pl.semaphore_signal(barrier, inc=1, device_id={"tp": lax.rem(core + step, cores)}, device_id_type=MESH)

    @pl.when(section > 0)
    def _():
        for other in range(cores):
            pl.semaphore_signal(barrier, inc=1, device_id={"section": section - 1, "tp": other}, device_id_type=MESH)

    @pl.when(section < sections - 1)
    def _():
        for other in range(cores):
            pl.semaphore_signal(barrier, inc=1, device_id={"section": section + 1, "tp": other}, device_id_type=MESH)

    def peer_copy(step):
        return pltpu.make_async_remote_copy(
            src_ref=ss_all.at[core], dst_ref=ss_all.at[core],
            send_sem=peer_sem.at[0, step], recv_sem=peer_sem.at[1, core],
            device_id={"tp": lax.rem(core + step, cores)}, device_id_type=MESH)

    def peer_arrival(other):
        return pltpu.make_async_remote_copy(
            src_ref=ss_all.at[other], dst_ref=ss_all.at[other],
            send_sem=peer_sem.at[0, 0], recv_sem=peer_sem.at[1, other],
            device_id={"tp": lax.rem(core + 1, cores)}, device_id_type=MESH)

    def next_copy(r):
        return pltpu.make_async_remote_copy(
            src_ref=res.at[r], dst_ref=h_in.at[r],
            send_sem=h_ssem.at[r], recv_sem=h_rsem.at[r],
            device_id={"section": section + 1}, device_id_type=MESH)

    def next_sum(r, other):
        return pltpu.make_async_remote_copy(
            src_ref=ss_out.at[r], dst_ref=ss_all.at[core, r],
            send_sem=ss_ssem.at[r, other], recv_sem=ss_rsem.at[r, core],
            device_id={"section": section + 1, "tp": other}, device_id_type=MESH)

    def sum_arrival(r, other):
        return pltpu.make_async_remote_copy(
            src_ref=ss_out.at[r], dst_ref=ss_all.at[other, r],
            send_sem=ss_ssem.at[r, other], recv_sem=ss_rsem.at[r, other],
            device_id={"tp": lax.rem(core + 1, cores)}, device_id_type=MESH)

    def own_copy(u):
        return pltpu.make_async_remote_copy(
            src_ref=send.at[u], dst_ref=recv.at[u],
            send_sem=mig_send.at[u], recv_sem=mig_recv.at[u],
            device_id={"inst": source}, device_id_type=MESH)

    def moved_copy(j):
        return pltpu.make_async_remote_copy(
            src_ref=send.at[levels[0] + j], dst_ref=moved.at[j],
            send_sem=moved_send.at[j], recv_sem=moved_recv.at[j],
            device_id={"groups": beside}, device_id_type=MESH)

    def count_copy(step, slot):
        return pltpu.make_async_remote_copy(
            src_ref=counts.at[slot], dst_ref=counts.at[slot],
            send_sem=count_ssem.at[step], recv_sem=count_rsem.at[slot],
            device_id={"groups": lax.rem(group + step, groups)}, device_id_type=MESH)

    for copy in small[:3]:
        copy.wait()
    if spare > 0:
        lane = lax.broadcasted_iota(jnp.int32, counts.shape[1:], 1)
        held = jnp.zeros(counts.shape[1:], jnp.int32)
        for i in range(instances):
            held = jnp.where(lane == i, lax.div(lens[i, mig_req[i]] + (unit - 1), unit), held)
        counts[group] = held
    neighbours = jnp.minimum(section, 1) + jnp.minimum(sections - 1 - section, 1)
    pl.semaphore_wait(barrier, greeted + cores * neighbours)
    if spare > 0:
        for step in range(1, groups):
            count_copy(step, group).start()

    handed = mig_req[inst]
    def hand_over(which, stored):
        for i in range(LOADS):
            loads[which * LOADS + i].wait()

        def gather(c, carry):
            u = KINDS * c + which
            span = pl.ds(pl.multiple_of(lax.rem(c, split) * unit, unit), unit)
            send[u] = stored[tables[0, handed, lax.div(c, split)], span, :]

            @pl.when(u < lead)
            def _():
                own_copy(u).start()
            if spare > 0:
                @pl.when(u >= levels[0])
                def _():
                    moved_copy(u - levels[0]).start()
            return carry
        lax.fori_loop(0, chunks, gather, 0)

    hand_over(0, k_all)
    for copy in small[3:]:
        copy.wait()

    for i in range(heads):
        lanes = slice(i * HD, (i + 1) * HD)
        span = slice(i * steps, (i + 1) * steps)
        gain_q[span, :] = jnp.broadcast_to(gain_attn[0:1, lanes], (steps, HD))
        gain_o[span, :] = jnp.broadcast_to(gain_out[0:1, lanes], (steps, HD))

    tile = 2 * steps

    def row_sums(a):
        a = jnp.sum((a * a).reshape(rows // tile, tile, HD), axis=0)
        a = a[:steps] + a[steps:]
        a = jnp.broadcast_to(jnp.sum(a, axis=-1, keepdims=True), (steps, HD))
        return jnp.concatenate([a, a], axis=0)

    @pl.when(section == 0)
    def _():
        def spread(t, carry):
            e = emb[t].astype(jnp.float32)
            for i in range(heads):
                h_rows[pl.ds(i * steps + t, requests, stride=rows), :] = e[:, i * HD:(i + 1) * HD]
            return carry
        lax.fori_loop(0, steps, spread, 0)

        def first_sums(r, carry):
            ss_all[core, r] = row_sums(h_rows[pl.ds(pl.multiple_of(r * rows, rows), rows), :])
            return carry
        lax.fori_loop(0, requests, first_sums, 0)

    fk[...] = jnp.zeros_like(fk)
    fv[...] = jnp.zeros_like(fv)
    q_diag[...] = jnp.zeros_like(q_diag)

    @pl.when(section == 0)
    def _():
        for step in range(1, cores):
            peer_copy(step).start()

    hand_over(1, v_all)
    @pl.when(section == 0)
    def _():
        for step in range(1, cores):
            peer_arrival(lax.rem(core + step, cores)).wait_recv()

    def one_request(r, carry):
        @pl.when(section > 0)
        def _():
            next_copy(r).wait_recv()
            for other in range(cores):
                sum_arrival(r, other).wait_recv()
            h_rows[pl.ds(pl.multiple_of(r * rows, rows), rows), :] = h_in[r].astype(jnp.float32)

        squares = ss_all[0, r]
        for other in range(1, cores):
            squares = squares + ss_all[other, r]
        ratio = lax.rsqrt(squares / total_width + 1e-05)
        length = lens[inst, r]
        h = h_rows[pl.ds(pl.multiple_of(r * rows, rows), rows), :]
        x = h.reshape(rows // tile, tile, HD) * ratio[None] * gain_q[...].reshape(rows // tile, tile, HD)
        x = x.reshape(rows, HD)
        for g in range(heads_kv):
            lanes = slice(g * HD, (g + 1) * HD)
            span = slice(g * part, (g + 1) * part)
            key_sum = jnp.sum(x[span].reshape(part // tile, tile, HD), axis=0)
            value_sum = jnp.sum(h[span].reshape(part // tile, tile, HD), axis=0)
            fk[r, 0:steps, lanes] = (key_sum[:steps] + key_sum[steps:]) * (1.0 / share)
            fv[r, 0:steps, lanes] = (value_sum[:steps] + value_sum[steps:]) * (1.0 / share)
            q_diag[span, lanes] = x[span].astype(jnp.bfloat16)
        q = q_diag[...]
        row = lax.broadcasted_iota(jnp.int32, (blk, rows), 0)
        new_row = lax.broadcasted_iota(jnp.int32, (PAD, rows), 0)
        new_step = lax.rem(lax.broadcasted_iota(jnp.int32, (PAD, rows), 1), steps)
        scores = []
        for b in range(maxblk):
            s = lax.dot_general(k_all[tables[0, r, b]], q, NT, preferred_element_type=jnp.float32) * scale
            scores.append(jnp.where(row + b * blk < length, s, -jnp.inf))
        new = lax.dot_general(fk[r].astype(jnp.bfloat16), q, NT, preferred_element_type=jnp.float32) * scale
        new = jnp.where(new_row <= new_step, new, -jnp.inf)
        top = functools.reduce(jnp.maximum, scores)
        top = jnp.maximum(jnp.max(top, axis=0, keepdims=True), jnp.max(new, axis=0, keepdims=True))
        expo = [jnp.exp(s - top) for s in scores]
        expo_new = jnp.exp(new - top)
        total_weight = jnp.sum(functools.reduce(jnp.add, expo), axis=0, keepdims=True)
        total_weight = total_weight + jnp.sum(expo_new, axis=0, keepdims=True)
        inverse = 1.0 / total_weight
        weights = jnp.concatenate([(e * inverse).astype(jnp.bfloat16).T for e in expo], axis=1)
        weights_new = (expo_new * inverse).T.astype(jnp.bfloat16)
        values = [v_all[tables[0, r, b]] for b in range(maxblk)]
        fresh_values = fv[r].astype(jnp.bfloat16)
        outs = []
        for g in range(heads_kv):
            lanes = slice(g * HD, (g + 1) * HD)
            span = slice(g * part, (g + 1) * part)
            o = jnp.dot(weights[span], jnp.concatenate([v[:, lanes] for v in values], axis=0),
                        preferred_element_type=jnp.float32)
            o = o + jnp.dot(weights_new[span], fresh_values[:, lanes], preferred_element_type=jnp.float32)
            o = o * lax.rsqrt(jnp.mean(o * o, axis=-1, keepdims=True) + 1e-05)
            outs.append(o)
        y = (h + jnp.concatenate(outs, axis=0) * gain_o[...]).astype(jnp.bfloat16)
        res[r] = y
        y = y.astype(jnp.float32)
        y_rows[pl.ds(pl.multiple_of(r * rows, rows), rows), :] = y
        ss_out[r] = row_sums(y)

        @pl.when(section < sections - 1)
        def _():
            next_copy(r).start()
            for other in range(cores):
                next_sum(r, other).start()
        return carry

    lax.fori_loop(0, requests, one_request, 0)

    fresh[0] = fk[handed].astype(jnp.bfloat16)
    fresh[1] = fv[handed].astype(jnp.bfloat16)

    if spare > 0:
        for step in range(1, groups):
            count_copy(step, lax.rem(group + step, groups)).wait_recv()
        most = jnp.zeros(counts.shape[1:], jnp.int32)
        for pair in range(0, groups, 2):
            most = jnp.maximum(most, counts[pair] + counts[pair + 1])
        lane = lax.broadcasted_iota(jnp.int32, most.shape, 1)
        choice = 0
        for members in classes:
            own = functools.reduce(jnp.logical_or, [lane == i for i in members])
            need = jnp.max(jnp.where(own, most, 0))
            choice = choice * len(levels)
            for level in levels[:-1]:
                choice = choice + jnp.where(need > level, 1, 0)
        pick[0] = choice
    else:
        pick[0] = 0

    def collect(t, carry):
        for i in range(heads):
            turn[t, :, i * HD:(i + 1) * HD] = y_rows[pl.ds(i * steps + t, requests, stride=rows), :]
        out[0, t] = turn[t].astype(jnp.bfloat16)
        return carry
    lax.fori_loop(0, steps, collect, 0)

    def taken(u, carry):
        own_copy(u).wait_recv()
        return carry
    lax.fori_loop(0, lead, taken, 0)

    def given(u, carry):
        own_copy(u).wait_send()
        return carry
    lax.fori_loop(0, lead, given, 0)
    if spare > 0:
        for j in range(spare):
            moved_copy(j).wait_recv()
        for j in range(spare):
            moved_copy(j).wait_send()
        for step in range(1, groups):
            count_copy(step, group).wait_send()

    @pl.when(section == 0)
    def _():
        for step in range(1, cores):
            peer_copy(step).wait_send()

    @pl.when(section < sections - 1)
    def _():
        for r in range(requests):
            next_copy(r).wait_send()
            for other in range(cores):
                next_sum(r, other).wait_send()


def finish(offset, classes, chosen, lowest, leads, lens_hbm, mig_hbm, send, moved, front, fresh_send,
           done,
           lens, mig_req, recv, mix, fresh, small_sem, mig_send, mig_recv, back_send, fresh_sem):
    inst = lax.axis_index("inst")
    group = lax.axis_index("groups")
    total, unit, _ = send.shape
    lead, least = by_instance(inst, leads), min(leads)
    source = jnp.bitwise_xor(inst, offset)
    beside = jnp.bitwise_xor(group, 1)
    balanced = lowest < total

    def slots_of(i):
        return by_instance(i, [
            level for k in range(len(leads)) for members, level in zip(classes, chosen) if k in members])

    going, coming = slots_of(inst), slots_of(source)
    sends, comes = going - lead, coming - lead
    mixed_out, mixed_in = total - going, total - coming

    small = [pltpu.make_async_copy(mig_hbm, mig_req, small_sem.at[0]), pltpu.make_async_copy(lens_hbm, lens, small_sem.at[1])]
    for copy in small:
        copy.start()
    barrier = pltpu.get_barrier_semaphore()
    pl.semaphore_signal(barrier, inc=1, device_id={"inst": source}, device_id_type=MESH)
    if balanced:
        pl.semaphore_signal(barrier, inc=1, device_id={"groups": beside}, device_id_type=MESH)
    for copy in small:
        copy.wait()
    pl.semaphore_wait(barrier, 2 if balanced else 1)

    def out_slot(i):
        return jnp.where(i < mixed_out, going - 1 - i, lead + i - mixed_out)

    def copy_from(ref, u):
        return pltpu.make_async_remote_copy(
            src_ref=ref, dst_ref=recv.at[u - least],
            send_sem=mig_send.at[u - least], recv_sem=mig_recv.at[u - least],
            device_id={"inst": source}, device_id_type=MESH)

    def back_copy(j):
        return pltpu.make_async_remote_copy(
            src_ref=recv.at[coming - 1 - j - least], dst_ref=recv.at[coming + j - least],
            send_sem=back_send.at[j], recv_sem=mig_recv.at[coming + j - least],
            device_id={"groups": beside}, device_id_type=MESH)

    fresh_copy = pltpu.make_async_remote_copy(
        src_ref=fresh_send, dst_ref=fresh, send_sem=fresh_sem.at[0], recv_sem=fresh_sem.at[1],
        device_id={"inst": source}, device_id_type=MESH)
    fresh_copy.start()
    handed_chunks = lax.div(lens[inst, mig_req[inst]] + (unit - 1), unit)
    source_len = lens[source, mig_req[source]]

    def put(i):
        u = out_slot(i)
        if balanced:
            @pl.when(i < mixed_out)
            def _():
                mix[i] = jnp.where(lax.div(u, KINDS) < handed_chunks, send[u], moved[going + i - lowest])
                copy_from(mix.at[i], u).start()

        @pl.when(i >= mixed_out)
        def _():
            copy_from(send.at[u], u).start()

    def settle(u, block):
        which, c = lax.rem(u, KINDS), lax.div(u, KINDS)
        done[which, c] = place(block, fresh[which], c * unit, source_len)

    def launch(i, carry):
        put(i)
        return carry
    lax.fori_loop(0, jnp.minimum(WINDOW, sends), launch, 0)
    fresh_copy.wait_recv()

    def settle_front(u, carry):
        settle(u, front[u])
        return carry
    lax.fori_loop(0, lead, settle_front, 0)

    def step(i, carry):
        u = jnp.where(i < comes, jnp.where(i < mixed_in, coming - 1 - i, lead + i - mixed_in), coming + i - comes)
        copy_from(send.at[u], u).wait_recv()
        if balanced:
            @pl.when(i < mixed_in)
            def _():
                back_copy(i).start()

        @pl.when(i < sends)
        def _():
            s = out_slot(i)
            copy_from(send.at[s], s).wait_send()

        @pl.when(i + WINDOW < sends)
        def _():
            put(i + WINDOW)
        settle(u, recv[u - least])
        return carry
    lax.fori_loop(0, total - lead, step, 0)
    fresh_copy.wait_send()

    if balanced:
        def returned(j, carry):
            back_copy(j).wait_send()
            return carry
        lax.fori_loop(0, mixed_in, returned, 0)


def store(res, done, res_out, k_out, v_out, sems, res_sem):
    copies = [pltpu.make_async_copy(res, res_out, res_sem)]
    part = done.shape[1] // STORES
    for which, dst in enumerate((k_out, v_out)):
        for i in range(STORES):
            span = pl.ds(i * part, part)
            copies.append(pltpu.make_async_copy(done.at[which, span], dst.at[span], sems.at[which, i]))
    for copy in copies:
        copy.start()
    for copy in copies:
        copy.wait()


def local(emb, attn_gain, out_gain, k_cache, v_cache, tables, lens, partner, mig_req):
    steps, requests, width = emb.shape
    _, _, pool, blk, kv_local = k_cache.shape
    maxblk = tables.shape[2]
    total = KINDS * SPLIT * maxblk
    cores = lax.axis_size("tp")
    groups = lax.axis_size("groups")
    context = maxblk * blk
    heads_kv = kv_local // HD
    rows = width // HD * steps
    bf16, f32 = jnp.bfloat16, jnp.float32
    vmem = pl.BlockSpec(memory_space=pltpu.VMEM)
    smem = pl.BlockSpec(memory_space=pltpu.SMEM)
    hbm = pl.BlockSpec(memory_space=pltpu.HBM)
    anywhere = pl.BlockSpec(memory_space=pl.ANY)
    dma = pltpu.SemaphoreType.DMA
    offsets = lax.axis_size("inst") - 1
    instances = lax.axis_size("inst")
    lead = total // 4

    def first_units(offset):
        return [lead + EXTRA if offsets == FEW and offset == 1 else lead] * instances

    def plan(offset):
        together = [tuple(range(instances))]
        if groups % 2 != 0:
            return together, [total]
        if offsets > FEW:
            return together, [total - lead, total]
        if offsets == FEW and offset > 1:
            return [(0, 3), (1, 2)], list(range(total - total // 3, total + 1, total // 6))
        step = total // 12
        return together, [total - lead - EXTRA, total - lead + EXTRA] + list(range(total - lead + step, total + 1, step))


    chunk = blk // SPLIT

    def unit(*count):
        return jax.ShapeDtypeStruct((*count, chunk, kv_local), bf16)

    def call_begin(offset):
        classes, levels = plan(offset)
        leads = first_units(offset)
        return pl.pallas_call(
            functools.partial(begin, offset, classes, levels, leads),
            out_shape=(
                jax.ShapeDtypeStruct((1,), jnp.int32),
                jax.ShapeDtypeStruct((1, steps, requests, width), bf16),
                unit(total),
                unit(max(total - levels[0], 1)),
                jax.ShapeDtypeStruct((KINDS, PAD, kv_local), bf16),
                unit(max(leads)),
            ),
            in_specs=[hbm] * 8,
            out_specs=(smem, vmem, vmem, vmem, vmem, vmem),
            scratch_shapes=[
                pltpu.SMEM(tables.shape, jnp.int32),
                pltpu.SMEM(lens.shape, jnp.int32),
                pltpu.SMEM(mig_req.shape, jnp.int32),
                pltpu.VMEM(emb.shape, bf16),
                pltpu.VMEM(attn_gain.shape, f32),
                pltpu.VMEM(out_gain.shape, f32),
                pltpu.VMEM((rows, HD), f32),
                pltpu.VMEM((rows, HD), f32),
                pltpu.VMEM((steps, requests, width), f32),
                pltpu.VMEM((pool, blk, kv_local), bf16),
                pltpu.VMEM((pool, blk, kv_local), bf16),
                pltpu.VMEM((groups, 8, 128), jnp.int32),
                pltpu.VMEM((requests * rows, HD), f32),
                pltpu.VMEM((requests * rows, HD), f32),
                pltpu.VMEM((requests, rows, HD), bf16),
                pltpu.VMEM((requests, rows, HD), bf16),
                pltpu.VMEM((cores, requests, 2 * steps, HD), f32),
                pltpu.VMEM((requests, 2 * steps, HD), f32),
                pltpu.VMEM((requests, PAD, kv_local), f32),
                pltpu.VMEM((requests, PAD, kv_local), f32),
                pltpu.VMEM((rows, heads_kv * HD), bf16),
                dma((6,)),
                dma((KINDS, LOADS)),
                dma((max(leads),)),
                dma((max(leads),)),
                dma((max(total - levels[0], 1),)),
                dma((max(total - levels[0], 1),)),
                dma((groups,)),
                dma((groups,)),
                dma((requests,)),
                dma((requests,)),
                dma((requests, cores)),
                dma((requests, cores)),
                dma((2, cores)),
            ],
            compiler_params=pltpu.CompilerParams(
                collective_id=offset - 1, has_side_effects=True, vmem_limit_bytes=LIMIT),
        )

    numbers = itertools.count(offsets)

    def call_finish(offset, chosen):
        classes, levels = plan(offset)
        leads = first_units(offset)
        return pl.pallas_call(
            functools.partial(finish, offset, classes, chosen, levels[0], leads),
            out_shape=unit(KINDS, total // KINDS),
            in_specs=[hbm] * 2 + [vmem] * 4,
            out_specs=vmem,
            scratch_shapes=[
                pltpu.SMEM(lens.shape, jnp.int32),
                pltpu.SMEM(mig_req.shape, jnp.int32),
                pltpu.VMEM((total - min(leads), chunk, kv_local), bf16),
                pltpu.VMEM((max(total - levels[0], 1), chunk, kv_local), bf16),
                pltpu.VMEM((KINDS, PAD, kv_local), bf16),
                dma((2,)),
                dma((total - min(leads),)),
                dma((total - min(leads),)),
                dma((max(total - levels[0], 1),)),
                dma((2,)),
            ],
            compiler_params=pltpu.CompilerParams(
                collective_id=next(numbers), has_side_effects=True, vmem_limit_bytes=LIMIT),
        )

    call_store = pl.pallas_call(
        store,
        out_shape=(
            jax.ShapeDtypeStruct((1, steps, requests, width), bf16),
            unit(total // KINDS),
            unit(total // KINDS),
        ),
        in_specs=[anywhere] * 2,
        out_specs=(hbm,) * 3,
        scratch_shapes=[dma((KINDS, STORES)), dma],
        compiler_params=pltpu.CompilerParams(vmem_limit_bytes=LIMIT),
    )

    def way(offset):
        def run(*operands):
            pick, out, send, moved, fresh, front = call_begin(offset)(*operands)

            classes, levels = plan(offset)
            combos = list(itertools.product(levels, repeat=len(classes)))

            def rest(chosen):
                def run_rest(lens, mig_req, out, send, moved, fresh, front):
                    return call_store(out, call_finish(offset, chosen)(lens, mig_req, send, moved, front, fresh))
                return run_rest
            res, k, v = lax.switch(
                pick[0], [rest(chosen) for chosen in combos],
                operands[1], operands[2], out, send, moved, fresh, front)
            return res, k.reshape(1, 1, context, kv_local), v.reshape(1, 1, context, kv_local)
        return run

    return tuple(lax.switch(
        partner[0] - 1, [way(offset) for offset in range(1, offsets + 1)],
        tables, lens, mig_req, emb, attn_gain, out_gain, k_cache, v_cache))


def solution(mesh):
    return jax.shard_map(
        local,
        mesh=mesh,
        in_specs=(
            P(None, ("groups", "inst"), "tp"),
            P("section", "tp"),
            P("section", "tp"),
            P(("groups", "inst"), "section", None, None, "tp"),
            P(("groups", "inst"), "section", None, None, "tp"),
            P(("groups", "inst"), None, None),
            P("groups", None),
            P(),
            P("groups"),
        ),
        out_specs=(
            P("section", None, ("groups", "inst"), "tp"),
            P(("groups", "inst"), "section", None, "tp"),
            P(("groups", "inst"), "section", None, "tp"),
        ),
        check_vma=False,
    )
```

```python
import functools
import itertools

import jax
import jax.numpy as jnp
from jax import lax
from jax.experimental import pallas as pl
from jax.experimental.pallas import tpu as pltpu
from jax.sharding import PartitionSpec as P

QH = 64
KVH = 8
HD = 128
LOADS = 3
STORES = 2
PAD = 8
KINDS = 2
SPLIT = 2
WINDOW = 6
LIMIT = 20 << 20
FEW = 3
EXTRA = 1
MESH = pl.DeviceIdType.MESH
NT = (((1,), (1,)), ((), ()))


def by_instance(i, values):
    chosen = values[-1]
    if len(set(values)) > 1:
        for k, value in enumerate(values[:-1]):
            chosen = jnp.where(i == k, value, chosen)
    return chosen


def place(block, fresh, first_row, source_len):
    blk, width = block.shape
    pos = lax.broadcasted_iota(jnp.int32, (blk, PAD), 0) + first_row - source_len
    hit = jnp.where(pos == lax.broadcasted_iota(jnp.int32, (blk, PAD), 1), 1.0, 0.0).astype(jnp.bfloat16)
    placed = jnp.dot(hit, fresh, preferred_element_type=jnp.float32)
    row = lax.broadcasted_iota(jnp.int32, (blk, width), 0) + first_row
    return jnp.where(row < source_len, block.astype(jnp.float32), placed).astype(jnp.bfloat16)


def begin(offset, classes, levels, leads, tables_hbm, lens_hbm, mig_hbm, emb_hbm, gain_attn_hbm, gain_out_hbm, k_hbm, v_hbm,
          pick, out, send, moved, fresh, recv,
          tables, lens, mig_req, emb, gain_attn, gain_out, gain_q, gain_o, turn,
          k_all, v_all, counts,
          h_rows, y_rows, res, h_in, ss_all, ss_out, fk, fv, q_diag,
          small_sem, load_sem, mig_send, mig_recv, moved_send, moved_recv, count_ssem, count_rsem,
          h_ssem, h_rsem, ss_ssem, ss_rsem, peer_sem):
    sections = lax.axis_size("section")
    cores = lax.axis_size("tp")
    groups = lax.axis_size("groups")
    section = lax.axis_index("section")
    core = lax.axis_index("tp")
    inst = lax.axis_index("inst")
    group = lax.axis_index("groups")
    steps, requests, width = emb.shape
    pool, blk, kv_local = k_all.shape
    instances = lens.shape[0]
    total, unit, _ = send.shape
    chunks = total // KINDS
    split = blk // unit
    maxblk = chunks // split
    spare = total - levels[0]
    lead = by_instance(inst, leads)
    heads_kv = kv_local // HD
    heads = width // HD
    share = QH // KVH
    rows = heads * steps
    part = share * steps
    scale = HD ** (-0.5)
    total_width = width * cores
    source = jnp.bitwise_xor(inst, offset)
    beside = jnp.bitwise_xor(group, 1)

    small = []
    for i, (src, dst) in enumerate((
            (mig_hbm, mig_req), (tables_hbm, tables), (lens_hbm, lens),
            (emb_hbm, emb), (gain_attn_hbm, gain_attn), (gain_out_hbm, gain_out))):
        small.append(pltpu.make_async_copy(src, dst, small_sem.at[i]))
    loads = []
    piece = pool // LOADS
    for which, (src, dst) in enumerate(((k_hbm, k_all), (v_hbm, v_all))):
        for i in range(LOADS):
            loads.append(pltpu.make_async_copy(
                src.at[0, 0, pl.ds(i * piece, piece)], dst.at[pl.ds(i * piece, piece)], load_sem.at[which, i]))
    for copy in small[:3] + loads[:LOADS] + small[3:] + loads[LOADS:]:
        copy.start()

    barrier = pltpu.get_barrier_semaphore()
    pl.semaphore_signal(barrier, inc=1, device_id={"inst": source}, device_id_type=MESH)
    greeted = cores
    if spare > 0:
        for step in range(1, groups):
            pl.semaphore_signal(barrier, inc=1, device_id={"groups": lax.rem(group + step, groups)}, device_id_type=MESH)
        greeted = greeted + groups - 1
    for step in range(1, cores):
        pl.semaphore_signal(barrier, inc=1, device_id={"tp": lax.rem(core + step, cores)}, device_id_type=MESH)

    @pl.when(section > 0)
    def _():
        for other in range(cores):
            pl.semaphore_signal(barrier, inc=1, device_id={"section": section - 1, "tp": other}, device_id_type=MESH)

    @pl.when(section < sections - 1)
    def _():
        for other in range(cores):
            pl.semaphore_signal(barrier, inc=1, device_id={"section": section + 1, "tp": other}, device_id_type=MESH)

    def peer_copy(step):
        return pltpu.make_async_remote_copy(
            src_ref=ss_all.at[core], dst_ref=ss_all.at[core],
            send_sem=peer_sem.at[0, step], recv_sem=peer_sem.at[1, core],
            device_id={"tp": lax.rem(core + step, cores)}, device_id_type=MESH)

    def peer_arrival(other):
        return pltpu.make_async_remote_copy(
            src_ref=ss_all.at[other], dst_ref=ss_all.at[other],
            send_sem=peer_sem.at[0, 0], recv_sem=peer_sem.at[1, other],
            device_id={"tp": lax.rem(core + 1, cores)}, device_id_type=MESH)

    def next_copy(r):
        return pltpu.make_async_remote_copy(
            src_ref=res.at[r], dst_ref=h_in.at[r],
            send_sem=h_ssem.at[r], recv_sem=h_rsem.at[r],
            device_id={"section": section + 1}, device_id_type=MESH)

    def next_sum(r, other):
        return pltpu.make_async_remote_copy(
            src_ref=ss_out.at[r], dst_ref=ss_all.at[core, r],
            send_sem=ss_ssem.at[r, other], recv_sem=ss_rsem.at[r, core],
            device_id={"section": section + 1, "tp": other}, device_id_type=MESH)

    def sum_arrival(r, other):
        return pltpu.make_async_remote_copy(
            src_ref=ss_out.at[r], dst_ref=ss_all.at[other, r],
            send_sem=ss_ssem.at[r, other], recv_sem=ss_rsem.at[r, other],
            device_id={"tp": lax.rem(core + 1, cores)}, device_id_type=MESH)

    def own_copy(u):
        return pltpu.make_async_remote_copy(
            src_ref=send.at[u], dst_ref=recv.at[u],
            send_sem=mig_send.at[u], recv_sem=mig_recv.at[u],
            device_id={"inst": source}, device_id_type=MESH)

    def moved_copy(j):
        return pltpu.make_async_remote_copy(
            src_ref=send.at[levels[0] + j], dst_ref=moved.at[j],
            send_sem=moved_send.at[j], recv_sem=moved_recv.at[j],
            device_id={"groups": beside}, device_id_type=MESH)

    def count_copy(step, slot):
        return pltpu.make_async_remote_copy(
            src_ref=counts.at[slot], dst_ref=counts.at[slot],
            send_sem=count_ssem.at[step], recv_sem=count_rsem.at[slot],
            device_id={"groups": lax.rem(group + step, groups)}, device_id_type=MESH)

    for copy in small[:3]:
        copy.wait()
    if spare > 0:
        lane = lax.broadcasted_iota(jnp.int32, counts.shape[1:], 1)
        held = jnp.zeros(counts.shape[1:], jnp.int32)
        for i in range(instances):
            held = jnp.where(lane == i, lax.div(lens[i, mig_req[i]] + (unit - 1), unit), held)
        counts[group] = held
    neighbours = jnp.minimum(section, 1) + jnp.minimum(sections - 1 - section, 1)
    pl.semaphore_wait(barrier, greeted + cores * neighbours)
    if spare > 0:
        for step in range(1, groups):
            count_copy(step, group).start()

    handed = mig_req[inst]
    def hand_over(which, stored):
        for i in range(LOADS):
            loads[which * LOADS + i].wait()

        def gather(c, carry):
            u = KINDS * c + which
            span = pl.ds(pl.multiple_of(lax.rem(c, split) * unit, unit), unit)
            send[u] = stored[tables[0, handed, lax.div(c, split)], span, :]

            @pl.when(u < lead)
            def _():
                own_copy(u).start()
            if spare > 0:
                @pl.when(u >= levels[0])
                def _():
                    moved_copy(u - levels[0]).start()
            return carry
        lax.fori_loop(0, chunks, gather, 0)

    hand_over(0, k_all)
    for copy in small[3:]:
        copy.wait()

    for i in range(heads):
        lanes = slice(i * HD, (i + 1) * HD)
        span = slice(i * steps, (i + 1) * steps)
        gain_q[span, :] = jnp.broadcast_to(gain_attn[0:1, lanes], (steps, HD))
        gain_o[span, :] = jnp.broadcast_to(gain_out[0:1, lanes], (steps, HD))

    tile = 2 * steps

    def row_sums(a):
        a = jnp.sum((a * a).reshape(rows // tile, tile, HD), axis=0)
        a = a[:steps] + a[steps:]
        a = jnp.broadcast_to(jnp.sum(a, axis=-1, keepdims=True), (steps, HD))
        return jnp.concatenate([a, a], axis=0)

    @pl.when(section == 0)
    def _():
        def spread(t, carry):
            e = emb[t].astype(jnp.float32)
            for i in range(heads):
                h_rows[pl.ds(i * steps + t, requests, stride=rows), :] = e[:, i * HD:(i + 1) * HD]
            return carry
        lax.fori_loop(0, steps, spread, 0)

        def first_sums(r, carry):
            ss_all[core, r] = row_sums(h_rows[pl.ds(pl.multiple_of(r * rows, rows), rows), :])
            return carry
        lax.fori_loop(0, requests, first_sums, 0)

    fk[...] = jnp.zeros_like(fk)
    fv[...] = jnp.zeros_like(fv)
    q_diag[...] = jnp.zeros_like(q_diag)

    @pl.when(section == 0)
    def _():
        for step in range(1, cores):
            peer_copy(step).start()

    hand_over(1, v_all)
    @pl.when(section == 0)
    def _():
        for step in range(1, cores):
            peer_arrival(lax.rem(core + step, cores)).wait_recv()

    def one_request(r, carry):
        @pl.when(section > 0)
        def _():
            next_copy(r).wait_recv()
            for other in range(cores):
                sum_arrival(r, other).wait_recv()
            h_rows[pl.ds(pl.multiple_of(r * rows, rows), rows), :] = h_in[r].astype(jnp.float32)

        squares = ss_all[0, r]
        for other in range(1, cores):
            squares = squares + ss_all[other, r]
        ratio = lax.rsqrt(squares / total_width + 1e-05)
        length = lens[inst, r]
        h = h_rows[pl.ds(pl.multiple_of(r * rows, rows), rows), :]
        x = h.reshape(rows // tile, tile, HD) * ratio[None] * gain_q[...].reshape(rows // tile, tile, HD)
        x = x.reshape(rows, HD)
        for g in range(heads_kv):
            lanes = slice(g * HD, (g + 1) * HD)
            span = slice(g * part, (g + 1) * part)
            key_sum = jnp.sum(x[span].reshape(part // tile, tile, HD), axis=0)
            value_sum = jnp.sum(h[span].reshape(part // tile, tile, HD), axis=0)
            fk[r, 0:steps, lanes] = (key_sum[:steps] + key_sum[steps:]) * (1.0 / share)
            fv[r, 0:steps, lanes] = (value_sum[:steps] + value_sum[steps:]) * (1.0 / share)
            q_diag[span, lanes] = x[span].astype(jnp.bfloat16)
        q = q_diag[...]
        row = lax.broadcasted_iota(jnp.int32, (blk, rows), 0)
        new_row = lax.broadcasted_iota(jnp.int32, (PAD, rows), 0)
        new_step = lax.rem(lax.broadcasted_iota(jnp.int32, (PAD, rows), 1), steps)
        scores = []
        for b in range(maxblk):
            s = lax.dot_general(k_all[tables[0, r, b]], q, NT, preferred_element_type=jnp.float32) * scale
            scores.append(jnp.where(row + b * blk < length, s, -jnp.inf))
        new = lax.dot_general(fk[r].astype(jnp.bfloat16), q, NT, preferred_element_type=jnp.float32) * scale
        new = jnp.where(new_row <= new_step, new, -jnp.inf)
        top = functools.reduce(jnp.maximum, scores)
        top = jnp.maximum(jnp.max(top, axis=0, keepdims=True), jnp.max(new, axis=0, keepdims=True))
        expo = [jnp.exp(s - top) for s in scores]
        expo_new = jnp.exp(new - top)
        total_weight = jnp.sum(functools.reduce(jnp.add, expo), axis=0, keepdims=True)
        total_weight = total_weight + jnp.sum(expo_new, axis=0, keepdims=True)
        inverse = 1.0 / total_weight
        weights = jnp.concatenate([(e * inverse).astype(jnp.bfloat16).T for e in expo], axis=1)
        weights_new = (expo_new * inverse).T.astype(jnp.bfloat16)
        values = [v_all[tables[0, r, b]] for b in range(maxblk)]
        fresh_values = fv[r].astype(jnp.bfloat16)
        outs = []
        for g in range(heads_kv):
            lanes = slice(g * HD, (g + 1) * HD)
            span = slice(g * part, (g + 1) * part)
            o = jnp.dot(weights[span], jnp.concatenate([v[:, lanes] for v in values], axis=0),
                        preferred_element_type=jnp.float32)
            o = o + jnp.dot(weights_new[span], fresh_values[:, lanes], preferred_element_type=jnp.float32)
            o = o * lax.rsqrt(jnp.mean(o * o, axis=-1, keepdims=True) + 1e-05)
            outs.append(o)
        y = (h + jnp.concatenate(outs, axis=0) * gain_o[...]).astype(jnp.bfloat16)
        res[r] = y
        y = y.astype(jnp.float32)
        y_rows[pl.ds(pl.multiple_of(r * rows, rows), rows), :] = y
        ss_out[r] = row_sums(y)

        @pl.when(section < sections - 1)
        def _():
            next_copy(r).start()
            for other in range(cores):
                next_sum(r, other).start()
        return carry

    lax.fori_loop(0, requests, one_request, 0)

    fresh[0] = fk[handed].astype(jnp.bfloat16)
    fresh[1] = fv[handed].astype(jnp.bfloat16)

    if spare > 0:
        for step in range(1, groups):
            count_copy(step, lax.rem(group + step, groups)).wait_recv()
        most = jnp.zeros(counts.shape[1:], jnp.int32)
        for pair in range(0, groups, 2):
            most = jnp.maximum(most, counts[pair] + counts[pair + 1])
        lane = lax.broadcasted_iota(jnp.int32, most.shape, 1)
        choice = 0
        for members in classes:
            own = functools.reduce(jnp.logical_or, [lane == i for i in members])
            need = jnp.max(jnp.where(own, most, 0))
            choice = choice * len(levels)
            for level in levels[:-1]:
                choice = choice + jnp.where(need > level, 1, 0)
        pick[0] = choice
    else:
        pick[0] = 0

    def collect(t, carry):
        for i in range(heads):
            turn[t, :, i * HD:(i + 1) * HD] = y_rows[pl.ds(i * steps + t, requests, stride=rows), :]
        out[0, t] = turn[t].astype(jnp.bfloat16)
        return carry
    lax.fori_loop(0, steps, collect, 0)

    def taken(u, carry):
        own_copy(u).wait_recv()
        return carry
    lax.fori_loop(0, lead, taken, 0)

    def given(u, carry):
        own_copy(u).wait_send()
        return carry
    lax.fori_loop(0, lead, given, 0)
    if spare > 0:
        for j in range(spare):
            moved_copy(j).wait_recv()
        for j in range(spare):
            moved_copy(j).wait_send()
        for step in range(1, groups):
            count_copy(step, group).wait_send()

    @pl.when(section == 0)
    def _():
        for step in range(1, cores):
            peer_copy(step).wait_send()

    @pl.when(section < sections - 1)
    def _():
        for r in range(requests):
            next_copy(r).wait_send()
            for other in range(cores):
                next_sum(r, other).wait_send()


def finish(offset, classes, chosen, lowest, leads, lens_hbm, mig_hbm, send, moved, front, fresh_send,
           done,
           lens, mig_req, recv, mix, fresh, small_sem, mig_send, mig_recv, back_send, fresh_sem):
    inst = lax.axis_index("inst")
    group = lax.axis_index("groups")
    total, unit, _ = send.shape
    lead, least = by_instance(inst, leads), min(leads)
    source = jnp.bitwise_xor(inst, offset)
    beside = jnp.bitwise_xor(group, 1)
    balanced = lowest < total

    def slots_of(i):
        return by_instance(i, [
            level for k in range(len(leads)) for members, level in zip(classes, chosen) if k in members])

    going, coming = slots_of(inst), slots_of(source)
    sends, comes = going - lead, coming - lead
    mixed_out, mixed_in = total - going, total - coming

    small = [pltpu.make_async_copy(mig_hbm, mig_req, small_sem.at[0]), pltpu.make_async_copy(lens_hbm, lens, small_sem.at[1])]
    for copy in small:
        copy.start()
    barrier = pltpu.get_barrier_semaphore()
    pl.semaphore_signal(barrier, inc=1, device_id={"inst": source}, device_id_type=MESH)
    if balanced:
        pl.semaphore_signal(barrier, inc=1, device_id={"groups": beside}, device_id_type=MESH)
    for copy in small:
        copy.wait()
    pl.semaphore_wait(barrier, 2 if balanced else 1)

    def out_slot(i):
        return jnp.where(i < mixed_out, going - 1 - i, lead + i - mixed_out)

    def copy_from(ref, u):
        return pltpu.make_async_remote_copy(
            src_ref=ref, dst_ref=recv.at[u - least],
            send_sem=mig_send.at[u - least], recv_sem=mig_recv.at[u - least],
            device_id={"inst": source}, device_id_type=MESH)

    def back_copy(j):
        return pltpu.make_async_remote_copy(
            src_ref=recv.at[coming - 1 - j - least], dst_ref=recv.at[coming + j - least],
            send_sem=back_send.at[j], recv_sem=mig_recv.at[coming + j - least],
            device_id={"groups": beside}, device_id_type=MESH)

    fresh_copy = pltpu.make_async_remote_copy(
        src_ref=fresh_send, dst_ref=fresh, send_sem=fresh_sem.at[0], recv_sem=fresh_sem.at[1],
        device_id={"inst": source}, device_id_type=MESH)
    fresh_copy.start()
    handed_chunks = lax.div(lens[inst, mig_req[inst]] + (unit - 1), unit)
    source_len = lens[source, mig_req[source]]

    def put(i):
        u = out_slot(i)
        if balanced:
            @pl.when(i < mixed_out)
            def _():
                mix[i] = jnp.where(lax.div(u, KINDS) < handed_chunks, send[u], moved[going + i - lowest])
                copy_from(mix.at[i], u).start()

        @pl.when(i >= mixed_out)
        def _():
            copy_from(send.at[u], u).start()

    def settle(u, block):
        which, c = lax.rem(u, KINDS), lax.div(u, KINDS)
        done[which, c] = place(block, fresh[which], c * unit, source_len)

    def launch(i, carry):
        put(i)
        return carry
    lax.fori_loop(0, jnp.minimum(WINDOW, sends), launch, 0)
    fresh_copy.wait_recv()

    def settle_front(u, carry):
        settle(u, front[u])
        return carry
    lax.fori_loop(0, lead, settle_front, 0)

    def step(i, carry):
        u = jnp.where(i < comes, jnp.where(i < mixed_in, coming - 1 - i, lead + i - mixed_in), coming + i - comes)
        copy_from(send.at[u], u).wait_recv()
        if balanced:
            @pl.when(i < mixed_in)
            def _():
                back_copy(i).start()

        @pl.when(i < sends)
        def _():
            s = out_slot(i)
            copy_from(send.at[s], s).wait_send()

        @pl.when(i + WINDOW < sends)
        def _():
            put(i + WINDOW)
        settle(u, recv[u - least])
        return carry
    lax.fori_loop(0, total - lead, step, 0)
    fresh_copy.wait_send()

    if balanced:
        def returned(j, carry):
            back_copy(j).wait_send()
            return carry
        lax.fori_loop(0, mixed_in, returned, 0)


def store(res, done, res_out, k_out, v_out, sems, res_sem):
    copies = [pltpu.make_async_copy(res, res_out, res_sem)]
    part = done.shape[1] // STORES
    for which, dst in enumerate((k_out, v_out)):
        for i in range(STORES):
            span = pl.ds(i * part, part)
            copies.append(pltpu.make_async_copy(done.at[which, span], dst.at[span], sems.at[which, i]))
    for copy in copies:
        copy.start()
    for copy in copies:
        copy.wait()


def local(emb, attn_gain, out_gain, k_cache, v_cache, tables, lens, partner, mig_req):
    steps, requests, width = emb.shape
    _, _, pool, blk, kv_local = k_cache.shape
    maxblk = tables.shape[2]
    total = KINDS * SPLIT * maxblk
    cores = lax.axis_size("tp")
    groups = lax.axis_size("groups")
    context = maxblk * blk
    heads_kv = kv_local // HD
    rows = width // HD * steps
    bf16, f32 = jnp.bfloat16, jnp.float32
    vmem = pl.BlockSpec(memory_space=pltpu.VMEM)
    smem = pl.BlockSpec(memory_space=pltpu.SMEM)
    hbm = pl.BlockSpec(memory_space=pltpu.HBM)
    anywhere = pl.BlockSpec(memory_space=pl.ANY)
    dma = pltpu.SemaphoreType.DMA
    offsets = lax.axis_size("inst") - 1
    instances = lax.axis_size("inst")
    lead = total // 4

    def first_units(offset):
        return [lead + EXTRA if offsets == FEW and offset == 1 else lead] * instances

    def plan(offset):
        together = [tuple(range(instances))]
        if groups % 2 != 0:
            return together, [total]
        if offsets > FEW:
            return together, [total - lead, total]
        if offsets == FEW and offset > 1:
            return [(0, 3), (1, 2)], list(range(total - total // 3, total + 1, total // 6))
        step = total // 12
        return together, [total - lead - EXTRA, total - lead + EXTRA] + list(range(total - lead + step, total + 1, step))


    chunk = blk // SPLIT

    def unit(*count):
        return jax.ShapeDtypeStruct((*count, chunk, kv_local), bf16)

    def call_begin(offset):
        classes, levels = plan(offset)
        leads = first_units(offset)
        return pl.pallas_call(
            functools.partial(begin, offset, classes, levels, leads),
            out_shape=(
                jax.ShapeDtypeStruct((1,), jnp.int32),
                jax.ShapeDtypeStruct((1, steps, requests, width), bf16),
                unit(total),
                unit(max(total - levels[0], 1)),
                jax.ShapeDtypeStruct((KINDS, PAD, kv_local), bf16),
                unit(max(leads)),
            ),
            in_specs=[hbm] * 8,
            out_specs=(smem, vmem, vmem, vmem, vmem, vmem),
            scratch_shapes=[
                pltpu.SMEM(tables.shape, jnp.int32),
                pltpu.SMEM(lens.shape, jnp.int32),
                pltpu.SMEM(mig_req.shape, jnp.int32),
                pltpu.VMEM(emb.shape, bf16),
                pltpu.VMEM(attn_gain.shape, f32),
                pltpu.VMEM(out_gain.shape, f32),
                pltpu.VMEM((rows, HD), f32),
                pltpu.VMEM((rows, HD), f32),
                pltpu.VMEM((steps, requests, width), f32),
                pltpu.VMEM((pool, blk, kv_local), bf16),
                pltpu.VMEM((pool, blk, kv_local), bf16),
                pltpu.VMEM((groups, 8, 128), jnp.int32),
                pltpu.VMEM((requests * rows, HD), f32),
                pltpu.VMEM((requests * rows, HD), f32),
                pltpu.VMEM((requests, rows, HD), bf16),
                pltpu.VMEM((requests, rows, HD), bf16),
                pltpu.VMEM((cores, requests, 2 * steps, HD), f32),
                pltpu.VMEM((requests, 2 * steps, HD), f32),
                pltpu.VMEM((requests, PAD, kv_local), f32),
                pltpu.VMEM((requests, PAD, kv_local), f32),
                pltpu.VMEM((rows, heads_kv * HD), bf16),
                dma((6,)),
                dma((KINDS, LOADS)),
                dma((max(leads),)),
                dma((max(leads),)),
                dma((max(total - levels[0], 1),)),
                dma((max(total - levels[0], 1),)),
                dma((groups,)),
                dma((groups,)),
                dma((requests,)),
                dma((requests,)),
                dma((requests, cores)),
                dma((requests, cores)),
                dma((2, cores)),
            ],
            compiler_params=pltpu.CompilerParams(
                collective_id=offset - 1, has_side_effects=True, vmem_limit_bytes=LIMIT),
        )

    numbers = itertools.count(offsets)

    def call_finish(offset, chosen):
        classes, levels = plan(offset)
        leads = first_units(offset)
        return pl.pallas_call(
            functools.partial(finish, offset, classes, chosen, levels[0], leads),
            out_shape=unit(KINDS, total // KINDS),
            in_specs=[hbm] * 2 + [vmem] * 4,
            out_specs=vmem,
            scratch_shapes=[
                pltpu.SMEM(lens.shape, jnp.int32),
                pltpu.SMEM(mig_req.shape, jnp.int32),
                pltpu.VMEM((total - min(leads), chunk, kv_local), bf16),
                pltpu.VMEM((max(total - levels[0], 1), chunk, kv_local), bf16),
                pltpu.VMEM((KINDS, PAD, kv_local), bf16),
                dma((2,)),
                dma((total - min(leads),)),
                dma((total - min(leads),)),
                dma((max(total - levels[0], 1),)),
                dma((2,)),
            ],
            compiler_params=pltpu.CompilerParams(
                collective_id=next(numbers), has_side_effects=True, vmem_limit_bytes=LIMIT),
        )

    call_store = pl.pallas_call(
        store,
        out_shape=(
            jax.ShapeDtypeStruct((1, steps, requests, width), bf16),
            unit(total // KINDS),
            unit(total // KINDS),
        ),
        in_specs=[anywhere] * 2,
        out_specs=(hbm,) * 3,
        scratch_shapes=[dma((KINDS, STORES)), dma],
        compiler_params=pltpu.CompilerParams(vmem_limit_bytes=LIMIT),
    )

    def way(offset):
        def run(*operands):
            pick, out, send, moved, fresh, front = call_begin(offset)(*operands)

            classes, levels = plan(offset)
            combos = list(itertools.product(levels, repeat=len(classes)))

            def rest(chosen):
                def run_rest(lens, mig_req, out, send, moved, fresh, front):
                    return call_store(out, call_finish(offset, chosen)(lens, mig_req, send, moved, front, fresh))
                return run_rest
            res, k, v = lax.switch(
                pick[0], [rest(chosen) for chosen in combos],
                operands[1], operands[2], out, send, moved, fresh, front)
            return res, k.reshape(1, 1, context, kv_local), v.reshape(1, 1, context, kv_local)
        return run

    return tuple(lax.switch(
        partner[0] - 1, [way(offset) for offset in range(1, offsets + 1)],
        tables, lens, mig_req, emb, attn_gain, out_gain, k_cache, v_cache))


def solution(mesh):
    return jax.shard_map(
        local,
        mesh=mesh,
        in_specs=(
            P(None, ("groups", "inst"), "tp"),
            P("section", "tp"),
            P("section", "tp"),
            P(("groups", "inst"), "section", None, None, "tp"),
            P(("groups", "inst"), "section", None, None, "tp"),
            P(("groups", "inst"), None, None),
            P("groups", None),
            P(),
            P("groups"),
        ),
        out_specs=(
            P("section", None, ("groups", "inst"), "tp"),
            P(("groups", "inst"), "section", None, "tp"),
            P(("groups", "inst"), "section", None, "tp"),
        ),
        check_vma=False,
    )
```

```python
import functools
import itertools

import jax
import jax.numpy as jnp
from jax import lax
from jax.experimental import pallas as pl
from jax.experimental.pallas import tpu as pltpu
from jax.sharding import PartitionSpec as P

QH = 64
KVH = 8
HD = 128
LOADS = 3
STORES = 2
PAD = 8
KINDS = 2
SPLIT = 2
WINDOW = 6
LIMIT = 20 << 20
FEW = 3
EXTRA = 1
MESH = pl.DeviceIdType.MESH
NT = (((1,), (1,)), ((), ()))


def by_instance(i, values):
    chosen = values[-1]
    if len(set(values)) > 1:
        for k, value in enumerate(values[:-1]):
            chosen = jnp.where(i == k, value, chosen)
    return chosen


def place(block, fresh, first_row, source_len):
    blk, width = block.shape
    pos = lax.broadcasted_iota(jnp.int32, (blk, PAD), 0) + first_row - source_len
    hit = jnp.where(pos == lax.broadcasted_iota(jnp.int32, (blk, PAD), 1), 1.0, 0.0).astype(jnp.bfloat16)
    placed = jnp.dot(hit, fresh, preferred_element_type=jnp.float32)
    row = lax.broadcasted_iota(jnp.int32, (blk, width), 0) + first_row
    return jnp.where(row < source_len, block.astype(jnp.float32), placed).astype(jnp.bfloat16)


def begin(offset, classes, levels, leads, tables_hbm, lens_hbm, mig_hbm, emb_hbm, gain_attn_hbm, gain_out_hbm, k_hbm, v_hbm,
          pick, out, send, moved, fresh, recv,
          tables, lens, mig_req, emb, gain_attn, gain_out, gain_q, gain_o, turn,
          k_all, v_all, counts,
          h_rows, y_rows, res, h_in, ss_all, ss_out, fk, fv, q_diag,
          small_sem, load_sem, mig_send, mig_recv, moved_send, moved_recv, count_ssem, count_rsem,
          h_ssem, h_rsem, ss_ssem, ss_rsem, peer_sem):
    sections = lax.axis_size("section")
    cores = lax.axis_size("tp")
    groups = lax.axis_size("groups")
    section = lax.axis_index("section")
    core = lax.axis_index("tp")
    inst = lax.axis_index("inst")
    group = lax.axis_index("groups")
    steps, requests, width = emb.shape
    pool, blk, kv_local = k_all.shape
    instances = lens.shape[0]
    total, unit, _ = send.shape
    chunks = total // KINDS
    split = blk // unit
    maxblk = chunks // split
    spare = total - levels[0]
    lead = by_instance(inst, leads)
    heads_kv = kv_local // HD
    heads = width // HD
    share = QH // KVH
    rows = heads * steps
    part = share * steps
    scale = HD ** (-0.5)
    total_width = width * cores
    source = jnp.bitwise_xor(inst, offset)
    beside = jnp.bitwise_xor(group, 1)

    small = []
    for i, (src, dst) in enumerate((
            (mig_hbm, mig_req), (tables_hbm, tables), (lens_hbm, lens),
            (emb_hbm, emb), (gain_attn_hbm, gain_attn), (gain_out_hbm, gain_out))):
        small.append(pltpu.make_async_copy(src, dst, small_sem.at[i]))
    loads = []
    piece = pool // LOADS
    for which, (src, dst) in enumerate(((k_hbm, k_all), (v_hbm, v_all))):
        for i in range(LOADS):
            loads.append(pltpu.make_async_copy(
                src.at[0, 0, pl.ds(i * piece, piece)], dst.at[pl.ds(i * piece, piece)], load_sem.at[which, i]))
    for copy in small[:3] + loads[:LOADS] + small[3:] + loads[LOADS:]:
        copy.start()

    barrier = pltpu.get_barrier_semaphore()
    pl.semaphore_signal(barrier, inc=1, device_id={"inst": source}, device_id_type=MESH)
    greeted = cores
    if spare > 0:
        for step in range(1, groups):
            pl.semaphore_signal(barrier, inc=1, device_id={"groups": lax.rem(group + step, groups)}, device_id_type=MESH)
        greeted = greeted + groups - 1
    for step in range(1, cores):
        pl.semaphore_signal(barrier, inc=1, device_id={"tp": lax.rem(core + step, cores)}, device_id_type=MESH)

    @pl.when(section > 0)
    def _():
        for other in range(cores):
            pl.semaphore_signal(barrier, inc=1, device_id={"section": section - 1, "tp": other}, device_id_type=MESH)

    @pl.when(section < sections - 1)
    def _():
        for other in range(cores):
            pl.semaphore_signal(barrier, inc=1, device_id={"section": section + 1, "tp": other}, device_id_type=MESH)

    def peer_copy(step):
        return pltpu.make_async_remote_copy(
            src_ref=ss_all.at[core], dst_ref=ss_all.at[core],
            send_sem=peer_sem.at[0, step], recv_sem=peer_sem.at[1, core],
            device_id={"tp": lax.rem(core + step, cores)}, device_id_type=MESH)

    def peer_arrival(other):
        return pltpu.make_async_remote_copy(
            src_ref=ss_all.at[other], dst_ref=ss_all.at[other],
            send_sem=peer_sem.at[0, 0], recv_sem=peer_sem.at[1, other],
            device_id={"tp": lax.rem(core + 1, cores)}, device_id_type=MESH)

    def next_copy(r):
        return pltpu.make_async_remote_copy(
            src_ref=res.at[r], dst_ref=h_in.at[r],
            send_sem=h_ssem.at[r], recv_sem=h_rsem.at[r],
            device_id={"section": section + 1}, device_id_type=MESH)

    def next_sum(r, other):
        return pltpu.make_async_remote_copy(
            src_ref=ss_out.at[r], dst_ref=ss_all.at[core, r],
            send_sem=ss_ssem.at[r, other], recv_sem=ss_rsem.at[r, core],
            device_id={"section": section + 1, "tp": other}, device_id_type=MESH)

    def sum_arrival(r, other):
        return pltpu.make_async_remote_copy(
            src_ref=ss_out.at[r], dst_ref=ss_all.at[other, r],
            send_sem=ss_ssem.at[r, other], recv_sem=ss_rsem.at[r, other],
            device_id={"tp": lax.rem(core + 1, cores)}, device_id_type=MESH)

    def own_copy(u):
        return pltpu.make_async_remote_copy(
            src_ref=send.at[u], dst_ref=recv.at[u],
            send_sem=mig_send.at[u], recv_sem=mig_recv.at[u],
            device_id={"inst": source}, device_id_type=MESH)

    def moved_copy(j):
        return pltpu.make_async_remote_copy(
            src_ref=send.at[levels[0] + j], dst_ref=moved.at[j],
            send_sem=moved_send.at[j], recv_sem=moved_recv.at[j],
            device_id={"groups": beside}, device_id_type=MESH)

    def count_copy(step, slot):
        return pltpu.make_async_remote_copy(
            src_ref=counts.at[slot], dst_ref=counts.at[slot],
            send_sem=count_ssem.at[step], recv_sem=count_rsem.at[slot],
            device_id={"groups": lax.rem(group + step, groups)}, device_id_type=MESH)

    for copy in small[:3]:
        copy.wait()
    if spare > 0:
        lane = lax.broadcasted_iota(jnp.int32, counts.shape[1:], 1)
        held = jnp.zeros(counts.shape[1:], jnp.int32)
        for i in range(instances):
            held = jnp.where(lane == i, lax.div(lens[i, mig_req[i]] + (unit - 1), unit), held)
        counts[group] = held
    neighbours = jnp.minimum(section, 1) + jnp.minimum(sections - 1 - section, 1)
    pl.semaphore_wait(barrier, greeted + cores * neighbours)
    if spare > 0:
        for step in range(1, groups):
            count_copy(step, group).start()

    handed = mig_req[inst]
    def hand_over(which, stored):
        for i in range(LOADS):
            loads[which * LOADS + i].wait()

        def gather(c, carry):
            u = KINDS * c + which
            span = pl.ds(pl.multiple_of(lax.rem(c, split) * unit, unit), unit)
            send[u] = stored[tables[0, handed, lax.div(c, split)], span, :]

            @pl.when(u < lead)
            def _():
                own_copy(u).start()
            if spare > 0:
                @pl.when(u >= levels[0])
                def _():
                    moved_copy(u - levels[0]).start()
            return carry
        lax.fori_loop(0, chunks, gather, 0)

    hand_over(0, k_all)
    for copy in small[3:]:
        copy.wait()

    for i in range(heads):
        lanes = slice(i * HD, (i + 1) * HD)
        span = slice(i * steps, (i + 1) * steps)
        gain_q[span, :] = jnp.broadcast_to(gain_attn[0:1, lanes], (steps, HD))
        gain_o[span, :] = jnp.broadcast_to(gain_out[0:1, lanes], (steps, HD))

    tile = 2 * steps

    def row_sums(a):
        a = jnp.sum((a * a).reshape(rows // tile, tile, HD), axis=0)
        a = a[:steps] + a[steps:]
        a = jnp.broadcast_to(jnp.sum(a, axis=-1, keepdims=True), (steps, HD))
        return jnp.concatenate([a, a], axis=0)

    @pl.when(section == 0)
    def _():
        def spread(t, carry):
            e = emb[t].astype(jnp.float32)
            for i in range(heads):
                h_rows[pl.ds(i * steps + t, requests, stride=rows), :] = e[:, i * HD:(i + 1) * HD]
            return carry
        lax.fori_loop(0, steps, spread, 0)

        def first_sums(r, carry):
            ss_all[core, r] = row_sums(h_rows[pl.ds(pl.multiple_of(r * rows, rows), rows), :])
            return carry
        lax.fori_loop(0, requests, first_sums, 0)

    fk[...] = jnp.zeros_like(fk)
    fv[...] = jnp.zeros_like(fv)
    q_diag[...] = jnp.zeros_like(q_diag)

    @pl.when(section == 0)
    def _():
        for step in range(1, cores):
            peer_copy(step).start()

    hand_over(1, v_all)
    @pl.when(section == 0)
    def _():
        for step in range(1, cores):
            peer_arrival(lax.rem(core + step, cores)).wait_recv()

    def one_request(r, carry):
        @pl.when(section > 0)
        def _():
            next_copy(r).wait_recv()
            for other in range(cores):
                sum_arrival(r, other).wait_recv()
            h_rows[pl.ds(pl.multiple_of(r * rows, rows), rows), :] = h_in[r].astype(jnp.float32)

        squares = ss_all[0, r]
        for other in range(1, cores):
            squares = squares + ss_all[other, r]
        ratio = lax.rsqrt(squares / total_width + 1e-05)
        length = lens[inst, r]
        h = h_rows[pl.ds(pl.multiple_of(r * rows, rows), rows), :]
        x = h.reshape(rows // tile, tile, HD) * ratio[None] * gain_q[...].reshape(rows // tile, tile, HD)
        x = x.reshape(rows, HD)
        for g in range(heads_kv):
            lanes = slice(g * HD, (g + 1) * HD)
            span = slice(g * part, (g + 1) * part)
            key_sum = jnp.sum(x[span].reshape(part // tile, tile, HD), axis=0)
            value_sum = jnp.sum(h[span].reshape(part // tile, tile, HD), axis=0)
            fk[r, 0:steps, lanes] = (key_sum[:steps] + key_sum[steps:]) * (1.0 / share)
            fv[r, 0:steps, lanes] = (value_sum[:steps] + value_sum[steps:]) * (1.0 / share)
            q_diag[span, lanes] = x[span].astype(jnp.bfloat16)
        q = q_diag[...]
        row = lax.broadcasted_iota(jnp.int32, (blk, rows), 0)
        new_row = lax.broadcasted_iota(jnp.int32, (PAD, rows), 0)
        new_step = lax.rem(lax.broadcasted_iota(jnp.int32, (PAD, rows), 1), steps)
        scores = []
        for b in range(maxblk):
            s = lax.dot_general(k_all[tables[0, r, b]], q, NT, preferred_element_type=jnp.float32) * scale
            scores.append(jnp.where(row + b * blk < length, s, -jnp.inf))
        new = lax.dot_general(fk[r].astype(jnp.bfloat16), q, NT, preferred_element_type=jnp.float32) * scale
        new = jnp.where(new_row <= new_step, new, -jnp.inf)
        top = functools.reduce(jnp.maximum, scores)
        top = jnp.maximum(jnp.max(top, axis=0, keepdims=True), jnp.max(new, axis=0, keepdims=True))
        expo = [jnp.exp(s - top) for s in scores]
        expo_new = jnp.exp(new - top)
        total_weight = jnp.sum(functools.reduce(jnp.add, expo), axis=0, keepdims=True)
        total_weight = total_weight + jnp.sum(expo_new, axis=0, keepdims=True)
        inverse = 1.0 / total_weight
        weights = jnp.concatenate([(e * inverse).astype(jnp.bfloat16).T for e in expo], axis=1)
        weights_new = (expo_new * inverse).T.astype(jnp.bfloat16)
        values = [v_all[tables[0, r, b]] for b in range(maxblk)]
        fresh_values = fv[r].astype(jnp.bfloat16)
        outs = []
        for g in range(heads_kv):
            lanes = slice(g * HD, (g + 1) * HD)
            span = slice(g * part, (g + 1) * part)
            o = jnp.dot(weights[span], jnp.concatenate([v[:, lanes] for v in values], axis=0),
                        preferred_element_type=jnp.float32)
            o = o + jnp.dot(weights_new[span], fresh_values[:, lanes], preferred_element_type=jnp.float32)
            o = o * lax.rsqrt(jnp.mean(o * o, axis=-1, keepdims=True) + 1e-05)
            outs.append(o)
        y = (h + jnp.concatenate(outs, axis=0) * gain_o[...]).astype(jnp.bfloat16)
        res[r] = y
        y = y.astype(jnp.float32)
        y_rows[pl.ds(pl.multiple_of(r * rows, rows), rows), :] = y
        ss_out[r] = row_sums(y)

        @pl.when(section < sections - 1)
        def _():
            next_copy(r).start()
            for other in range(cores):
                next_sum(r, other).start()
        return carry

    lax.fori_loop(0, requests, one_request, 0)

    fresh[0] = fk[handed].astype(jnp.bfloat16)
    fresh[1] = fv[handed].astype(jnp.bfloat16)

    if spare > 0:
        for step in range(1, groups):
            count_copy(step, lax.rem(group + step, groups)).wait_recv()
        most = jnp.zeros(counts.shape[1:], jnp.int32)
        for pair in range(0, groups, 2):
            most = jnp.maximum(most, counts[pair] + counts[pair + 1])
        lane = lax.broadcasted_iota(jnp.int32, most.shape, 1)
        choice = 0
        for members in classes:
            own = functools.reduce(jnp.logical_or, [lane == i for i in members])
            need = jnp.max(jnp.where(own, most, 0))
            choice = choice * len(levels)
            for level in levels[:-1]:
                choice = choice + jnp.where(need > level, 1, 0)
        pick[0] = choice
    else:
        pick[0] = 0

    def collect(t, carry):
        for i in range(heads):
            turn[t, :, i * HD:(i + 1) * HD] = y_rows[pl.ds(i * steps + t, requests, stride=rows), :]
        out[0, t] = turn[t].astype(jnp.bfloat16)
        return carry
    lax.fori_loop(0, steps, collect, 0)

    def taken(u, carry):
        own_copy(u).wait_recv()
        return carry
    lax.fori_loop(0, lead, taken, 0)

    def given(u, carry):
        own_copy(u).wait_send()
        return carry
    lax.fori_loop(0, lead, given, 0)
    if spare > 0:
        for j in range(spare):
            moved_copy(j).wait_recv()
        for j in range(spare):
            moved_copy(j).wait_send()
        for step in range(1, groups):
            count_copy(step, group).wait_send()

    @pl.when(section == 0)
    def _():
        for step in range(1, cores):
            peer_copy(step).wait_send()

    @pl.when(section < sections - 1)
    def _():
        for r in range(requests):
            next_copy(r).wait_send()
            for other in range(cores):
                next_sum(r, other).wait_send()


def finish(offset, classes, chosen, lowest, leads, lens_hbm, mig_hbm, send, moved, front, fresh_send,
           done,
           lens, mig_req, recv, mix, fresh, small_sem, mig_send, mig_recv, back_send, fresh_sem):
    inst = lax.axis_index("inst")
    group = lax.axis_index("groups")
    total, unit, _ = send.shape
    lead, least = by_instance(inst, leads), min(leads)
    source = jnp.bitwise_xor(inst, offset)
    beside = jnp.bitwise_xor(group, 1)
    balanced = lowest < total

    def slots_of(i):
        return by_instance(i, [
            level for k in range(len(leads)) for members, level in zip(classes, chosen) if k in members])

    going, coming = slots_of(inst), slots_of(source)
    sends, comes = going - lead, coming - lead
    mixed_out, mixed_in = total - going, total - coming

    small = [pltpu.make_async_copy(mig_hbm, mig_req, small_sem.at[0]), pltpu.make_async_copy(lens_hbm, lens, small_sem.at[1])]
    for copy in small:
        copy.start()
    barrier = pltpu.get_barrier_semaphore()
    pl.semaphore_signal(barrier, inc=1, device_id={"inst": source}, device_id_type=MESH)
    if balanced:
        pl.semaphore_signal(barrier, inc=1, device_id={"groups": beside}, device_id_type=MESH)
    for copy in small:
        copy.wait()
    pl.semaphore_wait(barrier, 2 if balanced else 1)

    def out_slot(i):
        return jnp.where(i < mixed_out, going - 1 - i, lead + i - mixed_out)

    def copy_from(ref, u):
        return pltpu.make_async_remote_copy(
            src_ref=ref, dst_ref=recv.at[u - least],
            send_sem=mig_send.at[u - least], recv_sem=mig_recv.at[u - least],
            device_id={"inst": source}, device_id_type=MESH)

    def back_copy(j):
        return pltpu.make_async_remote_copy(
            src_ref=recv.at[coming - 1 - j - least], dst_ref=recv.at[coming + j - least],
            send_sem=back_send.at[j], recv_sem=mig_recv.at[coming + j - least],
            device_id={"groups": beside}, device_id_type=MESH)

    fresh_copy = pltpu.make_async_remote_copy(
        src_ref=fresh_send, dst_ref=fresh, send_sem=fresh_sem.at[0], recv_sem=fresh_sem.at[1],
        device_id={"inst": source}, device_id_type=MESH)
    fresh_copy.start()
    handed_chunks = lax.div(lens[inst, mig_req[inst]] + (unit - 1), unit)
    source_len = lens[source, mig_req[source]]

    def put(i):
        u = out_slot(i)
        if balanced:
            @pl.when(i < mixed_out)
            def _():
                mix[i] = jnp.where(lax.div(u, KINDS) < handed_chunks, send[u], moved[going + i - lowest])
                copy_from(mix.at[i], u).start()

        @pl.when(i >= mixed_out)
        def _():
            copy_from(send.at[u], u).start()

    def settle(u, block):
        which, c = lax.rem(u, KINDS), lax.div(u, KINDS)
        done[which, c] = place(block, fresh[which], c * unit, source_len)

    def launch(i, carry):
        put(i)
        return carry
    lax.fori_loop(0, jnp.minimum(WINDOW, sends), launch, 0)
    fresh_copy.wait_recv()

    def settle_front(u, carry):
        settle(u, front[u])
        return carry
    lax.fori_loop(0, lead, settle_front, 0)

    def step(i, carry):
        u = jnp.where(i < comes, jnp.where(i < mixed_in, coming - 1 - i, lead + i - mixed_in), coming + i - comes)
        copy_from(send.at[u], u).wait_recv()
        if balanced:
            @pl.when(i < mixed_in)
            def _():
                back_copy(i).start()

        @pl.when(i < sends)
        def _():
            s = out_slot(i)
            copy_from(send.at[s], s).wait_send()

        @pl.when(i + WINDOW < sends)
        def _():
            put(i + WINDOW)
        settle(u, recv[u - least])
        return carry
    lax.fori_loop(0, total - lead, step, 0)
    fresh_copy.wait_send()

    if balanced:
        def returned(j, carry):
            back_copy(j).wait_send()
            return carry
        lax.fori_loop(0, mixed_in, returned, 0)


def store(res, done, res_out, k_out, v_out, sems, res_sem):
    copies = [pltpu.make_async_copy(res, res_out, res_sem)]
    part = done.shape[1] // STORES
    for which, dst in enumerate((k_out, v_out)):
        for i in range(STORES):
            span = pl.ds(i * part, part)
            copies.append(pltpu.make_async_copy(done.at[which, span], dst.at[span], sems.at[which, i]))
    for copy in copies:
        copy.start()
    for copy in copies:
        copy.wait()


def local(emb, attn_gain, out_gain, k_cache, v_cache, tables, lens, partner, mig_req):
    steps, requests, width = emb.shape
    _, _, pool, blk, kv_local = k_cache.shape
    maxblk = tables.shape[2]
    total = KINDS * SPLIT * maxblk
    cores = lax.axis_size("tp")
    groups = lax.axis_size("groups")
    context = maxblk * blk
    heads_kv = kv_local // HD
    rows = width // HD * steps
    bf16, f32 = jnp.bfloat16, jnp.float32
    vmem = pl.BlockSpec(memory_space=pltpu.VMEM)
    smem = pl.BlockSpec(memory_space=pltpu.SMEM)
    hbm = pl.BlockSpec(memory_space=pltpu.HBM)
    anywhere = pl.BlockSpec(memory_space=pl.ANY)
    dma = pltpu.SemaphoreType.DMA
    offsets = lax.axis_size("inst") - 1
    instances = lax.axis_size("inst")
    lead = total // 4

    def first_units(offset):
        return [lead + EXTRA if offsets == FEW and offset == 1 else lead] * instances

    def plan(offset):
        together = [tuple(range(instances))]
        if groups % 2 != 0:
            return together, [total]
        if offsets > FEW:
            return together, [total - lead, total]
        if offsets == FEW and offset > 1:
            return [(0, 3), (1, 2)], list(range(total - total // 3, total + 1, total // 6))
        step = total // 12
        return together, [total - lead - EXTRA, *range(total - lead + EXTRA, total - step + 1), total]


    chunk = blk // SPLIT

    def unit(*count):
        return jax.ShapeDtypeStruct((*count, chunk, kv_local), bf16)

    def call_begin(offset):
        classes, levels = plan(offset)
        leads = first_units(offset)
        return pl.pallas_call(
            functools.partial(begin, offset, classes, levels, leads),
            out_shape=(
                jax.ShapeDtypeStruct((1,), jnp.int32),
                jax.ShapeDtypeStruct((1, steps, requests, width), bf16),
                unit(total),
                unit(max(total - levels[0], 1)),
                jax.ShapeDtypeStruct((KINDS, PAD, kv_local), bf16),
                unit(max(leads)),
            ),
            in_specs=[hbm] * 8,
            out_specs=(smem, vmem, vmem, vmem, vmem, vmem),
            scratch_shapes=[
                pltpu.SMEM(tables.shape, jnp.int32),
                pltpu.SMEM(lens.shape, jnp.int32),
                pltpu.SMEM(mig_req.shape, jnp.int32),
                pltpu.VMEM(emb.shape, bf16),
                pltpu.VMEM(attn_gain.shape, f32),
                pltpu.VMEM(out_gain.shape, f32),
                pltpu.VMEM((rows, HD), f32),
                pltpu.VMEM((rows, HD), f32),
                pltpu.VMEM((steps, requests, width), f32),
                pltpu.VMEM((pool, blk, kv_local), bf16),
                pltpu.VMEM((pool, blk, kv_local), bf16),
                pltpu.VMEM((groups, 8, 128), jnp.int32),
                pltpu.VMEM((requests * rows, HD), f32),
                pltpu.VMEM((requests * rows, HD), f32),
                pltpu.VMEM((requests, rows, HD), bf16),
                pltpu.VMEM((requests, rows, HD), bf16),
                pltpu.VMEM((cores, requests, 2 * steps, HD), f32),
                pltpu.VMEM((requests, 2 * steps, HD), f32),
                pltpu.VMEM((requests, PAD, kv_local), f32),
                pltpu.VMEM((requests, PAD, kv_local), f32),
                pltpu.VMEM((rows, heads_kv * HD), bf16),
                dma((6,)),
                dma((KINDS, LOADS)),
                dma((max(leads),)),
                dma((max(leads),)),
                dma((max(total - levels[0], 1),)),
                dma((max(total - levels[0], 1),)),
                dma((groups,)),
                dma((groups,)),
                dma((requests,)),
                dma((requests,)),
                dma((requests, cores)),
                dma((requests, cores)),
                dma((2, cores)),
            ],
            compiler_params=pltpu.CompilerParams(
                collective_id=offset - 1, has_side_effects=True, vmem_limit_bytes=LIMIT),
        )

    numbers = itertools.count(offsets)

    def call_finish(offset, chosen):
        classes, levels = plan(offset)
        leads = first_units(offset)
        return pl.pallas_call(
            functools.partial(finish, offset, classes, chosen, levels[0], leads),
            out_shape=unit(KINDS, total // KINDS),
            in_specs=[hbm] * 2 + [vmem] * 4,
            out_specs=vmem,
            scratch_shapes=[
                pltpu.SMEM(lens.shape, jnp.int32),
                pltpu.SMEM(mig_req.shape, jnp.int32),
                pltpu.VMEM((total - min(leads), chunk, kv_local), bf16),
                pltpu.VMEM((max(total - levels[0], 1), chunk, kv_local), bf16),
                pltpu.VMEM((KINDS, PAD, kv_local), bf16),
                dma((2,)),
                dma((total - min(leads),)),
                dma((total - min(leads),)),
                dma((max(total - levels[0], 1),)),
                dma((2,)),
            ],
            compiler_params=pltpu.CompilerParams(
                collective_id=next(numbers), has_side_effects=True, vmem_limit_bytes=LIMIT),
        )

    call_store = pl.pallas_call(
        store,
        out_shape=(
            jax.ShapeDtypeStruct((1, steps, requests, width), bf16),
            unit(total // KINDS),
            unit(total // KINDS),
        ),
        in_specs=[anywhere] * 2,
        out_specs=(hbm,) * 3,
        scratch_shapes=[dma((KINDS, STORES)), dma],
        compiler_params=pltpu.CompilerParams(vmem_limit_bytes=LIMIT),
    )

    def way(offset):
        def run(*operands):
            pick, out, send, moved, fresh, front = call_begin(offset)(*operands)

            classes, levels = plan(offset)
            combos = list(itertools.product(levels, repeat=len(classes)))

            def rest(chosen):
                def run_rest(lens, mig_req, out, send, moved, fresh, front):
                    return call_store(out, call_finish(offset, chosen)(lens, mig_req, send, moved, front, fresh))
                return run_rest
            res, k, v = lax.switch(
                pick[0], [rest(chosen) for chosen in combos],
                operands[1], operands[2], out, send, moved, fresh, front)
            return res, k.reshape(1, 1, context, kv_local), v.reshape(1, 1, context, kv_local)
        return run

    return tuple(lax.switch(
        partner[0] - 1, [way(offset) for offset in range(1, offsets + 1)],
        tables, lens, mig_req, emb, attn_gain, out_gain, k_cache, v_cache))


def solution(mesh):
    return jax.shard_map(
        local,
        mesh=mesh,
        in_specs=(
            P(None, ("groups", "inst"), "tp"),
            P("section", "tp"),
            P("section", "tp"),
            P(("groups", "inst"), "section", None, None, "tp"),
            P(("groups", "inst"), "section", None, None, "tp"),
            P(("groups", "inst"), None, None),
            P("groups", None),
            P(),
            P("groups"),
        ),
        out_specs=(
            P("section", None, ("groups", "inst"), "tp"),
            P(("groups", "inst"), "section", None, "tp"),
            P(("groups", "inst"), "section", None, "tp"),
        ),
        check_vma=False,
    )
```
